32 devices in a mesh: seq: 8 (over z, core), rows: 4 (over y, x).
Axes of the slice: x: 2, y: 2, z: 4, core: 2. Of those that a mesh axis runs over, the one named last changes fastest.
Arguments:
- hidden_in: bfloat16 [8, 1024, 1024], P('rows', 'seq'), may hold values from -6 to 6
- lengths: int32 [8, 16], P('rows'), may hold values from 1 to 256, 1024 in all within a row
- norm1_gain: bfloat16 [1024], P(('seq', 'rows')), may hold values from 0.099609375 to 1.8984375
- w_query: bfloat16 [1024, 1024], P(('seq', 'rows')), may hold values from -0.25 to 0.25
- w_key: bfloat16 [1024, 1024], P(('seq', 'rows')), may hold values from -0.25 to 0.25
- w_value: bfloat16 [1024, 1024], P(('seq', 'rows')), may hold values from -0.1875 to 0.1875
- w_out: bfloat16 [1024, 1024], P(('seq', 'rows')), may hold values from -0.5 to 0.5
- norm2_gain: bfloat16 [1024], P(('seq', 'rows')), may hold values from 0.099609375 to 1.8984375
- w_gate: bfloat16 [1024, 2816], P(('seq', 'rows')), may hold values from -0.1875 to 0.1875
- w_up: bfloat16 [1024, 2816], P(('seq', 'rows')), may hold values from -0.1875 to 0.1875
- w_down: bfloat16 [1024, 2816], P(('seq', 'rows')), may hold values from -0.15625 to 0.15625
- out_grad: bfloat16 [8, 1024, 1024], P('rows', 'seq'), may hold values from -6 to 6
Outputs:
- block_out: bfloat16 [8, 1024, 1024], P('rows', 'seq')
- grad_in: float32 [8, 1024, 1024], P('rows', 'seq')
- grad_norm1: float32 [1024], P(('seq', 'rows'))
- grad_query: float32 [1024, 1024], P(('seq', 'rows'))
- grad_key: float32 [1024, 1024], P(('seq', 'rows'))
- grad_value: float32 [1024, 1024], P(('seq', 'rows'))
- grad_wout: float32 [1024, 1024], P(('seq', 'rows'))
- grad_norm2: float32 [1024], P(('seq', 'rows'))
- grad_gate: float32 [1024, 2816], P(('seq', 'rows'))
- grad_up: float32 [1024, 2816], P(('seq', 'rows'))
- grad_down: float32 [1024, 2816], P(('seq', 'rows'))
The draws below stay inside these ranges and needn't reach their ends.
Inputs may be any that keep to these rules, and one draw needn't show every extreme that they name: lengths[r] lists the lengths of the documents packed in order into row r; they sum to 1024, and the longest of each row has exactly 256 tokens.
All inputs are finite; a program needn't handle non-finite values.
Results may differ from the reference program's by a relative error of at most 0.014.
The reference program's roundings to bfloat16 on the way count: a program that leaves them out, or rounds other values in their place, can miss the bound.
Values may be sent and summed in bfloat16 or wider, within the bound.
A program may use at most 104 MiB of HBM per device.

```python
import math
import jax
import jax.numpy as jnp
import numpy as np
from jax import lax

D = 1024
HEADS = 8
HEAD_DIM = 128
FF = 2816
WINDOW = 64
SEQ_LEN = 1024
ROWS = 8
DOCS = 16
MOST = 256


def shard_levels(rng, extent, split, low, top_value):
    factor_of, own = 1.0, jax.random.fold_in(rng, 6)
    for position, blocks in split:
        heights = jnp.exp(jax.random.uniform(jax.random.fold_in(own, position), (blocks,), jnp.float32, low / len(split), top_value / len(split)))
        factor_of = factor_of * jnp.repeat(heights, extent[position] // blocks).reshape([-1 if axis == position else 1 for axis in range(len(extent))])
    return factor_of


def split_up(count, total, limit, skew):
    portions = [(1 << 20) // math.isqrt(standing ** skew) + 1 for standing in range(2, count + 1)]
    surplus, holding = total - limit - (count - 1), [1] * (count - 1)
    while surplus > 0:
        movable = [i for i in range(count - 1) if holding[i] < limit]
        whole, budget = sum([portions[i] for i in movable]), surplus
        for i in movable:
            extra = min(limit - holding[i], max(1, budget * portions[i] // whole), surplus)
            holding[i] = holding[i] + extra
            surplus = surplus - extra
    return np.array([limit] + holding)


def uneven_parts(key, count, total, most, slope):
    if count == 2:
        one = jax.random.randint(key, (), max(1, total - most), min(most, total - 1) + 1)
        return jnp.stack([one, total - one])
    sizes = jnp.asarray(split_up(count, total, most, slope), jnp.int32)
    couples = (count - 1) // 2
    giver, sink = sizes[1:1 + 2 * couples:2], sizes[2:2 + 2 * couples:2]
    slack = jnp.minimum(giver - 1, most - sink)
    passed = jax.random.randint(jax.random.fold_in(key, 1), (couples,), 0, 1 << 20) % (slack + 1)
    sizes = sizes.at[1:1 + 2 * couples:2].set(giver - passed).at[2:2 + 2 * couples:2].set(sink + passed)
    return sizes[jax.random.permutation(jax.random.fold_in(key, 2), count)]


def noise(key, shape, spread, reach, split=(), kind=jnp.bfloat16):
    values = spread * jax.random.normal(key, shape, jnp.float32)
    if split:
        values = values * shard_levels(key, shape, split, -0.22, 0.18)
    return jnp.clip(values, -reach, reach).astype(kind)


def setup_inputs(seed: int = 0) -> dict:
    seeds = jax.random.split(jax.random.key(seed), 13)
    hidden_in = noise(seeds[0], (ROWS, SEQ_LEN, D), 1.0, 6.0, ((0, 4), (1, 8)))
    lengths = jax.vmap(lambda own: uneven_parts(own, DOCS, SEQ_LEN, MOST, 2))(jax.random.split(seeds[1], ROWS)).reshape((ROWS, DOCS)).astype(jnp.int32)
    norm1_gain = jnp.clip(1.0 + 0.18 * jax.random.normal(seeds[2], (D,), jnp.float32), 0.099609375, 1.8984375).astype(jnp.bfloat16)
    w_query = noise(seeds[3], (D, D), (D // 2) ** -0.5, 0.25, ((0, 32),))
    w_key = noise(seeds[4], (D, D), (D // 2) ** -0.5, 0.25, ((0, 32),))
    w_value = noise(seeds[5], (D, D), D ** -0.5, 0.1875, ((0, 32),))
    w_out = noise(seeds[6], (D, D), (D // 8) ** -0.5, 0.5, ((0, 32),))
    norm2_gain = jnp.clip(1.0 + 0.18 * jax.random.normal(seeds[7], (D,), jnp.float32), 0.099609375, 1.8984375).astype(jnp.bfloat16)
    w_gate = noise(seeds[8], (D, FF), D ** -0.5, 0.1875, ((0, 32),))
    w_up = noise(seeds[9], (D, FF), D ** -0.5, 0.1875, ((0, 32),))
    w_down = noise(seeds[10], (D, FF), (FF // 2) ** -0.5, 0.15625, ((0, 32),))
    out_grad = noise(seeds[11], (ROWS, SEQ_LEN, D), 1.0, 6.0, ((0, 4), (1, 8)))
    return {"hidden_in": hidden_in, "lengths": lengths, "norm1_gain": norm1_gain, "w_query": w_query, "w_key": w_key, "w_value": w_value, "w_out": w_out, "norm2_gain": norm2_gain, "w_gate": w_gate, "w_up": w_up, "w_down": w_down, "out_grad": out_grad}


@jax.custom_vjp
def low(v):
    return lax.optimization_barrier(v.astype(jnp.bfloat16)).astype(jnp.float32)

@jax.custom_vjp
def low_back(v):
    return v

def low_keep(v):
    return (low(v), None)

def low_pass(kept, grad):
    return (grad,)

def back_keep(v):
    return (v, None)

def back_low(kept, grad):
    return (low(grad),)
low.defvjp(low_keep, low_pass)
low_back.defvjp(back_keep, back_low)
query_block = 512
highest = lax.Precision.HIGHEST

def rms_scale(values, gain):
    factor = lax.rsqrt(lax.optimization_barrier(jnp.mean(values * values, axis=-1, keepdims=True)) + 1e-05)
    return values * factor * gain

def matmul(left, right):
    return jnp.dot(left, right, precision=highest)

def reference(hidden_in, lengths, norm1_gain, w_query, w_key, w_value, w_out, norm2_gain, w_gate, w_up, w_down, out_grad):
    ends = jnp.cumsum(lengths, axis=1).astype(jnp.int32)
    positions = jnp.arange(SEQ_LEN, dtype=jnp.int32)
    starts = lax.optimization_barrier(jnp.max(jnp.where(ends[:, None, :] <= positions[None, :, None], ends[:, None, :], jnp.zeros_like(ends[:, None, :])), axis=2)).astype(jnp.int32)
    score_scale = 1.0 / HEAD_DIM ** 0.5
    blocks = SEQ_LEN // query_block

    def forward(inputs, gain_one, wq, wk, wv, wo, gain_two, wg, wu, wd):

        def row_layer(pair):
            row, start = pair
            normed = low(rms_scale(row, gain_one))
            queries = low(low_back(matmul(normed, wq)))
            keys = low(low_back(matmul(normed, wk)))
            values = low(low_back(matmul(normed, wv)))
            padding = jnp.zeros((WINDOW, D), jnp.float32)
            keys_pad = jnp.concatenate([padding, keys], axis=0)
            values_pad = jnp.concatenate([padding, values], axis=0)

            def block_fn(index):
                first = (index * query_block).astype(jnp.int32)
                query_part = lax.dynamic_slice_in_dim(queries, first, query_block, 0).reshape(query_block, HEADS, HEAD_DIM)
                key_part = lax.dynamic_slice_in_dim(keys_pad, first, query_block + WINDOW, 0).reshape(query_block + WINDOW, HEADS, HEAD_DIM)
                value_part = lax.dynamic_slice_in_dim(values_pad, first, query_block + WINDOW, 0).reshape(query_block + WINDOW, HEADS, HEAD_DIM)
                start_part = lax.dynamic_slice_in_dim(start, first, query_block, 0)
                query_pos = first + jnp.arange(query_block, dtype=jnp.int32)
                key_pos = first - WINDOW + jnp.arange(query_block + WINDOW, dtype=jnp.int32)
                allowed = (key_pos[None, :] >= start_part[:, None]) & (key_pos[None, :] <= query_pos[:, None]) & (query_pos[:, None] - key_pos[None, :] < WINDOW)
                scores = low_back(jnp.einsum('qhd,khd->hqk', query_part, key_part, precision=highest) * score_scale)
                scores = jnp.where(allowed[None], scores, -1e+30)
                top = lax.optimization_barrier(jnp.max(scores, axis=-1, keepdims=True))
                weights = jnp.exp(scores - top)
                probs = weights / lax.optimization_barrier(jnp.sum(weights, axis=-1, keepdims=True))
                mixed = jnp.einsum('hqk,khd->qhd', low(probs), value_part, precision=highest)
                return mixed.reshape(query_block, D)
            attended = lax.map(jax.checkpoint(block_fn), jnp.arange(blocks, dtype=jnp.int32)).reshape(SEQ_LEN, D)
            attended = low(low_back(attended))
            middle = row + low_back(matmul(attended, wo))
            normed_two = low(rms_scale(middle, gain_two))
            gates = low_back(matmul(normed_two, wg))
            ups = low_back(matmul(normed_two, wu))
            hidden_act = low(jax.nn.silu(gates) * ups)
            branch = low_back(matmul(hidden_act, wd.T))
            return middle + branch
        return lax.map(row_layer, (inputs, starts))
    primals = (hidden_in.astype(jnp.float32), norm1_gain.astype(jnp.float32), w_query.astype(jnp.float32), w_key.astype(jnp.float32), w_value.astype(jnp.float32), w_out.astype(jnp.float32), norm2_gain.astype(jnp.float32), w_gate.astype(jnp.float32), w_up.astype(jnp.float32), w_down.astype(jnp.float32))
    result, pullback = jax.vjp(forward, *primals)
    grads = pullback(out_grad.astype(jnp.float32))
    return (result.astype(jnp.bfloat16), grads[0], grads[1], grads[2], grads[3], grads[4], grads[5], grads[6], grads[7], grads[8], grads[9])
```

```python
import functools
import math

import jax
import jax.numpy as jnp
from jax import lax
from jax.experimental import pallas as pl
from jax.experimental.pallas import tpu as pltpu
from jax.sharding import PartitionSpec as P

HEADS = 8
HEAD_DIM = 128
WINDOW = 64
LANES = 128
MESH = pl.DeviceIdType.MESH


def passed_along(block, axis, distance):
    devices = range(lax.axis_size(axis))
    route = [(i - distance, i) for i in devices if i - distance in devices]
    return lax.ppermute(block, axis, route)


def rms_scale(values, gain):
    factor = lax.rsqrt(jnp.mean(values * values, axis=-1, keepdims=True) + 1e-05)
    return values * factor * gain


def swiglu(gates, ups):
    return jax.nn.silu(gates) * ups


def project(left, weight):
    return jnp.dot(left, weight, preferred_element_type=jnp.float32)


def project_back(grad, weight):
    return lax.dot_general(
        grad, weight, (((2,), (1,)), ((), ())), preferred_element_type=jnp.float32
    )


def weight_grad(left, grad):
    return jnp.einsum("rtd,rtf->df", left, grad, preferred_element_type=jnp.float32)


def split_heads(values):
    return values.reshape(values.shape[0], values.shape[1], HEADS, HEAD_DIM)


def merge_heads(values):
    return values.reshape(values.shape[0], values.shape[1], HEADS * HEAD_DIM)


def window_mask(lengths, seq_index, tokens):
    docs = lengths.shape[1]
    upto = jnp.arange(docs)[:, None] >= jnp.arange(docs)[None, :]
    ends = jnp.sum(jnp.where(upto[None], lengths[:, None, :], 0), axis=2)
    query_pos = seq_index * tokens + jnp.arange(tokens, dtype=jnp.int32)
    key_pos = seq_index * tokens - WINDOW + jnp.arange(tokens + WINDOW, dtype=jnp.int32)
    starts = jnp.max(
        jnp.where(
            ends[:, None, :] <= query_pos[None, :, None],
            ends[:, None, :],
            jnp.zeros_like(ends[:, None, :]),
        ),
        axis=2,
    )
    allowed = (
        (key_pos[None, None, :] >= starts[:, :, None])
        & (key_pos[None, None, :] <= query_pos[None, :, None])
        & (query_pos[None, :, None] - key_pos[None, None, :] < WINDOW)
    )
    return allowed[:, None]


def scores_of(queries, keys_all, allowed):
    score_scale = 1.0 / math.sqrt(HEAD_DIM)
    scores = (
        jnp.einsum(
            "rqhd,rkhd->rhqk",
            split_heads(queries),
            split_heads(keys_all),
            preferred_element_type=jnp.float32,
        )
        * score_scale
    )
    return jnp.where(allowed, scores, -1e30)


def gathered_by_xla(shards):
    return [lax.all_gather(s, ("seq", "rows"), axis=0, tiled=True) for s in shards]


def scattered_by_xla(totals):
    return [
        lax.psum_scatter(t.astype(jnp.float32), ("seq", "rows"), scatter_dimension=0, tiled=True)
        for t in totals
    ]


class Place:
    def __init__(self):
        seq, rows = lax.axis_index("seq"), lax.axis_index("rows")
        self.z, self.c = seq // 2, seq % 2
        self.y, self.x = rows // 2, rows % 2
        self.turn_y, self.turn_x = 1 - 2 * self.y, 1 - 2 * self.x

    def column(self, near, far):
        y, x, c = self.y, self.x, self.c
        if near:
            y, x = y + c * self.turn_y, x + (1 - c) * self.turn_x
        if far:
            y, x = y + (1 - c) * self.turn_y, x + c * self.turn_x
        return y, x

    def device(self, z, c, column):
        return (2 * z + c, 2 * column[0] + column[1])

    def near(self):
        return self.device(self.z, self.c, self.column(True, False))

    def far(self):
        return self.device(self.z, self.c, self.column(False, True))

    def peer(self):
        return self.device(self.z, 1 - self.c, (self.y, self.x))

    def along_z(self, step):
        return self.device((self.z + step) % 4, self.c, (self.y, self.x))

    def partners(self):
        return [self.near(), self.far(), self.peer()] + [self.along_z(i) for i in (1, 2, 3)]


def greet(partners):
    barrier = pltpu.get_barrier_semaphore()
    for partner in partners:
        pl.semaphore_signal(barrier, inc=1, device_id=partner, device_id_type=MESH)
    pl.semaphore_wait(barrier, len(partners))


def remote(source, target, send, recv, device):
    return pltpu.make_async_remote_copy(
        src_ref=source, dst_ref=target, send_sem=send, recv_sem=recv,
        device_id=device, device_id_type=MESH,
    )


def gather_kernel(count, *refs):
    shards, wholes = refs[:count], refs[count : 2 * count]
    own_sem, send, recv = refs[2 * count :]
    here = Place()
    z, c = here.z, here.c
    own, near, far, both = (
        here.column(False, False), here.column(True, False),
        here.column(False, True), here.column(True, True),
    )
    greet(here.partners())

    def block(k, core, column):
        return wholes[k].at[:, core, column[0], column[1]]

    def copy(k, number, view, device):
        return remote(view, view, send.at[k, number], recv.at[k, number], device)

    for k in range(count):
        slot = wholes[k].at[z, c, own[0], own[1]]
        for step in (1, 2, 3):
            remote(shards[k], slot, send.at[k, step - 1], recv.at[k, step - 1], here.along_z(step)).start()
        pltpu.make_async_copy(shards[k], slot, own_sem.at[k]).start()

    def second(k):
        for step in (1, 2, 3):
            slot = wholes[k].at[(z + 4 - step) % 4, c, own[0], own[1]]
            remote(shards[k], slot, send.at[k, step - 1], recv.at[k, step - 1], here.along_z(step)).wait()
        pltpu.make_async_copy(shards[k], wholes[k].at[z, c, own[0], own[1]], own_sem.at[k]).wait()
        copy(k, 3, block(k, c, own), here.near()).start()
        copy(k, 4, block(k, c, own), here.far()).start()
        copy(k, 6, block(k, c, own), here.peer()).start()

    def third(k):
        copy(k, 3, block(k, c, near), here.near()).wait()
        copy(k, 5, block(k, c, near), here.far()).start()
        copy(k, 7, block(k, c, near), here.peer()).start()

    def fourth(k):
        copy(k, 4, block(k, c, far), here.far()).wait()
        copy(k, 8, block(k, c, far), here.peer()).start()
        copy(k, 5, block(k, c, both), here.far()).wait()
        copy(k, 9, block(k, c, both), here.peer()).start()

    def fifth(k):
        for number, column in ((6, own), (7, near), (8, far), (9, both)):
            copy(k, number, block(k, 1 - c, column), here.peer()).wait()

    for tick in range(count + 3):
        for lag, step in enumerate((second, third, fourth, fifth)):
            if 0 <= tick - lag < count:
                step(tick - lag)


def gathered(shards):
    count = len(shards)
    wholes = pl.pallas_call(
        functools.partial(gather_kernel, count),
        out_shape=[jax.ShapeDtypeStruct((4, 2, 2, 2, *s.shape), s.dtype) for s in shards],
        in_specs=[pl.BlockSpec(memory_space=pl.ANY)] * count,
        out_specs=[pl.BlockSpec(memory_space=pl.ANY)] * count,
        scratch_shapes=[
            pltpu.SemaphoreType.DMA((count,)),
            pltpu.SemaphoreType.DMA((count, 10)),
            pltpu.SemaphoreType.DMA((count, 10)),
        ],
        compiler_params=pltpu.CompilerParams(collective_id=0, has_side_effects=True),
        name="gather_weights",
    )(*shards)
    return [w.reshape(-1, w.shape[-1]) for w in wholes]


def scatter_kernel(plan, count, *refs):
    grads, sums = refs[:count], refs[count : 2 * count]
    refs = refs[2 * count :]
    total = len(plan)
    mine, paired, twos, fours = (refs[i * total : (i + 1) * total] for i in range(4))
    own_sem, send, recv = refs[4 * total :]
    here = Place()
    z, c = here.z, here.c
    own, near, far, both = (
        here.column(False, False), here.column(True, False),
        here.column(False, True), here.column(True, True),
    )
    greet(here.partners())

    def own_copy(k):
        number, first, width = plan[k]
        return pltpu.make_async_copy(
            grads[number].at[:, c, :, :, :, pl.ds(first, width)], mine[k], own_sem.at[k]
        )

    def to_peer(k):
        number, first, width = plan[k]
        return remote(
            grads[number].at[:, 1 - c, :, :, :, pl.ds(first, width)], paired[k],
            send.at[k, 0], recv.at[k, 0], here.peer(),
        )

    def to_far(k, which):
        column = both if which else far
        return remote(
            mine[k].at[:, column[0], column[1]], twos[k].at[which],
            send.at[k, 1 + which], recv.at[k, 1 + which], here.far(),
        )

    def to_near(k):
        return remote(
            mine[k].at[:, near[0], near[1]], twos[k].at[2],
            send.at[k, 3], recv.at[k, 3], here.near(),
        )

    def to_z(k, step):
        return remote(
            mine[k].at[(z + step) % 4, own[0], own[1]], fours[k].at[step - 1],
            send.at[k, 3 + step], recv.at[k, 3 + step], here.along_z(step),
        )

    def add(left, right):
        return (left.astype(jnp.float32) + right.astype(jnp.float32)).astype(jnp.bfloat16)

    for k in range(total):
        to_peer(k).start()
        own_copy(k).start()

    def first(k):
        own_copy(k).wait()
        to_peer(k).wait()

        @pl.loop(0, 4)
        def _(level):
            mine[k][level] = add(mine[k][level], paired[k][level])

        to_far(k, 1).start()
        to_far(k, 0).start()

    def second(k):
        to_far(k, 1).wait()

        @pl.loop(0, 4)
        def _(level):
            view = mine[k].at[level, near[0], near[1]]
            view[...] = add(view[...], twos[k][1, level])

        to_near(k).start()
        to_far(k, 0).wait()

        @pl.loop(0, 4)
        def _(level):
            view = mine[k].at[level, own[0], own[1]]
            view[...] = add(view[...], twos[k][0, level])

    def third(k):
        to_near(k).wait()

        @pl.loop(0, 4)
        def _(level):
            view = mine[k].at[level, own[0], own[1]]
            view[...] = add(view[...], twos[k][2, level])

        for step in (1, 2, 3):
            to_z(k, step).start()

    def fourth(k):
        number, begin, width = plan[k]
        for step in (1, 2, 3):
            to_z(k, step).wait()
        value = mine[k][z, own[0], own[1]].astype(jnp.float32)
        for step in (1, 2, 3):
            value = value + fours[k][step - 1].astype(jnp.float32)
        sums[number][:, pl.ds(begin, width)] = value

    for tick in range(total + 3):
        for lag, step in enumerate((first, second, third, fourth)):
            if 0 <= tick - lag < total:
                step(tick - lag)


def scattered(totals):
    count = len(totals)
    block = totals[0].shape[0] // 32
    plan = []
    for number, t in enumerate(totals):
        width = t.shape[1]
        parts = 2 if width > 1024 else 1
        for part in range(parts):
            plan.append((number, part * (width // parts), width // parts))
    halves = [(4, 2, 2, block, width) for _, _, width in plan]
    thirds = [(3, 4, block, width) for _, _, width in plan]
    ends = [(3, block, width) for _, _, width in plan]
    return pl.pallas_call(
        functools.partial(scatter_kernel, plan, count),
        out_shape=[jax.ShapeDtypeStruct((block, t.shape[1]), jnp.float32) for t in totals],
        in_specs=[pl.BlockSpec(memory_space=pl.ANY)] * count,
        out_specs=[pl.BlockSpec(memory_space=pltpu.VMEM)] * count,
        scratch_shapes=[
            *[pltpu.VMEM(s, jnp.bfloat16) for shapes in (halves, halves, thirds, ends) for s in shapes],
            pltpu.SemaphoreType.DMA((len(plan),)),
            pltpu.SemaphoreType.DMA((len(plan), 7)),
            pltpu.SemaphoreType.DMA((len(plan), 7)),
        ],
        compiler_params=pltpu.CompilerParams(
            collective_id=1, has_side_effects=True, vmem_limit_bytes=60 * 2**20
        ),
        name="scatter_grads",
    )(*[t.astype(jnp.bfloat16).reshape(4, 2, 2, 2, block, t.shape[1]) for t in totals])


def layer(hidden_in, lengths, out_grad, gains, weights):
    score_scale = 1.0 / math.sqrt(HEAD_DIM)
    tokens = hidden_in.shape[1]
    gain_one, gain_two = gains
    w_query, w_key, w_value, w_out, w_gate, w_up, w_down = weights
    inputs = hidden_in.astype(jnp.float32)
    normed_one = rms_scale(inputs, gain_one).astype(jnp.bfloat16)
    queries = project(normed_one, w_query).astype(jnp.bfloat16)
    keys = project(normed_one, w_key).astype(jnp.bfloat16)
    values = project(normed_one, w_value).astype(jnp.bfloat16)
    tails = jnp.stack([keys[:, tokens - WINDOW :], values[:, tokens - WINDOW :]])
    received = passed_along(tails, "seq", 1)
    keys_all = jnp.concatenate([received[0], keys], axis=1)
    values_all = jnp.concatenate([received[1], values], axis=1)
    allowed = window_mask(lengths, lax.axis_index("seq"), tokens)
    scores = scores_of(queries, keys_all, allowed)
    top = jnp.max(scores, axis=-1, keepdims=True)
    exps = jnp.exp(scores - top)
    probs = exps / jnp.sum(exps, axis=-1, keepdims=True)
    probs_low = probs.astype(jnp.bfloat16)
    mixed = jnp.einsum(
        "rhqk,rkhd->rqhd", probs_low, split_heads(values_all), preferred_element_type=jnp.float32
    )
    attended = merge_heads(mixed).astype(jnp.bfloat16)
    middle = inputs + project(attended, w_out)
    normed_two = rms_scale(middle, gain_two).astype(jnp.bfloat16)
    gates = project(normed_two, w_gate)
    ups = project(normed_two, w_up)
    hidden_act = swiglu(gates, ups).astype(jnp.bfloat16)
    block_out = (middle + project_back(hidden_act, w_down)).astype(jnp.bfloat16)
    grad_hidden = project(out_grad, w_down)
    unused, swiglu_back = jax.vjp(swiglu, gates, ups)
    grad_gates, grad_ups = swiglu_back(grad_hidden)
    grad_gates = grad_gates.astype(jnp.bfloat16)
    grad_ups = grad_ups.astype(jnp.bfloat16)
    grad_down = weight_grad(out_grad, hidden_act)
    grad_gate = weight_grad(normed_two, grad_gates)
    grad_up = weight_grad(normed_two, grad_ups)
    grad_normed_two = project_back(grad_gates, w_gate) + project_back(grad_ups, w_up)
    unused, norm_two_back = jax.vjp(rms_scale, middle, gain_two)
    grad_middle_part, grad_norm2 = norm_two_back(grad_normed_two)
    grad_middle = out_grad.astype(jnp.float32) + grad_middle_part
    grad_branch = grad_middle.astype(jnp.bfloat16)
    grad_wout = weight_grad(attended, grad_branch)
    grad_attended = project_back(grad_branch, w_out).astype(jnp.bfloat16)
    grad_heads = split_heads(grad_attended)
    grad_values_all = jnp.einsum(
        "rhqk,rqhd->rkhd", probs_low, grad_heads, preferred_element_type=jnp.float32
    )
    grad_probs = jnp.einsum(
        "rqhd,rkhd->rhqk", grad_heads, split_heads(values_all), preferred_element_type=jnp.float32
    )
    grad_scores = (
        probs * (grad_probs - jnp.sum(grad_probs * probs, axis=-1, keepdims=True))
    ).astype(jnp.bfloat16)
    grad_queries = score_scale * merge_heads(
        jnp.einsum(
            "rhqk,rkhd->rqhd", grad_scores, split_heads(keys_all),
            preferred_element_type=jnp.float32,
        )
    )
    grad_keys_all = score_scale * merge_heads(
        jnp.einsum(
            "rhqk,rqhd->rkhd", grad_scores, split_heads(queries),
            preferred_element_type=jnp.float32,
        )
    )
    grad_values_all = merge_heads(grad_values_all)
    halo_grads = jnp.stack([grad_keys_all[:, :WINDOW], grad_values_all[:, :WINDOW]])
    returned = passed_along(halo_grads.astype(jnp.bfloat16), "seq", -1).astype(halo_grads.dtype)
    grad_keys = (
        grad_keys_all[:, WINDOW:].at[:, tokens - WINDOW :].add(returned[0]).astype(jnp.bfloat16)
    )
    grad_values = (
        grad_values_all[:, WINDOW:].at[:, tokens - WINDOW :].add(returned[1]).astype(jnp.bfloat16)
    )
    grad_queries = grad_queries.astype(jnp.bfloat16)
    grad_query = weight_grad(normed_one, grad_queries)
    grad_key = weight_grad(normed_one, grad_keys)
    grad_value = weight_grad(normed_one, grad_values)
    grad_normed_one = (
        project_back(grad_queries, w_query)
        + project_back(grad_keys, w_key)
        + project_back(grad_values, w_value)
    )
    unused, norm_one_back = jax.vjp(rms_scale, inputs, gain_one)
    grad_inputs_part, grad_norm1 = norm_one_back(grad_normed_one)
    grad_in = grad_middle + grad_inputs_part
    grads = (grad_query, grad_key, grad_value, grad_wout, grad_gate, grad_up, grad_down)
    return block_out, grad_in, (grad_norm1, grad_norm2), grads


def shards(
    hidden_in, lengths, norm1_gain, w_query, w_key, w_value, w_out,
    norm2_gain, w_gate, w_up, w_down, out_grad,
):
    gain_shards = (norm1_gain, norm2_gain)
    weight_shards = (w_query, w_key, w_value, w_out, w_gate, w_up, w_down)
    kernels = (lax.axis_size("seq"), lax.axis_size("rows")) == (8, 4)
    if kernels:
        both = jnp.concatenate(
            [jnp.broadcast_to(g[:, None], (g.shape[0], LANES)) for g in gain_shards], axis=1
        )
        both, *weights = gathered([both, *weight_shards])
        gains = [both[:, 0], both[:, LANES]]
    else:
        gains = gathered_by_xla(gain_shards)
        weights = gathered_by_xla(weight_shards)
    gains = [g.astype(jnp.float32) for g in gains]
    block_out, grad_in, norms, grads = layer(hidden_in, lengths, out_grad, gains, weights)
    if kernels:
        both = jnp.concatenate(
            [jnp.broadcast_to(g[:, None], (g.shape[0], LANES)) for g in norms], axis=1
        )
        *grads, both = scattered([*grads, both])
        norms = [both[:, 0], both[:, LANES]]
    else:
        norms = scattered_by_xla(norms)
        grads = scattered_by_xla(grads)
    return (
        block_out, grad_in, norms[0], grads[0], grads[1], grads[2], grads[3],
        norms[1], grads[4], grads[5], grads[6],
    )


def solution(mesh):
    tokens = P("rows", "seq", None)
    vector = P(("seq", "rows"))
    matrix = P(("seq", "rows"), None)
    in_specs = (
        tokens, P("rows", None), vector, matrix, matrix, matrix, matrix,
        vector, matrix, matrix, matrix, tokens,
    )
    out_specs = (
        tokens, tokens, vector, matrix, matrix, matrix, matrix,
        vector, matrix, matrix, matrix,
    )
    return jax.shard_map(shards, mesh=mesh, in_specs=in_specs, out_specs=out_specs, check_vma=False)
```

```python
import functools
import math

import jax
import jax.numpy as jnp
from jax import lax
from jax.experimental import pallas as pl
from jax.experimental.pallas import tpu as pltpu
from jax.sharding import PartitionSpec as P

HEADS = 8
HEAD_DIM = 128
WINDOW = 64
LANES = 128
MESH = pl.DeviceIdType.MESH


def passed_along(block, axis, distance):
    devices = range(lax.axis_size(axis))
    route = [(i - distance, i) for i in devices if i - distance in devices]
    return lax.ppermute(block, axis, route)


def rms_scale(values, gain):
    factor = lax.rsqrt(jnp.mean(values * values, axis=-1, keepdims=True) + 1e-05)
    return values * factor * gain


def swiglu(gates, ups):
    return jax.nn.silu(gates) * ups


def project(left, weight):
    return jnp.dot(left, weight, preferred_element_type=jnp.float32)


def project_back(grad, weight):
    return lax.dot_general(
        grad, weight, (((2,), (1,)), ((), ())), preferred_element_type=jnp.float32
    )


def weight_grad(left, grad):
    return jnp.einsum("rtd,rtf->df", left, grad, preferred_element_type=jnp.float32)


def split_heads(values):
    return values.reshape(values.shape[0], values.shape[1], HEADS, HEAD_DIM)


def merge_heads(values):
    return values.reshape(values.shape[0], values.shape[1], HEADS * HEAD_DIM)


def window_mask(lengths, seq_index, tokens):
    docs = lengths.shape[1]
    upto = jnp.arange(docs)[:, None] >= jnp.arange(docs)[None, :]
    ends = jnp.sum(jnp.where(upto[None], lengths[:, None, :], 0), axis=2)
    query_pos = seq_index * tokens + jnp.arange(tokens, dtype=jnp.int32)
    key_pos = seq_index * tokens - WINDOW + jnp.arange(tokens + WINDOW, dtype=jnp.int32)
    starts = jnp.max(
        jnp.where(
            ends[:, None, :] <= query_pos[None, :, None],
            ends[:, None, :],
            jnp.zeros_like(ends[:, None, :]),
        ),
        axis=2,
    )
    allowed = (
        (key_pos[None, None, :] >= starts[:, :, None])
        & (key_pos[None, None, :] <= query_pos[None, :, None])
        & (query_pos[None, :, None] - key_pos[None, None, :] < WINDOW)
    )
    return allowed[:, None]


def scores_of(queries, keys_all, allowed):
    score_scale = 1.0 / math.sqrt(HEAD_DIM)
    scores = (
        jnp.einsum(
            "rqhd,rkhd->rhqk",
            split_heads(queries),
            split_heads(keys_all),
            preferred_element_type=jnp.float32,
        )
        * score_scale
    )
    return jnp.where(allowed, scores, -1e30)


def gathered_by_xla(shards):
    return [lax.all_gather(s, ("seq", "rows"), axis=0, tiled=True) for s in shards]


def scattered_by_xla(totals):
    return [
        lax.psum_scatter(t.astype(jnp.float32), ("seq", "rows"), scatter_dimension=0, tiled=True)
        for t in totals
    ]


class Place:
    def __init__(self):
        seq, rows = lax.axis_index("seq"), lax.axis_index("rows")
        self.z, self.c = seq // 2, seq % 2
        self.y, self.x = rows // 2, rows % 2
        self.turn_y, self.turn_x = 1 - 2 * self.y, 1 - 2 * self.x

    def column(self, near, far):
        y, x, c = self.y, self.x, self.c
        if near:
            y, x = y + c * self.turn_y, x + (1 - c) * self.turn_x
        if far:
            y, x = y + (1 - c) * self.turn_y, x + c * self.turn_x
        return y, x

    def device(self, z, c, column):
        return (2 * z + c, 2 * column[0] + column[1])

    def near(self):
        return self.device(self.z, self.c, self.column(True, False))

    def far(self):
        return self.device(self.z, self.c, self.column(False, True))

    def peer(self):
        return self.device(self.z, 1 - self.c, (self.y, self.x))

    def along_z(self, step):
        return self.device((self.z + step) % 4, self.c, (self.y, self.x))

    def following(self):
        return ((2 * self.z + self.c + 1) % 8, 2 * self.y + self.x)

    def preceding(self):
        return ((2 * self.z + self.c + 7) % 8, 2 * self.y + self.x)

    def cross(self):
        return ((2 * self.z + self.c + 7 - 6 * self.c) % 8, 2 * self.y + self.x)

    def partners(self):
        return [self.near(), self.far(), self.peer()] + [self.along_z(i) for i in (1, 2, 3)]


def greet(partners):
    barrier = pltpu.get_barrier_semaphore()
    for partner in partners:
        pl.semaphore_signal(barrier, inc=1, device_id=partner, device_id_type=MESH)
    pl.semaphore_wait(barrier, len(partners))


def remote(source, target, send, recv, device):
    return pltpu.make_async_remote_copy(
        src_ref=source, dst_ref=target, send_sem=send, recv_sem=recv,
        device_id=device, device_id_type=MESH,
    )


SEQ_PIECES = 8
ROW_GROUPS = 4
TILE = 256
HALF = 512
PAD = 128


def nt_dot(left, right):
    return lax.dot_general(left, right, (((1,), (1,)), ((), ())), preferred_element_type=jnp.float32)


def tn_dot(left, right):
    return lax.dot_general(left, right, (((0,), (0,)), ((), ())), preferred_element_type=jnp.float32)


def mm(left, right):
    return jnp.dot(left, right, preferred_element_type=jnp.float32)


def flat(value):
    return value.reshape(-1, value.shape[-1])


class Gather:
    def __init__(self, here, own_sem, send, recv):
        self.here, self.own_sem, self.send, self.recv = here, own_sem, send, recv
        self.own, self.near = here.column(False, False), here.column(True, False)
        self.far, self.both = here.column(False, True), here.column(True, True)

    def slot(self, whole, z):
        return whole.at[z, self.here.c, self.own[0], self.own[1]]

    def block(self, whole, core, column):
        return whole.at[:, core, column[0], column[1]]

    def copy(self, k, number, view, device):
        return remote(view, view, self.send.at[k, number], self.recv.at[k, number], device)

    def fetch(self, k, parts, whole):
        slot = self.slot(whole, self.here.z)
        return [
            pltpu.make_async_copy(view, slot.at[:, pl.ds(first, width)], self.own_sem.at[k, i])
            for i, (view, first, width) in enumerate(parts)
        ]

    def first(self, k, parts, whole):
        for copy in self.fetch(k, parts, whole):
            copy.wait()
        slot = self.slot(whole, self.here.z)
        for step in (1, 2, 3):
            self.copy(k, step - 1, slot, self.here.along_z(step)).start()

    def second(self, k, whole):
        here = self.here
        for step in (1, 2, 3):
            self.copy(k, step - 1, self.slot(whole, (here.z + 4 - step) % 4), here.along_z(step)).wait()
        block = self.block(whole, here.c, self.own)
        self.copy(k, 3, block, here.near()).start()
        self.copy(k, 4, block, here.far()).start()
        self.copy(k, 6, block, here.peer()).start()

    def third(self, k, whole):
        here = self.here
        block = self.block(whole, here.c, self.near)
        self.copy(k, 3, block, here.near()).wait()
        self.copy(k, 5, block, here.far()).start()
        self.copy(k, 7, block, here.peer()).start()

    def fourth(self, k, whole):
        here = self.here
        for number, column in ((4, self.far), (5, self.both)):
            block = self.block(whole, here.c, column)
            self.copy(k, number, block, here.far()).wait()
            self.copy(k, number + 4, block, here.peer()).start()

    def fifth(self, k, whole):
        here = self.here
        for number, column in ((6, self.own), (7, self.near), (8, self.far), (9, self.both)):
            self.copy(k, number, self.block(whole, 1 - here.c, column), here.peer()).wait()


def forward_kernel(
    x_ref, og_ref, lengths_ref, gains_in, wq_in, wk_in, wv_in, wo_in, wg_in, wu_in, wd_in,
    out_ref, gm_ref, no_ref, q_ref, k_ref, v_ref, at_ref, p_ref, wa_out, gr_out, norm_ref,
    wn, wa, wm, mid, acc, gn, nt, side, side_peer, nt_t, og_t, tri, tri_peer, stage,
    own_sem, send, recv, halo_send, halo_recv, side_send, side_recv, tri_send, tri_recv,
    keep_sem, stage_sem,
):
    here = Place()
    z, c = here.z, here.c
    seq = lax.axis_index("seq")
    tiles = wm.shape[0]
    scale = 1.0 / math.sqrt(HEAD_DIM)
    tokens = x_ref.shape[0] // 2
    gather = Gather(here, own_sem, send, recv)

    attn = [(gains_in, 0, LANES)]
    for source in (wk_in, wv_in, wq_in, wo_in):
        attn += [(source, 0, HALF), (source, HALF, HALF)]
    early = len(attn)
    total = early + tiles

    def whole_of(k):
        return wn if k == 0 else wa.at[k - 1]

    def attn_parts(k):
        source, first, width = attn[k]
        return [(source.at[:, pl.ds(first, width)], 0, width)]

    def mlp_parts(f):
        column = pl.ds(pl.multiple_of(f * TILE, TILE), TILE)
        return [(w.at[:, column], i * TILE, TILE) for i, w in enumerate((wg_in, wu_in, wd_in))]

    for k in range(early):
        for copy in gather.fetch(k, attn_parts(k), whole_of(k)):
            copy.start()

    @pl.loop(0, tiles)
    def _(f):
        for copy in gather.fetch(early + f, mlp_parts(f), wm.at[f]):
            copy.start()

    @pl.when(seq == 0)
    def _():
        k_ref[:, 0:PAD, :] = jnp.zeros((2, PAD, k_ref.shape[2]), jnp.bfloat16)
        v_ref[:, 0:PAD, :] = jnp.zeros((2, PAD, v_ref.shape[2]), jnp.bfloat16)

    @pl.when(seq > 0)
    def _():
        k_ref[:, 0 : PAD - WINDOW, :] = jnp.zeros((2, PAD - WINDOW, k_ref.shape[2]), jnp.bfloat16)
        v_ref[:, 0 : PAD - WINDOW, :] = jnp.zeros((2, PAD - WINDOW, v_ref.shape[2]), jnp.bfloat16)

    greet(here.partners() + [here.cross()])

    def tick(t):
        for lag in range(5):
            k = t - lag
            if not 0 <= k < total:
                continue
            whole = whole_of(k) if k < early else wm.at[k - early]
            if lag == 0:
                gather.first(k, attn_parts(k) if k < early else mlp_parts(k - early), whole)
            else:
                (gather.second, gather.third, gather.fourth, gather.fifth)[lag - 1](k, whole)

    def keep(k):
        return pltpu.make_async_copy(wa.at[k - 1], wa_out.at[k - 1], keep_sem.at[k - 1])

    def halo(which):
        ref = (k_ref, v_ref)[which]
        ends = ref.at[:, pl.ds(ref.shape[1] - WINDOW, WINDOW), :]
        begins = ref.at[:, pl.ds(PAD - WINDOW, WINDOW), :]
        return remote(ends, begins, halo_send.at[which], halo_recv.at[which], here.following())

    def sides(number):
        return remote(
            side.at[number, :, 1 - c], side_peer.at[number],
            side_send.at[number], side_recv.at[number], here.peer(),
        )

    def spread(number, value):
        for i in range(8):
            side[number, i // 2, i % 2] = value[:, i * LANES : (i + 1) * LANES]

    def turned(number, target):
        for level in range(4):
            rows = slice(level * LANES, (level + 1) * LANES)
            target[rows, 0 : 2 * tokens] = (
                side[number, level, c].astype(jnp.float32).T.astype(jnp.bfloat16)
            )
            target[rows, 2 * tokens : 4 * tokens] = (
                side_peer[number, level].astype(jnp.float32).T.astype(jnp.bfloat16)
            )

    for t in range(4):
        tick(t)
        if t == 1:
            spread(0, og_ref[...])
            sides(0).start()
        if t == 3:
            sides(0).wait()
            turned(0, og_t)

    tick(4)
    gain_rows = flat(wn[...]).astype(jnp.float32).T
    norm_ref[0:8, :] = jnp.broadcast_to(gain_rows[0:1, :], (8, gain_rows.shape[1]))
    norm_ref[8:16, :] = jnp.broadcast_to(gain_rows[64:65, :], (8, gain_rows.shape[1]))
    x = x_ref[...].astype(jnp.float32)
    factor = lax.rsqrt(jnp.mean(x * x, axis=-1, keepdims=True) + 1e-05)
    no_ref[...] = (x * factor * norm_ref[0:1, :]).astype(jnp.bfloat16)

    def projected(k):
        tick(4 + k)
        keep(k).start()
        return mm(no_ref[...], flat(wa[k - 1])).astype(jnp.bfloat16)

    for k in range(1, 7):
        part = projected(k)
        cols = slice(((k - 1) % 2) * HALF, ((k - 1) % 2 + 1) * HALF)
        if k < 5:
            ref = k_ref if k < 3 else v_ref
            ref[:, PAD : PAD + tokens, cols] = part.reshape(2, tokens, HALF)
        else:
            q_ref[:, cols] = part
        if k in (2, 4):

            @pl.when(seq < SEQ_PIECES - 1)
            def _(which=k // 2 - 1):
                halo(which).start()

    for which in range(2):

        @pl.when(seq > 0)
        def _(which=which):
            halo(which).wait_recv()

        @pl.when(seq < SEQ_PIECES - 1)
        def _(which=which):
            halo(which).wait_send()

    def attend(row):
        ends = []
        reached = 0
        for doc in range(lengths_ref.shape[1]):
            reached = reached + lengths_ref[row, doc]
            ends.append(reached)
        query_pos = seq * tokens + lax.broadcasted_iota(jnp.int32, (tokens, PAD + tokens), 0)
        key_pos = seq * tokens - PAD + lax.broadcasted_iota(jnp.int32, (tokens, PAD + tokens), 1)
        start = jnp.zeros((tokens, PAD + tokens), jnp.int32)
        for end in ends:
            start = jnp.maximum(start, jnp.where(query_pos >= end, end, 0))
        allowed = (key_pos >= start) & (key_pos <= query_pos) & (query_pos - key_pos < WINDOW)
        for head in range(HEADS):
            cols = slice(head * HEAD_DIM, (head + 1) * HEAD_DIM)
            rows = slice(row * tokens, (row + 1) * tokens)
            scores = nt_dot(q_ref[rows, cols], k_ref[row, :, cols]) * scale
            scores = jnp.where(allowed, scores, -1e30)
            exps = jnp.exp(scores - jnp.max(scores, axis=-1, keepdims=True))
            probs = exps / jnp.sum(exps, axis=-1, keepdims=True)
            p_ref[row * HEADS + head] = probs
            at_ref[rows, cols] = mm(probs.astype(jnp.bfloat16), v_ref[row, :, cols]).astype(jnp.bfloat16)

    attend(0)
    tick(11)
    keep(7).start()
    attend(1)
    tick(12)
    keep(8).start()
    for k in (7, 8):
        cols = slice((k - 7) * HALF, (k - 6) * HALF)
        mid[:, cols] = x_ref[:, cols].astype(jnp.float32) + mm(at_ref[...], flat(wa[k - 1]))

    middle = mid[...]
    factor = lax.rsqrt(jnp.mean(middle * middle, axis=-1, keepdims=True) + 1e-05)
    normed_two = (middle * factor * norm_ref[8:9, :]).astype(jnp.bfloat16)
    nt[...] = normed_two
    spread(1, normed_two)
    sides(1).start()
    acc[...] = middle
    gn[...] = jnp.zeros(gn.shape, jnp.float32)
    sides(1).wait()
    turned(1, nt_t)

    def to_peer(f):
        return remote(tri.at[f % 2], tri_peer.at[f], tri_send.at[f], tri_recv.at[f], here.peer())

    def stored(f):
        return pltpu.make_async_copy(stage.at[f % 2], gr_out.at[f], stage_sem.at[f])

    def weight_grads(f):
        to_peer(f).wait()

        @pl.when(f >= 2)
        def _():
            stored(f - 2).wait()

        n = 2 * tokens
        for i, turn in ((0, nt_t), (1, nt_t), (2, og_t)):
            grad = mm(turn[:, 0:n], tri[f % 2, i]) + mm(turn[:, n : 2 * n], tri_peer[f, i])
            stage[f % 2, :, :, :, :, i * TILE : (i + 1) * TILE] = (
                grad.astype(jnp.bfloat16).reshape(4, 2, 2, -1, TILE)
            )
        stored(f).start()

    @pl.loop(0, tiles)
    def _(f):
        for lag, step in enumerate((None, gather.second, gather.third, gather.fourth)):
            ahead = f + 4 - lag

            @pl.when(ahead < tiles)
            def _(ahead=ahead, step=step):
                if step is None:
                    gather.first(early + ahead, mlp_parts(ahead), wm.at[ahead])
                else:
                    step(early + ahead, wm.at[ahead])

        gather.fifth(early + f, wm.at[f])
        w_gate = flat(wm[f, :, :, :, :, :, 0:TILE])
        w_up = flat(wm[f, :, :, :, :, :, TILE : 2 * TILE])
        w_down = flat(wm[f, :, :, :, :, :, 2 * TILE : 3 * TILE])
        gates = mm(nt[...], w_gate)
        ups = mm(nt[...], w_up)
        grad_hidden = mm(og_ref[...], w_down)
        sigmoid = 1.0 / (1.0 + jnp.exp(-gates))
        silu = gates * sigmoid
        hidden = (silu * ups).astype(jnp.bfloat16)
        grad_gates = (grad_hidden * ups * sigmoid * (1.0 + gates * (1.0 - sigmoid))).astype(jnp.bfloat16)
        grad_ups = (grad_hidden * silu).astype(jnp.bfloat16)
        tri[f % 2, 0] = grad_gates
        tri[f % 2, 1] = grad_ups
        tri[f % 2, 2] = hidden
        to_peer(f).start()
        acc[...] += nt_dot(hidden, w_down)
        gn[...] += nt_dot(grad_gates, w_gate) + nt_dot(grad_ups, w_up)

        @pl.when(f >= 1)
        def _():
            weight_grads(f - 1)

    weight_grads(tiles - 1)
    out_ref[...] = acc[...].astype(jnp.bfloat16)
    middle = mid[...]
    factor = lax.rsqrt(jnp.mean(middle * middle, axis=-1, keepdims=True) + 1e-05)
    grad_normed = gn[...]
    through = grad_normed * norm_ref[8:9, :]
    shift = jnp.mean(through * middle, axis=-1, keepdims=True) * factor * factor * factor
    gm_ref[...] = og_ref[...].astype(jnp.float32) + factor * through - middle * shift
    norm_ref[8:16, :] = jnp.broadcast_to(
        jnp.sum(grad_normed * middle * factor, axis=0, keepdims=True), (8, middle.shape[1])
    )
    stored(tiles - 2).wait()
    stored(tiles - 1).wait()
    for k in range(1, early):
        keep(k).wait()


def forward(hidden, out_grad, lengths, gains, weights):
    tokens, width = hidden.shape
    rows = gains.shape[0]
    tiles = weights[4].shape[1] // TILE
    low, full = jnp.bfloat16, jnp.float32
    whole = (4, 2, 2, 2, rows)
    early = 9
    count = early + tiles
    dma = pltpu.SemaphoreType.DMA
    vmem, anywhere = pl.BlockSpec(memory_space=pltpu.VMEM), pl.BlockSpec(memory_space=pl.ANY)
    shape = jax.ShapeDtypeStruct
    keys = (2, PAD + tokens // 2, width)
    return pl.pallas_call(
        forward_kernel,
        out_shape=[
            shape((tokens, width), low), shape((tokens, width), full), shape((tokens, width), low),
            shape((tokens, width), low), shape(keys, low), shape(keys, low),
            shape((tokens, width), low), shape((2 * HEADS, tokens // 2, PAD + tokens // 2), full),
            shape((8, *whole, HALF), low), shape((tiles, 4, 2, 2, rows, 3 * TILE), low),
            shape((16, width), full),
        ],
        in_specs=[vmem, vmem, pl.BlockSpec(memory_space=pltpu.SMEM)] + [anywhere] * 8,
        out_specs=[vmem] * 8 + [anywhere] * 2 + [vmem],
        scratch_shapes=[
            pltpu.VMEM((*whole, LANES), low), pltpu.VMEM((8, *whole, HALF), low),
            pltpu.VMEM((tiles, *whole, 3 * TILE), low),
            pltpu.VMEM((tokens, width), full), pltpu.VMEM((tokens, width), full),
            pltpu.VMEM((tokens, width), full), pltpu.VMEM((tokens, width), low),
            pltpu.VMEM((2, 4, 2, tokens, LANES), low), pltpu.VMEM((2, 4, tokens, LANES), low),
            pltpu.VMEM((width // 2, 2 * tokens), low), pltpu.VMEM((width // 2, 2 * tokens), low),
            pltpu.VMEM((2, 3, tokens, TILE), low), pltpu.VMEM((tiles, 3, tokens, TILE), low),
            pltpu.VMEM((2, 4, 2, 2, rows, 3 * TILE), low),
            dma((count, 3)), dma((count, 10)), dma((count, 10)), dma((2,)), dma((2,)),
            dma((2,)), dma((2,)), dma((tiles,)), dma((tiles,)), dma((8,)), dma((tiles,)),
        ],
        compiler_params=pltpu.CompilerParams(
            collective_id=0, has_side_effects=True, vmem_limit_bytes=60 * 2**20
        ),
        name="gather_and_forward",
    )(hidden, out_grad, lengths, gains, *weights)


class Scatter:
    def __init__(self, here, send, recv):
        self.here, self.send, self.recv = here, send, recv
        self.own, self.near = here.column(False, False), here.column(True, False)
        self.far, self.both = here.column(False, True), here.column(True, True)

    def copy(self, k, number, source, target, device):
        return remote(source, target, self.send.at[k, number], self.recv.at[k, number], device)

    def to_far(self, k, source, twos):
        return [
            self.copy(k, i, source.at[:, column[0], column[1]], twos.at[i], self.here.far())
            for i, column in enumerate((self.both, self.far))
        ]

    def to_near(self, k, near, twos):
        return self.copy(k, 2, near, twos.at[2], self.here.near())

    def to_z(self, k, own, fours, step):
        return self.copy(
            k, 2 + step, own.at[(self.here.z + step) % 4], fours.at[step - 1], self.here.along_z(step)
        )

    def first(self, k, source, twos):
        for copy in self.to_far(k, source, twos):
            copy.start()

    def add(self, target, other):
        @pl.loop(0, 4)
        def _(level):
            target[level] = (
                target[level].astype(jnp.float32) + other[level].astype(jnp.float32)
            ).astype(jnp.bfloat16)

    def second(self, k, source, own, near, twos):
        both, far = self.to_far(k, source, twos)
        both.wait()
        self.add(near, twos.at[0])
        self.to_near(k, near, twos).start()
        far.wait()
        self.add(own, twos.at[1])

    def third(self, k, own, near, twos, fours):
        self.to_near(k, near, twos).wait()
        self.add(own, twos.at[2])
        for step in (1, 2, 3):
            self.to_z(k, own, fours, step).start()

    def fourth(self, k, own, fours):
        for step in (1, 2, 3):
            self.to_z(k, own, fours, step).wait()
        total = own[self.here.z].astype(jnp.float32)
        for step in (1, 2, 3):
            total = total + fours[step - 1].astype(jnp.float32)
        return total


def backward_kernel(
    x_ref, gm_ref, no_ref, q_ref, k_ref, v_ref, at_ref, p_ref, norm_in, wa_in, gr_in,
    gi_ref, oq_ref, ok_ref, ov_ref, oo_ref, og_ref, ou_ref, od_ref, on_ref,
    wa, gat, gk_full, gv_full, edge, edge_in, outs, outs_peer, side, side_peer, no_t, at_t,
    mine, mlp_twos, mlp_fours, mg, attn_twos, attn_fours, nb, nb_peer, nb_sum, norm_twos, norm_fours,
    own_sem, send, recv, edge_send, edge_recv, side_send, side_recv, out_send, out_recv, pair_send,
    pair_recv, wa_sem,
):
    here = Place()
    z, c = here.z, here.c
    seq = lax.axis_index("seq")
    tiles = gr_in.shape[0]
    scale = 1.0 / math.sqrt(HEAD_DIM)
    tokens = x_ref.shape[0] // 2
    scatter = Scatter(here, send, recv)
    own, near = scatter.own, scatter.near
    attn = mg.shape[0]
    norm_at = tiles + attn - 1
    total = tiles + attn + 1

    @pl.when(seq == SEQ_PIECES - 1)
    def _():
        edge_in[...] = jnp.zeros(edge_in.shape, jnp.bfloat16)

    greet(here.partners() + [here.cross()])

    def chunk(k):
        if k < tiles:
            return gr_in.at[k], mine.at[k, 0], mine.at[k, 1], mlp_twos.at[k], mlp_fours.at[k]
        if k == norm_at:
            source, twos, fours = nb_sum, norm_twos, norm_fours
        else:
            i = k - tiles - (1 if k > norm_at else 0)
            source, twos, fours = mg.at[i], attn_twos.at[i], attn_fours.at[i]
        return source, source.at[:, own[0], own[1]], source.at[:, near[0], near[1]], twos, fours

    def fetches(k):
        return [
            pltpu.make_async_copy(gr_in.at[k, :, column[0], column[1]], mine.at[k, i], own_sem.at[k, i])
            for i, column in enumerate((own, near))
        ]

    weights = [pltpu.make_async_copy(wa_in.at[i], wa.at[i], wa_sem.at[i]) for i in range(8)]

    def store(k, value):
        if k < tiles:
            for i, ref in enumerate((og_ref, ou_ref, od_ref)):
                ref[:, k * TILE : (k + 1) * TILE] = value[:, i * TILE : (i + 1) * TILE]
        elif k == norm_at:
            on_ref[...] = value
        else:
            i = k - tiles - (1 if k > norm_at else 0)
            ref = (oo_ref, ov_ref, ok_ref, oq_ref)[i // 2]
            ref[:, (i % 2) * HALF : (i % 2 + 1) * HALF] = value

    def tick(t):
        for lag in range(4):
            k = t - lag
            if not 0 <= k < total:
                continue
            source, own_block, near_block, twos, fours = chunk(k)
            if lag == 0:
                scatter.first(k, source, twos)
                if k < tiles:
                    for copy in fetches(k):
                        copy.start()
            elif lag == 1:
                if k < tiles:
                    for copy in fetches(k):
                        copy.wait()
                scatter.second(k, source, own_block, near_block, twos)
            elif lag == 2:
                scatter.third(k, own_block, near_block, twos, fours)
            else:
                store(k, scatter.fourth(k, own_block, fours))

    def sides(number):
        return remote(
            side.at[number, :, 1 - c], side_peer.at[number],
            side_send.at[number], side_recv.at[number], here.peer(),
        )

    def spread(number, value):
        for i in range(8):
            side[number, i // 2, i % 2] = value[:, i * LANES : (i + 1) * LANES]

    def turned(number, target):
        for level in range(4):
            rows = slice(level * LANES, (level + 1) * LANES)
            target[rows, 0 : 2 * tokens] = (
                side[number, level, c].astype(jnp.float32).T.astype(jnp.bfloat16)
            )
            target[rows, 2 * tokens : 4 * tokens] = (
                side_peer[number, level].astype(jnp.float32).T.astype(jnp.bfloat16)
            )

    def out_copy(number):
        return remote(
            outs.at[number], outs_peer.at[number], out_send.at[number], out_recv.at[number], here.peer()
        )

    def edge_copy():
        return remote(edge, edge_in, edge_send.at[0], edge_recv.at[0], here.preceding())

    def pair_copy():
        return remote(nb.at[:, 1 - c], nb_peer, pair_send.at[0], pair_recv.at[0], here.peer())

    def begin():
        for copy in weights[6:] + weights[:6]:
            copy.start()
        outs[0] = gm_ref[...].astype(jnp.bfloat16)
        out_copy(0).start()
        spread(0, at_ref[...])
        sides(0).start()
        spread(1, no_ref[...])
        sides(1).start()

    def to_attended():
        for i in (6, 7):
            weights[i].wait()
        grad = nt_dot(outs[0, :, 0:HALF], flat(wa[6])) + nt_dot(outs[0, :, HALF:], flat(wa[7]))
        gat[...] = grad.astype(jnp.bfloat16)

    def attend_back(row):
        rows = slice(row * tokens, (row + 1) * tokens)
        for head in range(HEADS):
            cols = slice(head * HEAD_DIM, (head + 1) * HEAD_DIM)
            grad = gat[rows, cols]
            probs = p_ref[row * HEADS + head]
            gv_full[row, :, cols] = tn_dot(probs.astype(jnp.bfloat16), grad)
            grad_probs = nt_dot(grad, v_ref[row, :, cols])
            inner = jnp.sum(grad_probs * probs, axis=-1, keepdims=True)
            grad_scores = (probs * (grad_probs - inner)).astype(jnp.bfloat16)
            outs[3, rows, cols] = (mm(grad_scores, k_ref[row, :, cols]) * scale).astype(jnp.bfloat16)
            gk_full[row, :, cols] = tn_dot(grad_scores, q_ref[rows, cols]) * scale
        before = slice(PAD - WINDOW, PAD)
        edge[0, row] = gk_full[row, before, :].astype(jnp.bfloat16)
        edge[1, row] = gv_full[row, before, :].astype(jnp.bfloat16)

    def send_edge():
        out_copy(3).start()

        @pl.when(seq > 0)
        def _():
            edge_copy().start()

    def close_edge():
        @pl.when(seq < SEQ_PIECES - 1)
        def _():
            edge_copy().wait_recv()

        @pl.when(seq > 0)
        def _():
            edge_copy().wait_send()

        inside = tokens - WINDOW
        for which, number, source in ((0, 2, gk_full), (1, 1, gv_full)):
            for row in range(2):
                first = row * tokens
                outs[number, first : first + inside, :] = (
                    source[row, PAD : PAD + inside, :].astype(jnp.bfloat16)
                )
                outs[number, first + inside : first + tokens, :] = (
                    source[row, PAD + inside : PAD + tokens, :]
                    + edge_in[which, row].astype(jnp.float32)
                ).astype(jnp.bfloat16)
        out_copy(1).start()
        out_copy(2).start()

    def to_input():
        for i in range(6):
            weights[i].wait()
        grad_normed = jnp.zeros(gi_ref.shape, jnp.float32)
        for number, i in ((2, 0), (1, 2), (3, 4)):
            grad_normed = grad_normed + (
                nt_dot(outs[number, :, 0:HALF], flat(wa[i])) + nt_dot(outs[number, :, HALF:], flat(wa[i + 1]))
            )
        x = x_ref[...].astype(jnp.float32)
        factor = lax.rsqrt(jnp.mean(x * x, axis=-1, keepdims=True) + 1e-05)
        through = grad_normed * norm_in[0:1, :]
        shift = jnp.mean(through * x, axis=-1, keepdims=True) * factor * factor * factor
        gi_ref[...] = gm_ref[...] + factor * through - x * shift
        one = jnp.sum(grad_normed * x * factor, axis=0, keepdims=True)
        width = one.shape[1]
        stacked = jnp.concatenate(
            [
                jnp.broadcast_to(one, (LANES // 2, width)),
                jnp.broadcast_to(norm_in[8:9, :], (LANES // 2, width)),
            ],
            axis=0,
        )
        nb[...] = stacked.T.astype(jnp.bfloat16).reshape(nb.shape)
        pair_copy().start()

    def close_norm():
        pair_copy().wait()
        nb_sum[...] = (
            nb[:, c].astype(jnp.float32) + nb_peer[...].astype(jnp.float32)
        ).astype(jnp.bfloat16)

    def weight_grads(number):
        out_copy(number).wait()
        turn = at_t if number == 0 else no_t
        n = 2 * tokens
        for half in range(2):
            cols = slice(half * HALF, (half + 1) * HALF)
            grad = mm(turn[:, 0:n], outs[number, :, cols]) + mm(turn[:, n : 2 * n], outs_peer[number, :, cols])
            mg[2 * number + half] = grad.astype(jnp.bfloat16).reshape(mg.shape[1:])

    def turn_sides():
        sides(0).wait()
        turned(0, at_t)
        sides(1).wait()
        turned(1, no_t)

    work = {
        0: [begin], 1: [to_attended], 2: [lambda: attend_back(0)], 3: [lambda: attend_back(1), send_edge],
        4: [turn_sides], 5: [close_edge], 6: [to_input], 7: [lambda: weight_grads(0)],
        8: [lambda: weight_grads(1), close_norm], 9: [lambda: weight_grads(2)], 10: [lambda: weight_grads(3)],
    }
    for t in range(total + 3):
        tick(t)
        for step in work.get(t, ()):
            step()


def backward(hidden, saved):
    grad_middle, normed, queries, keys, values, attended, probs, weights, grads, norm = saved
    tokens, width = hidden.shape
    tiles, rows = grads.shape[0], grads.shape[4]
    low, full = jnp.bfloat16, jnp.float32
    dma = pltpu.SemaphoreType.DMA
    vmem, anywhere = pl.BlockSpec(memory_space=pltpu.VMEM), pl.BlockSpec(memory_space=pl.ANY)
    shape = jax.ShapeDtypeStruct
    attn = 8
    total = tiles + attn + 1
    wide, grid = 3 * TILE, (4, 2, 2, rows)
    scratch = [
        ((8, 4, 2, 2, 2, rows, HALF), low), ((tokens, width), low),
        (keys.shape, full), (keys.shape, full),
        ((2, 2, WINDOW, width), low), ((2, 2, WINDOW, width), low),
        ((4, tokens, width), low), ((4, tokens, width), low),
        ((2, 4, 2, tokens, LANES), low), ((2, 4, tokens, LANES), low),
        ((width // 2, 2 * tokens), low), ((width // 2, 2 * tokens), low),
        ((tiles, 2, 4, rows, wide), low), ((tiles, 3, 4, rows, wide), low), ((tiles, 3, rows, wide), low),
        ((attn, *grid, HALF), low), ((attn, 3, 4, rows, HALF), low), ((attn, 3, rows, HALF), low),
        ((4, 2, 2, 2, rows, LANES), low), ((*grid, LANES), low), ((*grid, LANES), low),
        ((3, 4, rows, LANES), low), ((3, rows, LANES), low),
    ]
    return pl.pallas_call(
        backward_kernel,
        out_shape=[shape((tokens, width), full)]
        + [shape((rows, width), full)] * 4 + [shape((rows, tiles * TILE), full)] * 3
        + [shape((rows, LANES), full)],
        in_specs=[vmem] * 9 + [anywhere] * 2,
        out_specs=[vmem] * 9,
        scratch_shapes=[pltpu.VMEM(*s) for s in scratch]
        + [
            dma((tiles, 2)), dma((total, 6)), dma((total, 6)), dma((1,)), dma((1,)), dma((2,)), dma((2,)),
            dma((4,)), dma((4,)), dma((1,)), dma((1,)), dma((8,)),
        ],
        compiler_params=pltpu.CompilerParams(
            collective_id=1, has_side_effects=True, vmem_limit_bytes=62 * 2**20
        ),
        name="scatter_and_backward",
    )(hidden, grad_middle, normed, queries, keys, values, attended, probs, norm, weights, grads)


def fused(hidden_in, lengths, out_grad, gain_shards, weight_shards):
    flat_in = hidden_in.reshape(-1, hidden_in.shape[-1])
    flat_grad = out_grad.reshape(flat_in.shape)
    gains = jnp.concatenate(
        [jnp.broadcast_to(g[:, None], (g.shape[0], LANES // 2)) for g in gain_shards], axis=1
    )
    block_out, *saved = forward(flat_in, flat_grad, lengths, gains, weight_shards)
    grad_in, query, key, value, wout, gate, up, down, norms = backward(flat_in, saved)
    return (
        block_out.reshape(hidden_in.shape), grad_in.reshape(hidden_in.shape),
        norms[:, 0], query, key, value, wout, norms[:, LANES // 2], gate, up, down,
    )


def layer(hidden_in, lengths, out_grad, gains, weights):
    score_scale = 1.0 / math.sqrt(HEAD_DIM)
    tokens = hidden_in.shape[1]
    gain_one, gain_two = gains
    w_query, w_key, w_value, w_out, w_gate, w_up, w_down = weights
    inputs = hidden_in.astype(jnp.float32)
    normed_one = rms_scale(inputs, gain_one).astype(jnp.bfloat16)
    queries = project(normed_one, w_query).astype(jnp.bfloat16)
    keys = project(normed_one, w_key).astype(jnp.bfloat16)
    values = project(normed_one, w_value).astype(jnp.bfloat16)
    tails = jnp.stack([keys[:, tokens - WINDOW :], values[:, tokens - WINDOW :]])
    received = passed_along(tails, "seq", 1)
    keys_all = jnp.concatenate([received[0], keys], axis=1)
    values_all = jnp.concatenate([received[1], values], axis=1)
    allowed = window_mask(lengths, lax.axis_index("seq"), tokens)
    scores = scores_of(queries, keys_all, allowed)
    top = jnp.max(scores, axis=-1, keepdims=True)
    exps = jnp.exp(scores - top)
    probs = exps / jnp.sum(exps, axis=-1, keepdims=True)
    probs_low = probs.astype(jnp.bfloat16)
    mixed = jnp.einsum(
        "rhqk,rkhd->rqhd", probs_low, split_heads(values_all), preferred_element_type=jnp.float32
    )
    attended = merge_heads(mixed).astype(jnp.bfloat16)
    middle = inputs + project(attended, w_out)
    normed_two = rms_scale(middle, gain_two).astype(jnp.bfloat16)
    gates = project(normed_two, w_gate)
    ups = project(normed_two, w_up)
    hidden_act = swiglu(gates, ups).astype(jnp.bfloat16)
    block_out = (middle + project_back(hidden_act, w_down)).astype(jnp.bfloat16)
    grad_hidden = project(out_grad, w_down)
    unused, swiglu_back = jax.vjp(swiglu, gates, ups)
    grad_gates, grad_ups = swiglu_back(grad_hidden)
    grad_gates = grad_gates.astype(jnp.bfloat16)
    grad_ups = grad_ups.astype(jnp.bfloat16)
    grad_down = weight_grad(out_grad, hidden_act)
    grad_gate = weight_grad(normed_two, grad_gates)
    grad_up = weight_grad(normed_two, grad_ups)
    grad_normed_two = project_back(grad_gates, w_gate) + project_back(grad_ups, w_up)
    unused, norm_two_back = jax.vjp(rms_scale, middle, gain_two)
    grad_middle_part, grad_norm2 = norm_two_back(grad_normed_two)
    grad_middle = out_grad.astype(jnp.float32) + grad_middle_part
    grad_branch = grad_middle.astype(jnp.bfloat16)
    grad_wout = weight_grad(attended, grad_branch)
    grad_attended = project_back(grad_branch, w_out).astype(jnp.bfloat16)
    grad_heads = split_heads(grad_attended)
    grad_values_all = jnp.einsum(
        "rhqk,rqhd->rkhd", probs_low, grad_heads, preferred_element_type=jnp.float32
    )
    grad_probs = jnp.einsum(
        "rqhd,rkhd->rhqk", grad_heads, split_heads(values_all), preferred_element_type=jnp.float32
    )
    grad_scores = (
        probs * (grad_probs - jnp.sum(grad_probs * probs, axis=-1, keepdims=True))
    ).astype(jnp.bfloat16)
    grad_queries = score_scale * merge_heads(
        jnp.einsum(
            "rhqk,rkhd->rqhd", grad_scores, split_heads(keys_all),
            preferred_element_type=jnp.float32,
        )
    )
    grad_keys_all = score_scale * merge_heads(
        jnp.einsum(
            "rhqk,rqhd->rkhd", grad_scores, split_heads(queries),
            preferred_element_type=jnp.float32,
        )
    )
    grad_values_all = merge_heads(grad_values_all)
    halo_grads = jnp.stack([grad_keys_all[:, :WINDOW], grad_values_all[:, :WINDOW]])
    returned = passed_along(halo_grads.astype(jnp.bfloat16), "seq", -1).astype(halo_grads.dtype)
    grad_keys = (
        grad_keys_all[:, WINDOW:].at[:, tokens - WINDOW :].add(returned[0]).astype(jnp.bfloat16)
    )
    grad_values = (
        grad_values_all[:, WINDOW:].at[:, tokens - WINDOW :].add(returned[1]).astype(jnp.bfloat16)
    )
    grad_queries = grad_queries.astype(jnp.bfloat16)
    grad_query = weight_grad(normed_one, grad_queries)
    grad_key = weight_grad(normed_one, grad_keys)
    grad_value = weight_grad(normed_one, grad_values)
    grad_normed_one = (
        project_back(grad_queries, w_query)
        + project_back(grad_keys, w_key)
        + project_back(grad_values, w_value)
    )
    unused, norm_one_back = jax.vjp(rms_scale, inputs, gain_one)
    grad_inputs_part, grad_norm1 = norm_one_back(grad_normed_one)
    grad_in = grad_middle + grad_inputs_part
    grads = (grad_query, grad_key, grad_value, grad_wout, grad_gate, grad_up, grad_down)
    return block_out, grad_in, (grad_norm1, grad_norm2), grads


def shards(
    hidden_in, lengths, norm1_gain, w_query, w_key, w_value, w_out,
    norm2_gain, w_gate, w_up, w_down, out_grad,
):
    gain_shards = (norm1_gain, norm2_gain)
    if (lax.axis_size("seq"), lax.axis_size("rows")) == (SEQ_PIECES, ROW_GROUPS):
        weight_shards = (w_query, w_key, w_value, w_out, w_gate, w_up, w_down)
        return fused(hidden_in, lengths, out_grad, gain_shards, weight_shards)
    weight_shards = (w_query, w_key, w_value, w_out, w_gate, w_up, w_down)
    gains = [g.astype(jnp.float32) for g in gathered_by_xla(gain_shards)]
    weights = gathered_by_xla(weight_shards)
    block_out, grad_in, norms, grads = layer(hidden_in, lengths, out_grad, gains, weights)
    norms, grads = scattered_by_xla(norms), scattered_by_xla(grads)
    return (
        block_out, grad_in, norms[0], grads[0], grads[1], grads[2], grads[3],
        norms[1], grads[4], grads[5], grads[6],
    )


def solution(mesh):
    tokens = P("rows", "seq", None)
    vector = P(("seq", "rows"))
    matrix = P(("seq", "rows"), None)
    in_specs = (
        tokens, P("rows", None), vector, matrix, matrix, matrix, matrix,
        vector, matrix, matrix, matrix, tokens,
    )
    out_specs = (
        tokens, tokens, vector, matrix, matrix, matrix, matrix,
        vector, matrix, matrix, matrix,
    )
    return jax.shard_map(shards, mesh=mesh, in_specs=in_specs, out_specs=out_specs, check_vma=False)
```

```python
import functools
import math

import jax
import jax.numpy as jnp
from jax import lax
from jax.experimental import pallas as pl
from jax.experimental.pallas import tpu as pltpu
from jax.sharding import PartitionSpec as P

HEADS = 8
HEAD_DIM = 128
WINDOW = 64
LANES = 128
MESH = pl.DeviceIdType.MESH


def passed_along(block, axis, distance):
    devices = range(lax.axis_size(axis))
    route = [(i - distance, i) for i in devices if i - distance in devices]
    return lax.ppermute(block, axis, route)


def rms_scale(values, gain):
    factor = lax.rsqrt(jnp.mean(values * values, axis=-1, keepdims=True) + 1e-05)
    return values * factor * gain


def swiglu(gates, ups):
    return jax.nn.silu(gates) * ups


def project(left, weight):
    return jnp.dot(left, weight, preferred_element_type=jnp.float32)


def project_back(grad, weight):
    return lax.dot_general(
        grad, weight, (((2,), (1,)), ((), ())), preferred_element_type=jnp.float32
    )


def weight_grad(left, grad):
    return jnp.einsum("rtd,rtf->df", left, grad, preferred_element_type=jnp.float32)


def split_heads(values):
    return values.reshape(values.shape[0], values.shape[1], HEADS, HEAD_DIM)


def merge_heads(values):
    return values.reshape(values.shape[0], values.shape[1], HEADS * HEAD_DIM)


def window_mask(lengths, seq_index, tokens):
    docs = lengths.shape[1]
    upto = jnp.arange(docs)[:, None] >= jnp.arange(docs)[None, :]
    ends = jnp.sum(jnp.where(upto[None], lengths[:, None, :], 0), axis=2)
    query_pos = seq_index * tokens + jnp.arange(tokens, dtype=jnp.int32)
    key_pos = seq_index * tokens - WINDOW + jnp.arange(tokens + WINDOW, dtype=jnp.int32)
    starts = jnp.max(
        jnp.where(
            ends[:, None, :] <= query_pos[None, :, None],
            ends[:, None, :],
            jnp.zeros_like(ends[:, None, :]),
        ),
        axis=2,
    )
    allowed = (
        (key_pos[None, None, :] >= starts[:, :, None])
        & (key_pos[None, None, :] <= query_pos[None, :, None])
        & (query_pos[None, :, None] - key_pos[None, None, :] < WINDOW)
    )
    return allowed[:, None]


def scores_of(queries, keys_all, allowed):
    score_scale = 1.0 / math.sqrt(HEAD_DIM)
    scores = (
        jnp.einsum(
            "rqhd,rkhd->rhqk",
            split_heads(queries),
            split_heads(keys_all),
            preferred_element_type=jnp.float32,
        )
        * score_scale
    )
    return jnp.where(allowed, scores, -1e30)


def gathered_by_xla(shards):
    return [lax.all_gather(s, ("seq", "rows"), axis=0, tiled=True) for s in shards]


def scattered_by_xla(totals):
    return [
        lax.psum_scatter(t.astype(jnp.float32), ("seq", "rows"), scatter_dimension=0, tiled=True)
        for t in totals
    ]


SEQ_PIECES = 8
ROW_GROUPS = 4
PART = 128
HALF = 512
PAD = 128
AHEAD = (11, 3, 2, 1)
FIRST_TILES = 7
SUM_LAGS = (0, 2, 4)


class Place:
    def __init__(self):
        seq, rows = lax.axis_index("seq"), lax.axis_index("rows")
        self.z, self.c = seq // 2, seq % 2
        self.k, self.h = self.z // 2, self.z % 2
        self.y, self.x = rows // 2, rows % 2
        self.turn_y, self.turn_x = 1 - 2 * self.y, 1 - 2 * self.x

    def column(self, near, far):
        y, x, c = self.y, self.x, self.c
        if near:
            y, x = y + c * self.turn_y, x + (1 - c) * self.turn_x
        if far:
            y, x = y + (1 - c) * self.turn_y, x + c * self.turn_x
        return y, x

    def device(self, z, c, column):
        return (2 * z + c, 2 * column[0] + column[1])

    def near(self):
        return self.device(self.z, self.c, self.column(True, False))

    def far(self):
        return self.device(self.z, self.c, self.column(False, True))

    def peer(self):
        return self.device(self.z, 1 - self.c, (self.y, self.x))

    def mate(self):
        return self.device(2 * self.k + 1 - self.h, self.c, (self.y, self.x))

    def across(self):
        return self.device(2 * (1 - self.k) + self.h, self.c, (self.y, self.x))

    def cross(self):
        return self.device(2 * (1 - self.k) + self.h, 1 - self.c, (self.y, self.x))

    def along_z(self, step):
        return self.device((self.z + step) % 4, self.c, (self.y, self.x))

    def partners(self):
        return [self.near(), self.far(), self.peer(), self.cross()] + [self.along_z(i) for i in (1, 2, 3)]


def greet(partners):
    barrier = pltpu.get_barrier_semaphore()
    for partner in partners:
        pl.semaphore_signal(barrier, inc=1, device_id=partner, device_id_type=MESH)
    pl.semaphore_wait(barrier, len(partners))


def remote(source, target, send, recv, device):
    return pltpu.make_async_remote_copy(
        src_ref=source, dst_ref=target, send_sem=send, recv_sem=recv,
        device_id=device, device_id_type=MESH,
    )


def nt_dot(left, right):
    return lax.dot_general(left, right, (((1,), (1,)), ((), ())), preferred_element_type=jnp.float32)


def tn_dot(left, right):
    return lax.dot_general(left, right, (((0,), (0,)), ((), ())), preferred_element_type=jnp.float32)


def mm(left, right):
    return jnp.dot(left, right, preferred_element_type=jnp.float32)


def flat(value):
    return value.reshape(-1, value.shape[-1])


def low(value):
    return value.astype(jnp.bfloat16)


def wide(value):
    return value.astype(jnp.float32)


def lanes_at(first, width):
    return pl.ds(pl.multiple_of(first, PART), width)


class Gather:
    def __init__(self, here, own_sem, send, recv):
        self.here, self.own_sem, self.send, self.recv = here, own_sem, send, recv
        self.own, self.near = here.column(False, False), here.column(True, False)
        self.far, self.both = here.column(False, True), here.column(True, True)

    def slot(self, whole):
        return whole.at[self.here.z, self.here.c, self.own[0], self.own[1]]

    def block(self, whole, core, column):
        return whole.at[:, core, column[0], column[1]]

    def copy(self, n, number, source, target, device):
        return remote(source, target, self.send.at[n, number], self.recv.at[n, number], device)

    def wait(self, n, number, view, device):
        self.copy(n, number, view, view, device).wait()

    def begin(self, n, parts, whole, pack):
        slot = self.slot(whole)
        for kept, given, first, width in parts:
            pltpu.make_async_copy(kept, slot.at[:, pl.ds(first, width)], self.own_sem.at[n, 0]).start()
            if pack is not None:
                pltpu.make_async_copy(given, pack.at[:, pl.ds(first, width)], self.own_sem.at[n, 1]).start()

    def first(self, n, whole, pack):
        slot = self.slot(whole)
        pltpu.make_async_copy(slot, slot, self.own_sem.at[n, 0]).wait()
        if pack is not None:
            pltpu.make_async_copy(pack, pack, self.own_sem.at[n, 1]).wait()
        for step in (1, 2, 3):
            source = slot if pack is None or step == 2 else pack
            self.copy(n, 0, source, slot, self.here.along_z(step)).start()

    def second(self, n, whole):
        here = self.here
        self.wait(n, 0, whole.at[pl.ds(0, 3), here.c, self.own[0], self.own[1]], here.along_z(1))
        block = self.block(whole, here.c, self.own)
        self.copy(n, 1, block, block, here.near()).start()
        self.copy(n, 2, block, block, here.far()).start()
        self.copy(n, 3, block, block, here.peer()).start()

    def third(self, n, whole):
        here = self.here
        block = self.block(whole, here.c, self.near)
        self.wait(n, 1, block, here.near())
        self.copy(n, 2, block, block, here.far()).start()
        self.copy(n, 3, block, block, here.peer()).start()

    def fourth(self, n, whole):
        here = self.here
        self.wait(n, 2, whole.at[:, here.c, 0], here.far())
        for column in (self.far, self.both):
            block = self.block(whole, here.c, column)
            self.copy(n, 3, block, block, here.peer()).start()

    def fifth(self, n, whole):
        self.wait(n, 3, whole.at[:, 1 - self.here.c], self.here.peer())


class Scatter:
    def __init__(self, here, send, recv):
        self.here, self.send, self.recv = here, send, recv
        self.own, self.near = here.column(False, False), here.column(True, False)
        self.far, self.both = here.column(False, True), here.column(True, True)

    def copy(self, n, number, source, target, device):
        return remote(source, target, self.send.at[n, number], self.recv.at[n, number], device)

    def view(self, source, column):
        if len(source.shape) == 5:
            return source.at[:, column[0], column[1]]
        return source.at[:, 2 * column[0] + column[1]]

    def to_far(self, n, source, twos):
        return [
            self.copy(n, i, self.view(source, column), twos.at[i], self.here.far())
            for i, column in enumerate((self.both, self.far))
        ]

    def to_near(self, n, source, twos):
        return self.copy(n, 2, self.view(source, self.near), twos.at[2], self.here.near())

    def first(self, n, source, twos):
        for copy in self.to_far(n, source, twos):
            copy.start()

    def add(self, target, other):
        @pl.loop(0, 4)
        def _(level):
            target[level] = low(wide(target[level]) + wide(other[level]))

    def second(self, n, source, twos):
        both, far = self.to_far(n, source, twos)
        both.wait()
        self.add(self.view(source, self.near), twos.at[0])
        self.to_near(n, source, twos).start()
        far.wait()
        self.add(self.view(source, self.own), twos.at[1])

    def third(self, n, source, twos, ends):
        self.to_near(n, source, twos).wait()
        own = self.view(source, self.own)
        self.add(own, twos.at[2])
        for step in (1, 2, 3):
            block = own.at[(self.here.z + step) % 4]
            self.copy(n, 3, block, ends.at[step - 1], self.here.along_z(step)).start()

    def fourth(self, n, source, ends):
        self.copy(n, 3, ends, ends, self.here.along_z(1)).wait()
        own = self.view(source, self.own)
        return wide(own[self.here.z]), [wide(ends[i]) for i in range(3)]


def layer_kernel(
    x_in, og_in, lengths_ref, gains_in, wq_in, wk_in, wv_in, wo_in, wg_in, wu_in, wd_in,
    out_ref, gi_ref, oq_ref, ok_ref, ov_ref, oo_ref, og_out, ou_out, od_out, on_ref,
    wn, wa, wo, wm, pack_a, pack_m, xm, og8, nt8, no8, at8, atb, og_peer, nt_peer, no_peer, at_peer,
    og_t, nt_t, q_ref, k_ref, v_ref, p_ref, mid, acc, gn, gain, tri, tri_peer,
    swap, swap_in, gat, edge, edge_in, outs, outs_peer, gb, gb_peer, mga,
    nb_peer, nb_sum, mlp_twos, mlp_ends, mga_twos, mga_ends, mgo_twos, mgo_ends, nb_twos, nb_ends,
    own_sem, g_send, g_recv, s_send, s_recv, halo_send, halo_recv, edge_send, edge_recv,
    side_send, side_recv, tri_send, tri_recv, swap_send, swap_recv, out_send, out_recv, host_sem,
):
    nb, ga_send, no_t = wn, swap.at[0, :, 0:HALF], nt_t
    here = Place()
    z, c, k, h = here.z, here.c, here.k, here.h
    tiles = wm.shape[0]
    span = tiles * PART
    scale = 1.0 / math.sqrt(HEAD_DIM)
    tokens = x_in.shape[0]
    piece = tokens // 2
    rows = wn.shape[4]
    gather = Gather(here, own_sem, g_send, g_recv)
    scatter = Scatter(here, s_send, s_recv)
    early = 6
    total = early + tiles

    def whole_of(n):
        if n == 0:
            return wn
        return wa.at[n - 1] if n < 4 else wo.at[n - 4]

    def pack_of(n):
        return pack_a.at[n - 1] if 1 <= n < 4 else None

    def parts_of(n):
        if n == 0:
            return [(gains_in, None, 0, LANES)]
        if n < 4:
            source = (wk_in, wv_in, wq_in)[n - 1]
            return [(source.at[:, lanes_at(h * HALF, HALF)], source.at[:, lanes_at((1 - h) * HALF, HALF)], 0, HALF)]
        return [(wo_in.at[:, pl.ds((n - 4) * HALF, HALF)], None, 0, HALF)]

    def mlp_parts(f):
        return [
            (
                w.at[:, lanes_at(h * span + f * PART, PART)],
                w.at[:, lanes_at((1 - h) * span + f * PART, PART)],
                i * PART, PART,
            )
            for i, w in enumerate((wg_in, wu_in, wd_in))
        ]

    def step(stage, n):
        late = n >= early
        whole = wm.at[n - early] if late else whole_of(n)
        if stage == 0:
            gather.first(n, whole, pack_m.at[n - early] if late else pack_of(n))
        else:
            (gather.second, gather.third, gather.fourth, gather.fifth)[stage - 1](n, whole)

    def steps(stage, *chunks_of):
        for n in chunks_of:
            step(stage, n)

    def tile_steps(f):
        for stage, ahead in enumerate(AHEAD):
            tile = f + ahead

            @pl.when(tile < tiles)
            def _(stage=stage, tile=tile):
                if stage == 0:
                    gather.first(early + tile, wm.at[tile], pack_m.at[tile])
                else:
                    (gather.second, gather.third, gather.fourth)[stage - 1](early + tile, wm.at[tile])

    def halo(which, kind):
        ref = (k_ref, v_ref)[which]
        tail, head = pl.ds((PAD + piece - WINDOW) // rows, WINDOW // rows), pl.ds((PAD - WINDOW) // rows, WINDOW // rows)
        if kind == 0:
            source, target, device = ref.at[:, tail], ref.at[:, head], here.peer()
        elif kind == 1:
            source, target, device = ref.at[pl.ds(0, 2), tail], ref.at[pl.ds(2, 2), head], here.peer()
        else:
            source, target, device = ref.at[pl.ds(2, 2), tail], ref.at[pl.ds(0, 2), head], here.cross()
        return remote(source, target, halo_send.at[which, kind // 2], halo_recv.at[which, kind // 2], device)

    def edge_copy(kind):
        if kind == 0:
            source, target, device = edge, edge_in, here.peer()
        elif kind == 1:
            source, target, device = edge.at[:, 1], edge_in.at[:, 0], here.peer()
        else:
            source, target, device = edge.at[:, 0], edge_in.at[:, 1], here.cross()
        return remote(source, target, edge_send.at[kind // 2], edge_recv.at[kind // 2], device)

    def x_copy():
        return remote(x_in, xm, swap_send.at[0], swap_recv.at[0], here.mate())

    def og_copy(slot):
        view = og8.at[:, :, slot]
        return remote(view, view, swap_send.at[1], swap_recv.at[1], here.mate())

    def nt_copy(slot):
        view = nt8.at[:, :, slot]
        return remote(view, view, swap_send.at[2], swap_recv.at[2], here.mate())

    def at_copy():
        return remote(atb.at[1 - h], at8.at[pl.ds(2 * h, 2)], swap_send.at[3], swap_recv.at[3], here.mate())

    def ga_copy():
        return remote(ga_send, gat.at[h], swap_send.at[4], swap_recv.at[4], here.mate())

    def swap_copy(number):
        return remote(
            swap.at[number % 2], swap_in.at[number], swap_send.at[5 + number], swap_recv.at[5 + number], here.mate()
        )

    def out_store():
        return pltpu.make_async_copy(swap.at[1], out_ref, host_sem.at[8])

    def x_again(i):
        return pltpu.make_async_copy(x_in.at[:, pl.ds(i * HALF, HALF)], gat.at[i], host_sem.at[9 + i])

    def side_copy(number, source, target):
        return remote(source, target, side_send.at[number], side_recv.at[number], here.peer())

    def og_side(number, slot):
        return side_copy(number, og8.at[:, 1 - c, slot], og_peer.at[:, slot])

    def nt_side(number, slot):
        return side_copy(number, nt8.at[:, 1 - c, slot], nt_peer.at[:, slot])

    def no_side():
        return side_copy(4, no8.at[:, 1 - c], no_peer)

    def at_side():
        return side_copy(5, at8.at[:, 1 - c], at_peer)

    def gb_side():
        return side_copy(6, gb, gb_peer)

    def pair_side():
        return side_copy(7, nb.at[:, 1 - c], nb_peer)

    def out_copy(m):
        return remote(outs.at[m], outs_peer.at[m], out_send.at[m], out_recv.at[m], here.peer())

    def tri_copy(f, slot):
        return remote(
            tri.at[f, :, slot], tri_peer.at[f, :, slot], tri_send.at[f], tri_recv.at[f], here.peer()
        )

    def spread(value, target, slot):
        for i in range(8):
            target[i // 2, i % 2, slot] = value[:, i * PART : (i + 1) * PART]

    def joined(source, slot):
        return jnp.concatenate([source[i // 2, i % 2, slot] for i in range(8)], axis=1)

    def turned(own_part, peer_part, target):
        for level in range(4):
            rows = slice(level * PART, (level + 1) * PART)
            left, right = own_part(level), peer_part(level)
            target[rows, 0 : left.shape[0]] = low(wide(left).T)
            target[rows, left.shape[0] : 2 * left.shape[0]] = low(wide(right).T)

    og_fetches = [
        pltpu.make_async_copy(og_in.at[:, pl.ds(i * PART, PART)], og8.at[i // 2, i % 2, h], host_sem.at[i])
        for i in range(8)
    ]
    x_fetches = [
        pltpu.make_async_copy(x_in.at[:, pl.ds(i * HALF, HALF)], outs.at[0, i], host_sem.at[9 + i]) for i in range(2)
    ]
    for n in range(early):
        gather.begin(n, parts_of(n), whole_of(n), pack_of(n))
    for copy in og_fetches + x_fetches:
        copy.start()

    @pl.loop(0, tiles)
    def _(f):
        gather.begin(early + f, mlp_parts(f), wm.at[f], pack_m.at[f])

    skipped, begun = (PAD - WINDOW) // rows, PAD // rows
    nothing = jnp.zeros((4, skipped, rows, HALF), jnp.bfloat16)
    for ref in (k_ref, v_ref):
        ref[:, 0:skipped] = nothing

    @pl.when((c == 0) & (k == 0))
    def _():
        for ref in (k_ref, v_ref):
            ref[0:2, skipped:begun] = nothing[0:2]

    @pl.when((c == 1) & (k == 1))
    def _():
        edge_in[:, 1] = jnp.zeros((2, 2, WINDOW, HALF), jnp.bfloat16)

    greet(here.partners())

    steps(0, 0, 1, 2, 3)
    x_copy().start()
    steps(0, 4, 5, 6, 7)
    steps(1, 0, 1, 2, 3)
    steps(2, 0, 1, 2, 3)
    steps(1, 4, 5)
    steps(3, 0, 1, 2, 3)
    for copy in og_fetches:
        copy.wait()
    og_side(0, h).start()
    steps(4, 0)

    gain_rows = wide(flat(wn[...])).T
    gain[0:8, :] = jnp.broadcast_to(gain_rows[0:1, :], (8, gain_rows.shape[1]))
    gain[8:16, :] = jnp.broadcast_to(gain_rows[64:65, :], (8, gain_rows.shape[1]))

    def normed_of(value, row):
        factor = lax.rsqrt(jnp.mean(value * value, axis=-1, keepdims=True) + 1e-05)
        return low(value * factor * gain[row : row + 1, :])

    for copy in x_fetches:
        copy.wait()
    spread(normed_of(wide(jnp.concatenate([outs[0, 0], outs[0, 1]], axis=1)), 0), no8, h)
    x_copy().wait()
    spread(normed_of(wide(xm[...]), 0), no8, 1 - h)
    no_side().start()

    def projected(n, slot):
        return low(mm(joined(no8, slot), flat(wa[n])))

    steps(1, 6)
    for n, ref in ((0, k_ref), (1, v_ref)):
        steps(4, 1 + n)
        for slot in range(2):
            ref[2 * slot : 2 * slot + 2, begun:] = projected(n, slot).reshape(2, piece // rows, rows, HALF)

        @pl.when(c == 0)
        def _(n=n):
            halo(n, 0).start()

        @pl.when(c == 1)
        def _(n=n):
            halo(n, 1).start()

        @pl.when((c == 1) & (k == 0))
        def _(n=n):
            halo(n, 2).start()

        if n == 0:
            steps(2, 4, 5)
        else:
            steps(0, *range(8, total))
            steps(1, 7)

    steps(4, 3)
    for slot in range(2):
        q_ref[slot] = projected(2, slot)
    steps(3, 4, 5)
    steps(2, 6)

    for n in range(2):

        @pl.when(c == 0)
        def _(n=n):
            halo(n, 0).wait_send()
            halo(n, 1).wait_recv()

        @pl.when(c == 1)
        def _(n=n):
            halo(n, 0).wait_recv()
            halo(n, 1).wait_send()

        @pl.when((c == 1) & (k == 0))
        def _(n=n):
            halo(n, 2).wait_send()

        @pl.when((c == 0) & (k == 1))
        def _(n=n):
            halo(n, 2).wait_recv()

    def mask_of(slot, row):
        first = (4 * k + 2 * slot + c) * piece
        query_pos = first + lax.broadcasted_iota(jnp.int32, (piece, PAD + piece), 0)
        key_pos = first - PAD + lax.broadcasted_iota(jnp.int32, (piece, PAD + piece), 1)
        start = jnp.zeros((piece, PAD + piece), jnp.int32)
        reached = 0
        for doc in range(lengths_ref.shape[1]):
            reached = reached + lengths_ref[row, doc]
            start = jnp.maximum(start, jnp.where(query_pos >= reached, reached, 0))
        return (key_pos >= start) & (key_pos <= query_pos) & (query_pos - key_pos < WINDOW)

    def attend(slot, row):
        allowed = mask_of(slot, row)
        span_rows = slice(row * piece, (row + 1) * piece)
        for head in range(HEADS // 2):
            cols = slice(head * HEAD_DIM, (head + 1) * HEAD_DIM)
            scores = nt_dot(q_ref[slot, span_rows, cols], flat(k_ref[2 * slot + row, :, :, cols])) * scale
            scores = jnp.where(allowed, scores, -1e30)
            exps = jnp.exp(scores - jnp.max(scores, axis=-1, keepdims=True))
            probs = exps / jnp.sum(exps, axis=-1, keepdims=True)
            p_ref[slot, row, head] = probs
            atb[slot, head // 2, head % 2, span_rows, :] = low(mm(low(probs), flat(v_ref[2 * slot + row, :, :, cols])))

    attend(1 - h, 0)
    attend(1 - h, 1)
    at_copy().start()
    og_copy(h).start()
    steps(1, 8)
    steps(2, 7)
    steps(3, 6)
    attend(h, 0)
    attend(h, 1)
    at8[pl.ds(2 * h, 2)] = atb[h]
    steps(4, 4, 5)
    at_copy().wait()
    at_side().start()
    attended = jnp.concatenate([at8[i // 2, i % 2] for i in range(8)], axis=1)
    for n in range(2):
        cols = slice(n * HALF, (n + 1) * HALF)
        mid[:, cols] = wide(outs[0, n]) + mm(attended, flat(wo[n]))
    middle = mid[...]
    spread(normed_of(middle, 8), nt8, h)
    nt_copy(h).start()
    nt_side(2, h).start()
    acc[h] = middle
    acc[1 - h] = jnp.zeros(middle.shape, jnp.float32)
    gn[...] = jnp.zeros(gn.shape, jnp.float32)

    def feed(f, slot):
        w_pair = flat(wm[f, :, :, :, :, :, 0 : 2 * PART])
        w_down = flat(wm[f, :, :, :, :, :, 2 * PART : 3 * PART])
        both = mm(joined(nt8, slot), w_pair)
        gates, ups = both[:, 0:PART], both[:, PART:]
        grad_hidden = mm(joined(og8, slot), w_down)
        sigmoid = 1.0 / (1.0 + jnp.exp(-gates))
        silu = gates * sigmoid
        hidden = low(silu * ups)
        grad_gates = low(grad_hidden * ups * sigmoid * (1.0 + gates * (1.0 - sigmoid)))
        grad_ups = low(grad_hidden * silu)
        tri[f, 0, slot] = grad_gates
        tri[f, 1, slot] = grad_ups
        tri[f, 2, slot] = hidden
        tri_copy(f, slot).start()
        acc[slot] += nt_dot(hidden, w_down)
        gn[slot] += nt_dot(jnp.concatenate([grad_gates, grad_ups], axis=1), w_pair)

    n_tokens = 2 * tokens

    def ff_grads(f):
        remote(tri.at[f], tri_peer.at[f], tri_send.at[f], tri_recv.at[f], here.peer()).wait()
        pair = mm(nt_t[:, 0:n_tokens], jnp.concatenate([flat(tri[f, 0]), flat(tri[f, 1])], axis=1)) + mm(
            nt_t[:, n_tokens:], jnp.concatenate([flat(tri_peer[f, 0]), flat(tri_peer[f, 1])], axis=1)
        )
        down = mm(og_t[:, 0:n_tokens], flat(tri[f, 2])) + mm(og_t[:, n_tokens:], flat(tri_peer[f, 2]))
        wm[f, :, 0, :, :, :, 0 : 2 * PART] = low(pair).reshape(4, 2, 2, -1, 2 * PART)
        wm[f, :, 0, :, :, :, 2 * PART : 3 * PART] = low(down).reshape(4, 2, 2, -1, PART)

    chunks = tiles + 6

    def chunk(n):
        if n < tiles:
            return wm.at[n, :, 0], mlp_twos.at[n], mlp_ends.at[n]
        n -= tiles
        if n < 2:
            return k_ref.at[:, pl.ds(4 * n, 4)], mgo_twos.at[n], mgo_ends.at[n]
        if n < 5:
            source = mga if n == 2 else v_ref.at[:, pl.ds(4 * (n - 3), 4)]
            return source, mga_twos.at[n - 2], mga_ends.at[n - 2]
        return nb_sum, nb_twos, nb_ends

    def store_tile(n, mine, others):
        back, across, on = others
        for half, value in ((h, mine + across), (1 - h, back + on)):
            for i, ref in enumerate((og_out, ou_out, od_out)):
                ref[:, lanes_at(half * span + n * PART, PART)] = value[:, i * PART : (i + 1) * PART]

    def store(n, mine, others):
        if n < tiles:
            store_tile(n, mine, others)
            return
        back, across, on = others
        n -= tiles
        if 2 <= n < 5:
            for half, value in ((h, mine + across), (1 - h, back + on)):
                (oq_ref, ok_ref, ov_ref)[n - 2][:, lanes_at(half * HALF, HALF)] = value
            return
        value = mine + back + across + on
        if n < 2:
            oo_ref[:, n * HALF : (n + 1) * HALF] = value
        else:
            on_ref[...] = value

    def sum_tick(t):
        for stage, lag in enumerate(SUM_LAGS):
            n = t - lag
            if not 0 <= n < chunks:
                continue
            source, twos, ends = chunk(n)
            if stage == 0:
                scatter.second(n, source, twos)
            elif stage == 1:
                scatter.third(n, source, twos, ends)
            else:
                store(n, *scatter.fourth(n, source, ends))

    def launch_tile(f):
        scatter.first(f, wm.at[f, :, 0], mlp_twos.at[f])

    def launch(n):
        source, twos, _ = chunk(n)
        scatter.first(n, source, twos)

    @pl.loop(0, FIRST_TILES)
    def _(f):
        tile_steps(f)
        gather.fifth(early + f, wm.at[f])
        feed(f, h)

    og_copy(1 - h).wait()
    og_side(1, 1 - h).start()
    nt_copy(1 - h).wait()
    nt_side(3, 1 - h).start()

    @pl.loop(0, FIRST_TILES)
    def _(f):
        @pl.when(FIRST_TILES + f < tiles)
        def _():
            tile_steps(FIRST_TILES + f)

        feed(f, 1 - h)

    @pl.loop(FIRST_TILES, tiles)
    def _(f):
        gather.fifth(early + f, wm.at[f])
        feed(f, h)
        feed(f, 1 - h)

    swap[0] = low(gn[1 - h])
    swap_copy(0).start()
    for number, slot in ((0, h), (1, 1 - h)):
        og_side(number, slot).wait()
    turned(lambda i: flat(og8[i, c]), lambda i: flat(og_peer[i]), og_t)
    for number, slot in ((2, h), (3, 1 - h)):
        nt_side(number, slot).wait()
    turned(lambda i: flat(nt8[i, c]), lambda i: flat(nt_peer[i]), nt_t)

    @pl.loop(0, tiles)
    def _(f):
        ff_grads(f)
        launch_tile(f)


    def close_middle():
        swap_copy(0).wait()
        middle = mid[...]
        factor = lax.rsqrt(jnp.mean(middle * middle, axis=-1, keepdims=True) + 1e-05)
        grad_normed = gn[h] + wide(swap_in[0])
        through = grad_normed * gain[8:9, :]
        shift = jnp.mean(through * middle, axis=-1, keepdims=True) * factor * factor * factor
        grad_middle = wide(joined(og8, h)) + factor * through - middle * shift
        gi_ref[...] = grad_middle
        gb[...] = low(grad_middle)
        gb_side().start()
        gain[8:16, :] = jnp.broadcast_to(
            jnp.sum(grad_normed * middle * factor, axis=0, keepdims=True), (8, middle.shape[1])
        )

    def to_attended():
        def part(half):
            rows = pl.ds(2 * half, 2)
            return low(nt_dot(gb[:, 0:HALF], flat(wo[0, rows])) + nt_dot(gb[:, HALF:], flat(wo[1, rows])))

        swap[0, :, 0:HALF] = part(1 - h)
        ga_copy().start()
        swap[1] = low(acc[1 - h])
        swap_copy(1).start()
        gat[h] = part(h)

    def keep_out():
        mid[...] = acc[h]

    def close_out():
        swap_copy(1).wait()
        swap[1] = low(mid[...] + wide(swap_in[1]))
        out_store().start()

    def attend_back(slot):
        for row in range(2):
            span_rows = slice(row * piece, (row + 1) * piece)
            for head in range(HEADS // 2):
                cols = slice(head * HEAD_DIM, (head + 1) * HEAD_DIM)
                there = slice(row * HALF + head * HEAD_DIM, row * HALF + (head + 1) * HEAD_DIM)
                grad = gat[slot, span_rows, cols]
                probs = p_ref[slot, row, head]
                gn[slot, :, there] = tn_dot(low(probs), grad)
                grad_probs = nt_dot(grad, flat(v_ref[2 * slot + row, :, :, cols]))
                inner = jnp.sum(grad_probs * probs, axis=-1, keepdims=True)
                grad_scores = low(probs * (grad_probs - inner))
                outs[2, slot, span_rows, cols] = low(mm(grad_scores, flat(k_ref[2 * slot + row, :, :, cols])) * scale)
                acc[slot, :, there] = tn_dot(grad_scores, q_ref[slot, span_rows, cols]) * scale
            there = slice(row * HALF, (row + 1) * HALF)
            edge[0, slot, row] = low(acc[slot, PAD - WINDOW : PAD, there])
            edge[1, slot, row] = low(gn[slot, PAD - WINDOW : PAD, there])

    def send_edge():
        out_copy(2).start()

        @pl.when(c == 1)
        def _():
            edge_copy(0).start()

        @pl.when(c == 0)
        def _():
            edge_copy(1).start()

        @pl.when((c == 0) & (k == 1))
        def _():
            edge_copy(2).start()

    def close_edge():
        @pl.when(c == 1)
        def _():
            edge_copy(0).wait_send()
            edge_copy(1).wait_recv()

        @pl.when(c == 0)
        def _():
            edge_copy(0).wait_recv()
            edge_copy(1).wait_send()

        @pl.when((c == 0) & (k == 1))
        def _():
            edge_copy(2).wait_send()

        @pl.when((c == 1) & (k == 0))
        def _():
            edge_copy(2).wait_recv()

        inside = piece - WINDOW
        for m, source in ((0, acc), (1, gn)):
            for slot in range(2):
                for row in range(2):
                    there = slice(row * HALF, (row + 1) * HALF)
                    first = row * piece
                    outs[m, slot, first : first + inside, :] = low(source[slot, PAD : PAD + inside, there])
                    outs[m, slot, first + inside : first + piece, :] = low(
                        source[slot, PAD + inside : PAD + piece, there] + wide(edge_in[m, slot, row])
                    )
            out_copy(m).start()

    def to_input(slot):
        grad = nt_dot(outs[0, slot], flat(wa[0]))
        for m in (1, 2):
            grad = grad + nt_dot(outs[m, slot], flat(wa[m]))
        return grad

    def inverse_rms(value):
        return lax.rsqrt(jnp.mean(value * value, axis=-1, keepdims=True) + 1e-05)

    def send_input():
        x = wide(xm[...])
        part = to_input(1 - h)
        swap[0] = low(part)
        swap_copy(2).start()
        one = jnp.sum(part * x * inverse_rms(x), axis=0, keepdims=True)
        part = to_input(h)
        acc[0] = part
        for i in range(2):
            x_again(i).wait()
        x = wide(jnp.concatenate([gat[0], gat[1]], axis=1))
        one = one + jnp.sum(part * x * inverse_rms(x), axis=0, keepdims=True)
        width = one.shape[1]
        stacked = jnp.concatenate(
            [
                jnp.broadcast_to(one, (LANES // 2, width)),
                jnp.broadcast_to(gain[8:9, :], (LANES // 2, width)),
            ],
            axis=0,
        )
        nb[...] = low(stacked.T).reshape(nb.shape)
        pair_side().start()

    def close_input():
        swap_copy(2).wait()
        grad_normed = acc[0] + wide(swap_in[2])
        x = wide(jnp.concatenate([gat[0], gat[1]], axis=1))
        factor = inverse_rms(x)
        through = grad_normed * gain[0:1, :]
        shift = jnp.mean(through * x, axis=-1, keepdims=True) * factor * factor * factor
        gi_ref[...] += factor * through - x * shift

    def close_norm():
        pair_side().wait()
        nb_sum[...] = low(wide(nb[:, c]) + wide(nb_peer[...]))

    def turn_normed():
        no_side().wait()
        turned(lambda i: flat(no8[i, c]), lambda i: flat(no_peer[i]), no_t)

    def wout_grads():
        at_side().wait()
        turned(lambda i: at8[i, c], lambda i: at_peer[i], og_t)
        gb_side().wait()
        for n in range(2):
            cols = slice(n * HALF, (n + 1) * HALF)
            grad = mm(og_t[:, 0:tokens], gb[:, cols]) + mm(og_t[:, tokens : 2 * tokens], gb_peer[:, cols])
            k_ref[:, 4 * n : 4 * n + 4] = low(grad).reshape(4, 4, -1, HALF)

    def attn_grads(m):
        out_copy(m).wait()
        grad = mm(no_t[:, 0:n_tokens], flat(outs[m])) + mm(no_t[:, n_tokens:], flat(outs_peer[m]))
        if m == 2:
            mga[...] = low(grad).reshape(mga.shape)
        else:
            v_ref[:, 4 * m : 4 * m + 4] = low(grad).reshape(4, 4, -1, HALF)

    def ticks(first, last):
        for t in range(first, last):
            sum_tick(t)

    ticks(0, 1)
    close_middle()
    to_attended()
    keep_out()
    ticks(1, 3)
    attend_back(h)
    ga_copy().wait()
    ticks(3, 4)
    attend_back(1 - h)
    send_edge()
    for i in range(2):
        x_again(i).start()
    ticks(4, 6)
    turn_normed()
    attn_grads(2)
    wout_grads()
    launch(tiles)
    launch(tiles + 1)
    launch(tiles + 2)
    ticks(6, 8)
    close_edge()
    send_input()
    for m in range(2):
        attn_grads(m)
        launch(tiles + 3 + m)
    close_norm()
    launch(tiles + 5)
    ticks(8, tiles + 1)
    close_out()
    ticks(tiles + 1, tiles + 2)
    close_input()
    ticks(tiles + 2, chunks + SUM_LAGS[-1])
    out_store().wait()


def deliver_kernel(count, *refs):
    sources, targets, held = (refs[i * count : (i + 1) * count] for i in range(3))
    in_sem, out_sem = refs[3 * count :]
    ins = [pltpu.make_async_copy(s, v, in_sem.at[i]) for i, (s, v) in enumerate(zip(sources, held))]
    outs = [pltpu.make_async_copy(v, t, out_sem.at[i]) for i, (v, t) in enumerate(zip(held, targets))]
    for copy in ins:
        copy.start()
    for arrived, leaving in zip(ins, outs):
        arrived.wait()
        leaving.start()
    for copy in outs:
        copy.wait()


def delivered(arrays):
    anywhere = pl.BlockSpec(memory_space=pl.ANY)
    count = len(arrays)
    return pl.pallas_call(
        functools.partial(deliver_kernel, count),
        out_shape=[jax.ShapeDtypeStruct(a.shape, a.dtype) for a in arrays],
        in_specs=[anywhere] * count,
        out_specs=[anywhere] * count,
        scratch_shapes=[pltpu.VMEM(a.shape, a.dtype) for a in arrays]
        + [pltpu.SemaphoreType.DMA((count,)), pltpu.SemaphoreType.DMA((count,))],
        compiler_params=pltpu.CompilerParams(vmem_limit_bytes=60 * 2**20),
        name="deliver",
    )(*arrays)


def fused(hidden_in, lengths, out_grad, gain_shards, weight_shards):
    hidden = hidden_in.reshape(-1, hidden_in.shape[-1])
    tokens, width = hidden.shape
    gains = jnp.concatenate(
        [jnp.broadcast_to(g[:, None], (g.shape[0], LANES // 2)) for g in gain_shards], axis=1
    )
    rows = gains.shape[0]
    tiles = weight_shards[4].shape[1] // (2 * PART)
    bf, fl = jnp.bfloat16, jnp.float32
    every, mine = (4, 2, 2, 2, rows), (4, 2, 2, rows)
    part = 3 * PART
    dma = pltpu.SemaphoreType.DMA
    vmem, anywhere = pl.BlockSpec(memory_space=pltpu.VMEM), pl.BlockSpec(memory_space=pl.ANY)
    shape = jax.ShapeDtypeStruct
    piece = tokens // 2
    keys = (4, (PAD + piece) // rows, rows, HALF)
    scratch = [
        ((*every, LANES), bf), ((3, *every, HALF), bf), ((2, *every, HALF), bf), ((tiles, *every, part), bf),
        ((3, rows, HALF), bf), ((tiles, rows, part), bf), ((tokens, width), bf),
        *[((4, 2, 2, tokens, PART), bf)] * 3, ((4, 2, tokens, PART), bf), ((2, 2, 2, tokens, PART), bf),
        *[((4, 2, tokens, PART), bf)] * 3, ((4, tokens, PART), bf),
        *[((width // 2, 4 * tokens), bf)] * 2,
        ((2, tokens, HALF), bf), (keys, bf), (keys, bf), ((2, 2, HEADS // 2, piece, PAD + piece), fl),
        ((tokens, width), fl), ((2, tokens, width), fl), ((2, tokens, width), fl),
        ((16, width), fl), ((tiles, 3, 2, tokens, PART), bf), ((tiles, 3, 2, tokens, PART), bf),
        ((2, tokens, width), bf), ((3, tokens, width), bf), ((2, tokens, HALF), bf),
        ((2, 2, 2, WINDOW, HALF), bf), ((2, 2, 2, WINDOW, HALF), bf),
        ((3, 2, tokens, HALF), bf), ((3, 2, tokens, HALF), bf), ((tokens, width), bf), ((tokens, width), bf),
        ((*mine, HALF), bf),
        ((*mine, LANES), bf), ((*mine, LANES), bf),
        ((tiles, 3, 4, rows, part), bf), ((tiles, 3, rows, part), bf),
        ((3, 3, 4, rows, HALF), bf), ((3, 3, rows, HALF), bf),
        ((2, 3, 4, rows, HALF), bf), ((2, 3, rows, HALF), bf),
        ((3, 4, rows, LANES), bf), ((3, rows, LANES), bf),
    ]
    count, chunks = 6 + tiles, 6 + tiles
    results = pl.pallas_call(
        layer_kernel,
        out_shape=[shape((tokens, width), bf), shape((tokens, width), fl)]
        + [shape((rows, width), fl)] * 4 + [shape((rows, 2 * tiles * PART), fl)] * 3
        + [shape((rows, LANES), fl)],
        in_specs=[anywhere, anywhere, pl.BlockSpec(memory_space=pltpu.SMEM)] + [anywhere] * 8,
        out_specs=[anywhere] + [vmem] * 9,
        scratch_shapes=[pltpu.VMEM(*s) for s in scratch]
        + [
            dma((count, 2)), dma((count, 4)), dma((count, 4)), dma((chunks, 4)), dma((chunks, 4)),
            dma((2, 2)), dma((2, 2)), dma((2,)), dma((2,)), dma((8,)), dma((8,)),
            dma((tiles,)), dma((tiles,)), dma((8,)), dma((8,)), dma((3,)), dma((3,)), dma((12,)),
        ],
        compiler_params=pltpu.CompilerParams(
            collective_id=0, has_side_effects=True, vmem_limit_bytes=63 * 2**20
        ),
        name="layer",
    )(hidden, out_grad.reshape(hidden.shape), lengths, gains, *weight_shards)
    block_out, grad_in, query, key, value, wout, gate, up, down, norms = delivered(results)
    return (
        block_out.reshape(hidden_in.shape), grad_in.reshape(hidden_in.shape),
        norms[:, 0], query, key, value, wout, norms[:, LANES // 2], gate, up, down,
    )


def layer(hidden_in, lengths, out_grad, gains, weights):
    score_scale = 1.0 / math.sqrt(HEAD_DIM)
    tokens = hidden_in.shape[1]
    gain_one, gain_two = gains
    w_query, w_key, w_value, w_out, w_gate, w_up, w_down = weights
    inputs = hidden_in.astype(jnp.float32)
    normed_one = rms_scale(inputs, gain_one).astype(jnp.bfloat16)
    queries = project(normed_one, w_query).astype(jnp.bfloat16)
    keys = project(normed_one, w_key).astype(jnp.bfloat16)
    values = project(normed_one, w_value).astype(jnp.bfloat16)
    tails = jnp.stack([keys[:, tokens - WINDOW :], values[:, tokens - WINDOW :]])
    received = passed_along(tails, "seq", 1)
    keys_all = jnp.concatenate([received[0], keys], axis=1)
    values_all = jnp.concatenate([received[1], values], axis=1)
    allowed = window_mask(lengths, lax.axis_index("seq"), tokens)
    scores = scores_of(queries, keys_all, allowed)
    top = jnp.max(scores, axis=-1, keepdims=True)
    exps = jnp.exp(scores - top)
    probs = exps / jnp.sum(exps, axis=-1, keepdims=True)
    probs_low = probs.astype(jnp.bfloat16)
    mixed = jnp.einsum(
        "rhqk,rkhd->rqhd", probs_low, split_heads(values_all), preferred_element_type=jnp.float32
    )
    attended = merge_heads(mixed).astype(jnp.bfloat16)
    middle = inputs + project(attended, w_out)
    normed_two = rms_scale(middle, gain_two).astype(jnp.bfloat16)
    gates = project(normed_two, w_gate)
    ups = project(normed_two, w_up)
    hidden_act = swiglu(gates, ups).astype(jnp.bfloat16)
    block_out = (middle + project_back(hidden_act, w_down)).astype(jnp.bfloat16)
    grad_hidden = project(out_grad, w_down)
    unused, swiglu_back = jax.vjp(swiglu, gates, ups)
    grad_gates, grad_ups = swiglu_back(grad_hidden)
    grad_gates = grad_gates.astype(jnp.bfloat16)
    grad_ups = grad_ups.astype(jnp.bfloat16)
    grad_down = weight_grad(out_grad, hidden_act)
    grad_gate = weight_grad(normed_two, grad_gates)
    grad_up = weight_grad(normed_two, grad_ups)
    grad_normed_two = project_back(grad_gates, w_gate) + project_back(grad_ups, w_up)
    unused, norm_two_back = jax.vjp(rms_scale, middle, gain_two)
    grad_middle_part, grad_norm2 = norm_two_back(grad_normed_two)
    grad_middle = out_grad.astype(jnp.float32) + grad_middle_part
    grad_branch = grad_middle.astype(jnp.bfloat16)
    grad_wout = weight_grad(attended, grad_branch)
    grad_attended = project_back(grad_branch, w_out).astype(jnp.bfloat16)
    grad_heads = split_heads(grad_attended)
    grad_values_all = jnp.einsum(
        "rhqk,rqhd->rkhd", probs_low, grad_heads, preferred_element_type=jnp.float32
    )
    grad_probs = jnp.einsum(
        "rqhd,rkhd->rhqk", grad_heads, split_heads(values_all), preferred_element_type=jnp.float32
    )
    grad_scores = (
        probs * (grad_probs - jnp.sum(grad_probs * probs, axis=-1, keepdims=True))
    ).astype(jnp.bfloat16)
    grad_queries = score_scale * merge_heads(
        jnp.einsum(
            "rhqk,rkhd->rqhd", grad_scores, split_heads(keys_all),
            preferred_element_type=jnp.float32,
        )
    )
    grad_keys_all = score_scale * merge_heads(
        jnp.einsum(
            "rhqk,rqhd->rkhd", grad_scores, split_heads(queries),
            preferred_element_type=jnp.float32,
        )
    )
    grad_values_all = merge_heads(grad_values_all)
    halo_grads = jnp.stack([grad_keys_all[:, :WINDOW], grad_values_all[:, :WINDOW]])
    returned = passed_along(halo_grads.astype(jnp.bfloat16), "seq", -1).astype(halo_grads.dtype)
    grad_keys = (
        grad_keys_all[:, WINDOW:].at[:, tokens - WINDOW :].add(returned[0]).astype(jnp.bfloat16)
    )
    grad_values = (
        grad_values_all[:, WINDOW:].at[:, tokens - WINDOW :].add(returned[1]).astype(jnp.bfloat16)
    )
    grad_queries = grad_queries.astype(jnp.bfloat16)
    grad_query = weight_grad(normed_one, grad_queries)
    grad_key = weight_grad(normed_one, grad_keys)
    grad_value = weight_grad(normed_one, grad_values)
    grad_normed_one = (
        project_back(grad_queries, w_query)
        + project_back(grad_keys, w_key)
        + project_back(grad_values, w_value)
    )
    unused, norm_one_back = jax.vjp(rms_scale, inputs, gain_one)
    grad_inputs_part, grad_norm1 = norm_one_back(grad_normed_one)
    grad_in = grad_middle + grad_inputs_part
    grads = (grad_query, grad_key, grad_value, grad_wout, grad_gate, grad_up, grad_down)
    return block_out, grad_in, (grad_norm1, grad_norm2), grads


def shards(
    hidden_in, lengths, norm1_gain, w_query, w_key, w_value, w_out,
    norm2_gain, w_gate, w_up, w_down, out_grad,
):
    gain_shards = (norm1_gain, norm2_gain)
    weight_shards = (w_query, w_key, w_value, w_out, w_gate, w_up, w_down)
    if (lax.axis_size("seq"), lax.axis_size("rows")) == (SEQ_PIECES, ROW_GROUPS):
        return fused(hidden_in, lengths, out_grad, gain_shards, weight_shards)
    gains = [g.astype(jnp.float32) for g in gathered_by_xla(gain_shards)]
    weights = gathered_by_xla(weight_shards)
    block_out, grad_in, norms, grads = layer(hidden_in, lengths, out_grad, gains, weights)
    norms, grads = scattered_by_xla(norms), scattered_by_xla(grads)
    return (
        block_out, grad_in, norms[0], grads[0], grads[1], grads[2], grads[3],
        norms[1], grads[4], grads[5], grads[6],
    )


def solution(mesh):
    tokens = P("rows", "seq", None)
    vector = P(("seq", "rows"))
    matrix = P(("seq", "rows"), None)
    in_specs = (
        tokens, P("rows", None), vector, matrix, matrix, matrix, matrix,
        vector, matrix, matrix, matrix, tokens,
    )
    out_specs = (
        tokens, tokens, vector, matrix, matrix, matrix, matrix,
        vector, matrix, matrix, matrix,
    )
    return jax.shard_map(shards, mesh=mesh, in_specs=in_specs, out_specs=out_specs, check_vma=False)
```

```python
import functools
import math

import jax
import jax.numpy as jnp
from jax import lax
from jax.experimental import pallas as pl
from jax.experimental.pallas import tpu as pltpu
from jax.sharding import PartitionSpec as P

HEADS = 8
HEAD_DIM = 128
WINDOW = 64
LANES = 128
MESH = pl.DeviceIdType.MESH


def passed_along(block, axis, distance):
    devices = range(lax.axis_size(axis))
    route = [(i - distance, i) for i in devices if i - distance in devices]
    return lax.ppermute(block, axis, route)


def rms_scale(values, gain):
    factor = lax.rsqrt(jnp.mean(values * values, axis=-1, keepdims=True) + 1e-05)
    return values * factor * gain


def swiglu(gates, ups):
    return jax.nn.silu(gates) * ups


def project(left, weight):
    return jnp.dot(left, weight, preferred_element_type=jnp.float32)


def project_back(grad, weight):
    return lax.dot_general(
        grad, weight, (((2,), (1,)), ((), ())), preferred_element_type=jnp.float32
    )


def weight_grad(left, grad):
    return jnp.einsum("rtd,rtf->df", left, grad, preferred_element_type=jnp.float32)


def split_heads(values):
    return values.reshape(values.shape[0], values.shape[1], HEADS, HEAD_DIM)


def merge_heads(values):
    return values.reshape(values.shape[0], values.shape[1], HEADS * HEAD_DIM)


def window_mask(lengths, seq_index, tokens):
    docs = lengths.shape[1]
    upto = jnp.arange(docs)[:, None] >= jnp.arange(docs)[None, :]
    ends = jnp.sum(jnp.where(upto[None], lengths[:, None, :], 0), axis=2)
    query_pos = seq_index * tokens + jnp.arange(tokens, dtype=jnp.int32)
    key_pos = seq_index * tokens - WINDOW + jnp.arange(tokens + WINDOW, dtype=jnp.int32)
    starts = jnp.max(
        jnp.where(
            ends[:, None, :] <= query_pos[None, :, None],
            ends[:, None, :],
            jnp.zeros_like(ends[:, None, :]),
        ),
        axis=2,
    )
    allowed = (
        (key_pos[None, None, :] >= starts[:, :, None])
        & (key_pos[None, None, :] <= query_pos[None, :, None])
        & (query_pos[None, :, None] - key_pos[None, None, :] < WINDOW)
    )
    return allowed[:, None]


def scores_of(queries, keys_all, allowed):
    score_scale = 1.0 / math.sqrt(HEAD_DIM)
    scores = (
        jnp.einsum(
            "rqhd,rkhd->rhqk",
            split_heads(queries),
            split_heads(keys_all),
            preferred_element_type=jnp.float32,
        )
        * score_scale
    )
    return jnp.where(allowed, scores, -1e30)


def gathered_by_xla(shards):
    return [lax.all_gather(s, ("seq", "rows"), axis=0, tiled=True) for s in shards]


def scattered_by_xla(totals):
    return [
        lax.psum_scatter(t.astype(jnp.float32), ("seq", "rows"), scatter_dimension=0, tiled=True)
        for t in totals
    ]


SEQ_PIECES = 8
ROW_GROUPS = 4
PART = 128
HALF = 512
PAD = 128
AHEAD = (11, 6, 4, 2)
FIRST_TILES = 7
SUM_LAGS = (0, 4, 8)


class Place:
    def __init__(self):
        seq, rows = lax.axis_index("seq"), lax.axis_index("rows")
        self.z, self.c = seq // 2, seq % 2
        self.k, self.h = self.z // 2, self.z % 2
        self.y, self.x = rows // 2, rows % 2
        self.turn_y, self.turn_x = 1 - 2 * self.y, 1 - 2 * self.x

    def column(self, near, far):
        y, x, c = self.y, self.x, self.c
        if near:
            y, x = y + c * self.turn_y, x + (1 - c) * self.turn_x
        if far:
            y, x = y + (1 - c) * self.turn_y, x + c * self.turn_x
        return y, x

    def device(self, z, c, column):
        return (2 * z + c, 2 * column[0] + column[1])

    def near(self):
        return self.device(self.z, self.c, self.column(True, False))

    def far(self):
        return self.device(self.z, self.c, self.column(False, True))

    def peer(self):
        return self.device(self.z, 1 - self.c, (self.y, self.x))

    def mate(self):
        return self.device(2 * self.k + 1 - self.h, self.c, (self.y, self.x))

    def across(self):
        return self.device(2 * (1 - self.k) + self.h, self.c, (self.y, self.x))

    def cross(self):
        return self.device(2 * (1 - self.k) + self.h, 1 - self.c, (self.y, self.x))

    def along_z(self, step):
        return self.device((self.z + step) % 4, self.c, (self.y, self.x))

    def partners(self):
        return [self.near(), self.far(), self.peer(), self.cross()] + [self.along_z(i) for i in (1, 2, 3)]


def greet(partners):
    barrier = pltpu.get_barrier_semaphore()
    for partner in partners:
        pl.semaphore_signal(barrier, inc=1, device_id=partner, device_id_type=MESH)
    pl.semaphore_wait(barrier, len(partners))


def remote(source, target, send, recv, device):
    return pltpu.make_async_remote_copy(
        src_ref=source, dst_ref=target, send_sem=send, recv_sem=recv,
        device_id=device, device_id_type=MESH,
    )


def nt_dot(left, right):
    return lax.dot_general(left, right, (((1,), (1,)), ((), ())), preferred_element_type=jnp.float32)


def tn_dot(left, right):
    return lax.dot_general(left, right, (((0,), (0,)), ((), ())), preferred_element_type=jnp.float32)


def mm(left, right):
    return jnp.dot(left, right, preferred_element_type=jnp.float32)


def flat(value):
    return value.reshape(-1, value.shape[-1])


def low(value):
    return value.astype(jnp.bfloat16)


def wide(value):
    return value.astype(jnp.float32)


def lanes_at(first, width):
    return pl.ds(pl.multiple_of(first, PART), width)


class Gather:
    def __init__(self, here, own_sem, send, recv):
        self.here, self.own_sem, self.send, self.recv = here, own_sem, send, recv
        self.own, self.near = here.column(False, False), here.column(True, False)
        self.far, self.both = here.column(False, True), here.column(True, True)

    def slot(self, whole):
        return whole.at[self.here.z, self.here.c, self.own[0], self.own[1]]

    def block(self, whole, core, column):
        return whole.at[:, core, column[0], column[1]]

    def copy(self, n, number, source, target, device):
        return remote(source, target, self.send.at[n, number], self.recv.at[n, number], device)

    def wait(self, n, number, view, device):
        self.copy(n, number, view, view, device).wait()

    def begin(self, n, parts, whole, pack):
        slot = self.slot(whole)
        for kept, given, first, width in parts:
            pltpu.make_async_copy(kept, slot.at[:, pl.ds(first, width)], self.own_sem.at[n, 0]).start()
            if pack is not None:
                pltpu.make_async_copy(given, pack.at[:, pl.ds(first, width)], self.own_sem.at[n, 1]).start()

    def first(self, n, whole, pack, fetched=True):
        slot = self.slot(whole)
        if fetched:
            pltpu.make_async_copy(slot, slot, self.own_sem.at[n, 0]).wait()
        if pack is not None:
            pltpu.make_async_copy(pack, pack, self.own_sem.at[n, 1]).wait()
        for step in (1, 2, 3):
            source = slot if pack is None or step == 2 else pack
            self.copy(n, 0, source, slot, self.here.along_z(step)).start()

    def second(self, n, whole):
        here = self.here
        self.wait(n, 0, whole.at[pl.ds(0, 3), here.c, self.own[0], self.own[1]], here.along_z(1))
        block = self.block(whole, here.c, self.own)
        self.copy(n, 1, block, block, here.near()).start()
        self.copy(n, 2, block, block, here.far()).start()
        self.copy(n, 3, block, block, here.peer()).start()

    def third(self, n, whole):
        here = self.here
        block = self.block(whole, here.c, self.near)
        self.wait(n, 1, block, here.near())
        self.copy(n, 2, block, block, here.far()).start()
        self.copy(n, 3, block, block, here.peer()).start()

    def fourth(self, n, whole):
        here = self.here
        self.wait(n, 2, whole.at[:, here.c, 0], here.far())
        for column in (self.far, self.both):
            block = self.block(whole, here.c, column)
            self.copy(n, 3, block, block, here.peer()).start()

    def fifth(self, n, whole):
        self.wait(n, 3, whole.at[:, 1 - self.here.c], self.here.peer())


class Scatter:
    def __init__(self, here, send, recv):
        self.here, self.send, self.recv = here, send, recv
        self.own, self.near = here.column(False, False), here.column(True, False)
        self.far, self.both = here.column(False, True), here.column(True, True)

    def copy(self, n, number, source, target, device):
        return remote(source, target, self.send.at[n, number], self.recv.at[n, number], device)

    def view(self, source, column):
        if len(source.shape) == 5:
            return source.at[:, column[0], column[1]]
        return source.at[:, 2 * column[0] + column[1]]

    def to_far(self, n, source, twos):
        return [
            self.copy(n, i, self.view(source, column), twos.at[i], self.here.far())
            for i, column in enumerate((self.both, self.far))
        ]

    def to_near(self, n, source, twos):
        return self.copy(n, 2, self.view(source, self.near), twos.at[2], self.here.near())

    def first(self, n, source, twos):
        for copy in self.to_far(n, source, twos):
            copy.start()

    def add(self, target, other):
        @pl.loop(0, 4)
        def _(level):
            target[level] = low(wide(target[level]) + wide(other[level]))

    def second(self, n, source, twos):
        both, far = self.to_far(n, source, twos)
        both.wait()
        self.add(self.view(source, self.near), twos.at[0])
        self.to_near(n, source, twos).start()
        far.wait()
        self.add(self.view(source, self.own), twos.at[1])

    def third(self, n, source, twos, ends):
        self.to_near(n, source, twos).wait()
        own = self.view(source, self.own)
        self.add(own, twos.at[2])
        for step in (1, 2, 3):
            block = own.at[(self.here.z + step) % 4]
            self.copy(n, 3, block, ends.at[step - 1], self.here.along_z(step)).start()

    def fourth(self, n, source, ends):
        self.copy(n, 3, ends, ends, self.here.along_z(1)).wait()
        own = self.view(source, self.own)
        return wide(own[self.here.z]), [wide(ends[i]) for i in range(3)]


def layer_kernel(
    x_in, og_in, lengths_ref, one_in, two_in, wq_in, wk_in, wv_in, wo_in, wg_in, wu_in, wd_in,
    out_ref, gi_ref, oq_ref, ok_ref, ov_ref, oo_ref, og_out, ou_out, od_out, on_ref,
    wn, wa, wo, wm, pack_a, pack_m, xm, og8, nt8, no8, at8, atb, og_peer, nt_peer, no_peer, at_peer,
    og_t, nt_t, q_ref, k_ref, v_ref, p_ref, mid, acc, gn, gain, tri, tri_peer,
    swap, swap_in, gat, edge, edge_in, outs, outs_peer, gb, gb_peer, mga,
    nb_peer, nb_sum, mlp_twos, mlp_ends, mga_twos, mga_ends, mgo_twos, mgo_ends, nb_twos, nb_ends,
    own_sem, g_send, g_recv, s_send, s_recv, halo_send, halo_recv, edge_send, edge_recv,
    side_send, side_recv, tri_send, tri_recv, swap_send, swap_recv, out_send, out_recv, host_sem,
):
    nb, ga_send, no_t = wn, swap.at[0, :, 0:HALF], nt_t
    here = Place()
    z, c, k, h = here.z, here.c, here.k, here.h
    tiles = wm.shape[0]
    span = tiles * PART
    scale = 1.0 / math.sqrt(HEAD_DIM)
    tokens = x_in.shape[0]
    piece = tokens // 2
    rows = wn.shape[4]
    gather = Gather(here, own_sem, g_send, g_recv)
    scatter = Scatter(here, s_send, s_recv)
    early = 6
    total = early + tiles

    def whole_of(n):
        if n == 0:
            return wn
        return wa.at[n - 1] if n < 4 else wo.at[n - 4]

    def pack_of(n):
        return pack_a.at[n - 1] if 1 <= n < 4 else None

    def parts_of(n):
        if n == 0:
            return []
        if n < 4:
            source = (wk_in, wv_in, wq_in)[n - 1]
            return [(source.at[:, lanes_at(h * HALF, HALF)], source.at[:, lanes_at((1 - h) * HALF, HALF)], 0, HALF)]
        return [(wo_in.at[:, pl.ds((n - 4) * HALF, HALF)], None, 0, HALF)]

    def mlp_parts(f):
        return [
            (
                w.at[:, lanes_at(h * span + f * PART, PART)],
                w.at[:, lanes_at((1 - h) * span + f * PART, PART)],
                i * PART, PART,
            )
            for i, w in enumerate((wg_in, wu_in, wd_in))
        ]

    def step(stage, n):
        late = n >= early
        whole = wm.at[n - early] if late else whole_of(n)
        if stage == 0:
            gather.first(n, whole, pack_m.at[n - early] if late else pack_of(n), n != 0)
        else:
            (gather.second, gather.third, gather.fourth, gather.fifth)[stage - 1](n, whole)

    def steps(stage, *chunks_of):
        for n in chunks_of:
            step(stage, n)

    def tile_steps(f):
        for stage, ahead in enumerate(AHEAD):
            tile = f + ahead

            @pl.when(tile < tiles)
            def _(stage=stage, tile=tile):
                if stage == 0:
                    gather.first(early + tile, wm.at[tile], pack_m.at[tile])
                else:
                    (gather.second, gather.third, gather.fourth)[stage - 1](early + tile, wm.at[tile])

    def halo(which, kind):
        ref = (k_ref, v_ref)[which]
        tail, head = pl.ds((PAD + piece - WINDOW) // rows, WINDOW // rows), pl.ds((PAD - WINDOW) // rows, WINDOW // rows)
        if kind == 0:
            source, target, device = ref.at[:, tail], ref.at[:, head], here.peer()
        elif kind == 1:
            source, target, device = ref.at[pl.ds(0, 2), tail], ref.at[pl.ds(2, 2), head], here.peer()
        else:
            source, target, device = ref.at[pl.ds(2, 2), tail], ref.at[pl.ds(0, 2), head], here.cross()
        return remote(source, target, halo_send.at[which, kind // 2], halo_recv.at[which, kind // 2], device)

    def edge_copy(kind):
        if kind == 0:
            source, target, device = edge, edge_in, here.peer()
        elif kind == 1:
            source, target, device = edge.at[:, 1], edge_in.at[:, 0], here.peer()
        else:
            source, target, device = edge.at[:, 0], edge_in.at[:, 1], here.cross()
        return remote(source, target, edge_send.at[kind // 2], edge_recv.at[kind // 2], device)

    def x_copy():
        return remote(x_in, xm, swap_send.at[0], swap_recv.at[0], here.mate())

    def og_copy(slot):
        view = og8.at[:, :, slot]
        return remote(view, view, swap_send.at[1], swap_recv.at[1], here.mate())

    def nt_copy(slot):
        view = nt8.at[:, :, slot]
        return remote(view, view, swap_send.at[2], swap_recv.at[2], here.mate())

    def at_copy():
        return remote(atb.at[1 - h], at8.at[pl.ds(2 * h, 2)], swap_send.at[3], swap_recv.at[3], here.mate())

    def ga_copy():
        return remote(ga_send, gat.at[h], swap_send.at[4], swap_recv.at[4], here.mate())

    def swap_copy(number):
        return remote(
            swap.at[number % 2], swap_in.at[number], swap_send.at[5 + number], swap_recv.at[5 + number], here.mate()
        )

    def out_store():
        return pltpu.make_async_copy(swap.at[1], out_ref, host_sem.at[8])

    def x_again(i):
        return pltpu.make_async_copy(x_in.at[:, pl.ds(i * HALF, HALF)], gat.at[i], host_sem.at[9 + i])

    def side_copy(number, source, target):
        return remote(source, target, side_send.at[number], side_recv.at[number], here.peer())

    def og_side(number, slot):
        return side_copy(number, og8.at[:, 1 - c, slot], og_peer.at[:, slot])

    def nt_side(number, slot):
        return side_copy(number, nt8.at[:, 1 - c, slot], nt_peer.at[:, slot])

    def no_side():
        return side_copy(4, no8.at[:, 1 - c], no_peer)

    def at_side():
        return side_copy(5, at8.at[:, 1 - c], at_peer)

    def gb_side():
        return side_copy(6, gb, gb_peer)

    def pair_side():
        return side_copy(7, nb.at[:, 1 - c], nb_peer)

    def out_copy(m):
        return remote(outs.at[m], outs_peer.at[m], out_send.at[m], out_recv.at[m], here.peer())

    def tri_copy(f, slot):
        return remote(
            tri.at[f, :, slot], tri_peer.at[f, :, slot], tri_send.at[f], tri_recv.at[f], here.peer()
        )

    def spread(value, target, slot):
        for i in range(8):
            target[i // 2, i % 2, slot] = value[:, i * PART : (i + 1) * PART]

    def joined(source, slot):
        return jnp.concatenate([source[i // 2, i % 2, slot] for i in range(8)], axis=1)

    def turned(own_part, peer_part, target):
        for level in range(4):
            rows = slice(level * PART, (level + 1) * PART)
            left, right = own_part(level), peer_part(level)
            target[rows, 0 : left.shape[0]] = low(wide(left).T)
            target[rows, left.shape[0] : 2 * left.shape[0]] = low(wide(right).T)

    def turned_slot(source, peer, target, slot):
        for level in range(4):
            rows = slice(level * PART, (level + 1) * PART)
            target[rows, lanes_at(slot * tokens, tokens)] = low(wide(source[level, c, slot]).T)
            target[rows, lanes_at((2 + slot) * tokens, tokens)] = low(wide(peer[level, slot]).T)

    og_fetches = [
        pltpu.make_async_copy(og_in.at[:, pl.ds(i * PART, PART)], og8.at[i // 2, i % 2, h], host_sem.at[i])
        for i in range(8)
    ]
    x_fetches = [
        pltpu.make_async_copy(x_in.at[:, pl.ds(i * HALF, HALF)], outs.at[0, i], host_sem.at[9 + i]) for i in range(2)
    ]
    for n in range(early):
        gather.begin(n, parts_of(n), whole_of(n), pack_of(n))
    gain_columns = [jnp.broadcast_to(wide(g[...])[None, :], (LANES // 2, rows)) for g in (one_in, two_in)]
    gather.slot(wn)[...] = low(jnp.concatenate(gain_columns, axis=0).T)
    for copy in og_fetches + x_fetches:
        copy.start()

    @pl.loop(0, tiles)
    def _(f):
        gather.begin(early + f, mlp_parts(f), wm.at[f], pack_m.at[f])

    skipped, begun = (PAD - WINDOW) // rows, PAD // rows
    nothing = jnp.zeros((4, skipped, rows, HALF), jnp.bfloat16)
    for ref in (k_ref, v_ref):
        ref[:, 0:skipped] = nothing

    @pl.when((c == 0) & (k == 0))
    def _():
        for ref in (k_ref, v_ref):
            ref[0:2, skipped:begun] = nothing[0:2]

    @pl.when((c == 1) & (k == 1))
    def _():
        edge_in[:, 1] = jnp.zeros((2, 2, WINDOW, HALF), jnp.bfloat16)

    greet(here.partners())

    steps(0, 0, 1, 2, 3)
    x_copy().start()
    steps(0, 4, 5, 6, 7)
    steps(1, 0, 1, 2, 3)
    steps(2, 0, 1, 2, 3)
    steps(1, 4, 5)
    steps(3, 0, 1, 2, 3)
    for copy in og_fetches:
        copy.wait()
    og_side(0, h).start()
    steps(4, 0)

    gain_rows = wide(flat(wn[...])).T
    gain[0:8, :] = jnp.broadcast_to(gain_rows[0:1, :], (8, gain_rows.shape[1]))
    gain[8:16, :] = jnp.broadcast_to(gain_rows[64:65, :], (8, gain_rows.shape[1]))

    def normed_of(value, row):
        factor = lax.rsqrt(jnp.mean(value * value, axis=-1, keepdims=True) + 1e-05)
        return low(value * factor * gain[row : row + 1, :])

    for copy in x_fetches:
        copy.wait()
    spread(normed_of(wide(jnp.concatenate([outs[0, 0], outs[0, 1]], axis=1)), 0), no8, h)
    x_copy().wait()
    spread(normed_of(wide(xm[...]), 0), no8, 1 - h)
    no_side().start()

    def projected(n, slot):
        return low(mm(joined(no8, slot), flat(wa[n])))

    steps(1, 6)
    for n, ref in ((0, k_ref), (1, v_ref)):
        steps(4, 1 + n)
        for slot in range(2):
            ref[2 * slot : 2 * slot + 2, begun:] = projected(n, slot).reshape(2, piece // rows, rows, HALF)

        @pl.when(c == 0)
        def _(n=n):
            halo(n, 0).start()

        @pl.when(c == 1)
        def _(n=n):
            halo(n, 1).start()

        @pl.when((c == 1) & (k == 0))
        def _(n=n):
            halo(n, 2).start()

        if n == 0:
            steps(2, 4, 5)
        else:
            steps(0, 8, 9, 10)
            steps(1, 7)

    steps(4, 3)
    for slot in range(2):
        q_ref[slot] = projected(2, slot)
    steps(3, 4, 5)
    steps(2, 6)

    for n in range(2):

        @pl.when(c == 0)
        def _(n=n):
            halo(n, 0).wait_send()
            halo(n, 1).wait_recv()

        @pl.when(c == 1)
        def _(n=n):
            halo(n, 0).wait_recv()
            halo(n, 1).wait_send()

        @pl.when((c == 1) & (k == 0))
        def _(n=n):
            halo(n, 2).wait_send()

        @pl.when((c == 0) & (k == 1))
        def _(n=n):
            halo(n, 2).wait_recv()

    def mask_of(slot, row):
        first = (4 * k + 2 * slot + c) * piece
        query_pos = first + lax.broadcasted_iota(jnp.int32, (piece, PAD + piece), 0)
        key_pos = first - PAD + lax.broadcasted_iota(jnp.int32, (piece, PAD + piece), 1)
        start = jnp.zeros((piece, PAD + piece), jnp.int32)
        reached = 0
        for doc in range(lengths_ref.shape[1]):
            reached = reached + lengths_ref[row, doc]
            start = jnp.maximum(start, jnp.where(query_pos >= reached, reached, 0))
        return (key_pos >= start) & (key_pos <= query_pos) & (query_pos - key_pos < WINDOW)

    def attend(slot, row):
        allowed = mask_of(slot, row)
        span_rows = slice(row * piece, (row + 1) * piece)
        for head in range(HEADS // 2):
            cols = slice(head * HEAD_DIM, (head + 1) * HEAD_DIM)
            scores = nt_dot(q_ref[slot, span_rows, cols], flat(k_ref[2 * slot + row, :, :, cols])) * scale
            scores = jnp.where(allowed, scores, -1e30)
            exps = jnp.exp(scores - jnp.max(scores, axis=-1, keepdims=True))
            probs = exps / jnp.sum(exps, axis=-1, keepdims=True)
            p_ref[slot, row, head] = probs
            atb[slot, head // 2, head % 2, span_rows, :] = low(mm(low(probs), flat(v_ref[2 * slot + row, :, :, cols])))

    attend(1 - h, 0)
    attend(1 - h, 1)
    at_copy().start()
    steps(0, *range(11, total))
    og_copy(h).start()
    steps(1, 8, 9)
    steps(2, 7)
    steps(3, 6)
    attend(h, 0)
    attend(h, 1)
    at8[pl.ds(2 * h, 2)] = atb[h]
    steps(4, 4, 5)
    steps(1, 10)
    steps(2, 8)
    at_copy().wait()
    at_side().start()
    attended = jnp.concatenate([at8[i // 2, i % 2] for i in range(8)], axis=1)
    for n in range(2):
        cols = slice(n * HALF, (n + 1) * HALF)
        mid[:, cols] = wide(outs[0, n]) + mm(attended, flat(wo[n]))
    middle = mid[...]
    spread(normed_of(middle, 8), nt8, h)
    nt_copy(h).start()
    nt_side(2, h).start()
    steps(1, 11)
    steps(2, 9)
    steps(3, 7)
    acc[h] = middle
    acc[1 - h] = jnp.zeros(middle.shape, jnp.float32)
    gn[...] = jnp.zeros(gn.shape, jnp.float32)

    def feed(f, slot):
        w_pair = flat(wm[f, :, :, :, :, :, 0 : 2 * PART])
        w_down = flat(wm[f, :, :, :, :, :, 2 * PART : 3 * PART])
        both = mm(joined(nt8, slot), w_pair)
        gates, ups = both[:, 0:PART], both[:, PART:]
        grad_hidden = mm(joined(og8, slot), w_down)
        sigmoid = 1.0 / (1.0 + jnp.exp(-gates))
        silu = gates * sigmoid
        hidden = low(silu * ups)
        grad_gates = low(grad_hidden * ups * sigmoid * (1.0 + gates * (1.0 - sigmoid)))
        grad_ups = low(grad_hidden * silu)
        tri[f, 0, slot] = grad_gates
        tri[f, 1, slot] = grad_ups
        tri[f, 2, slot] = hidden
        tri_copy(f, slot).start()
        acc[slot] += nt_dot(hidden, w_down)
        gn[slot] += nt_dot(jnp.concatenate([grad_gates, grad_ups], axis=1), w_pair)

    og_side(0, h).wait()
    turned_slot(og8, og_peer, og_t, h)
    nt_side(2, h).wait()
    turned_slot(nt8, nt_peer, nt_t, h)
    n_tokens = 2 * tokens

    def ff_grads(f):
        remote(tri.at[f], tri_peer.at[f], tri_send.at[f], tri_recv.at[f], here.peer()).wait()
        pair = mm(nt_t[:, 0:n_tokens], jnp.concatenate([flat(tri[f, 0]), flat(tri[f, 1])], axis=1)) + mm(
            nt_t[:, n_tokens:], jnp.concatenate([flat(tri_peer[f, 0]), flat(tri_peer[f, 1])], axis=1)
        )
        down = mm(og_t[:, 0:n_tokens], flat(tri[f, 2])) + mm(og_t[:, n_tokens:], flat(tri_peer[f, 2]))
        wm[f, :, 0, :, :, :, 0 : 2 * PART] = low(pair).reshape(4, 2, 2, -1, 2 * PART)
        wm[f, :, 0, :, :, :, 2 * PART : 3 * PART] = low(down).reshape(4, 2, 2, -1, PART)

    chunks = tiles + 6

    def chunk(n):
        if n < tiles:
            return wm.at[n, :, 0], mlp_twos.at[n], mlp_ends.at[n]
        n -= tiles
        if n < 2:
            return k_ref.at[:, pl.ds(4 * n, 4)], mgo_twos.at[n], mgo_ends.at[n]
        if n < 5:
            source = mga if n == 2 else v_ref.at[:, pl.ds(4 * (n - 3), 4)]
            return source, mga_twos.at[n - 2], mga_ends.at[n - 2]
        return nb_sum, nb_twos, nb_ends

    def store_tile(n, mine, others):
        back, across, on = others
        for half, value in ((h, mine + across), (1 - h, back + on)):
            for i, ref in enumerate((og_out, ou_out, od_out)):
                ref[:, lanes_at(half * span + n * PART, PART)] = value[:, i * PART : (i + 1) * PART]

    def store(n, mine, others):
        if n < tiles:
            store_tile(n, mine, others)
            return
        back, across, on = others
        n -= tiles
        if 2 <= n < 5:
            for half, value in ((h, mine + across), (1 - h, back + on)):
                (oq_ref, ok_ref, ov_ref)[n - 2][:, lanes_at(half * HALF, HALF)] = value
            return
        value = mine + back + across + on
        if n < 2:
            oo_ref[:, n * HALF : (n + 1) * HALF] = value
        else:
            on_ref[...] = value

    def sum_tick(t):
        for stage, lag in enumerate(SUM_LAGS):
            n = t - lag
            if not 0 <= n < chunks:
                continue
            source, twos, ends = chunk(n)
            if stage == 0:
                scatter.second(n, source, twos)
            elif stage == 1:
                scatter.third(n, source, twos, ends)
            else:
                store(n, *scatter.fourth(n, source, ends))

    def launch_tile(f):
        scatter.first(f, wm.at[f, :, 0], mlp_twos.at[f])

    def launch(n):
        source, twos, _ = chunk(n)
        scatter.first(n, source, twos)

    @pl.loop(0, FIRST_TILES)
    def _(f):
        tile_steps(f)
        gather.fifth(early + f, wm.at[f])
        feed(f, h)

    og_copy(1 - h).wait()
    og_side(1, 1 - h).start()
    nt_copy(1 - h).wait()
    nt_side(3, 1 - h).start()

    @pl.loop(0, FIRST_TILES)
    def _(f):
        @pl.when(FIRST_TILES + f < tiles)
        def _():
            tile_steps(FIRST_TILES + f)

        feed(f, 1 - h)

    @pl.loop(FIRST_TILES, tiles)
    def _(f):
        gather.fifth(early + f, wm.at[f])
        feed(f, h)
        feed(f, 1 - h)

    swap[0] = low(gn[1 - h])
    swap_copy(0).start()
    og_side(1, 1 - h).wait()
    turned_slot(og8, og_peer, og_t, 1 - h)
    nt_side(3, 1 - h).wait()
    turned_slot(nt8, nt_peer, nt_t, 1 - h)

    @pl.loop(0, tiles)
    def _(f):
        ff_grads(f)
        launch_tile(f)


    def close_middle():
        swap_copy(0).wait()
        middle = mid[...]
        factor = lax.rsqrt(jnp.mean(middle * middle, axis=-1, keepdims=True) + 1e-05)
        grad_normed = gn[h] + wide(swap_in[0])
        through = grad_normed * gain[8:9, :]
        shift = jnp.mean(through * middle, axis=-1, keepdims=True) * factor * factor * factor
        grad_middle = wide(joined(og8, h)) + factor * through - middle * shift
        gi_ref[...] = grad_middle
        gb[...] = low(grad_middle)
        gb_side().start()
        gain[8:16, :] = jnp.broadcast_to(
            jnp.sum(grad_normed * middle * factor, axis=0, keepdims=True), (8, middle.shape[1])
        )

    def to_attended():
        def part(half):
            rows = pl.ds(2 * half, 2)
            return low(nt_dot(gb[:, 0:HALF], flat(wo[0, rows])) + nt_dot(gb[:, HALF:], flat(wo[1, rows])))

        swap[0, :, 0:HALF] = part(1 - h)
        ga_copy().start()
        swap[1] = low(acc[1 - h])
        swap_copy(1).start()
        gat[h] = part(h)

    def keep_out():
        mid[...] = acc[h]

    def close_out():
        swap_copy(1).wait()
        swap[1] = low(mid[...] + wide(swap_in[1]))
        out_store().start()

    def attend_back(slot):
        for row in range(2):
            span_rows = slice(row * piece, (row + 1) * piece)
            for head in range(HEADS // 2):
                cols = slice(head * HEAD_DIM, (head + 1) * HEAD_DIM)
                there = slice(row * HALF + head * HEAD_DIM, row * HALF + (head + 1) * HEAD_DIM)
                grad = gat[slot, span_rows, cols]
                probs = p_ref[slot, row, head]
                gn[slot, :, there] = tn_dot(low(probs), grad)
                grad_probs = nt_dot(grad, flat(v_ref[2 * slot + row, :, :, cols]))
                inner = jnp.sum(grad_probs * probs, axis=-1, keepdims=True)
                grad_scores = low(probs * (grad_probs - inner))
                outs[2, slot, span_rows, cols] = low(mm(grad_scores, flat(k_ref[2 * slot + row, :, :, cols])) * scale)
                acc[slot, :, there] = tn_dot(grad_scores, q_ref[slot, span_rows, cols]) * scale
            there = slice(row * HALF, (row + 1) * HALF)
            edge[0, slot, row] = low(acc[slot, PAD - WINDOW : PAD, there])
            edge[1, slot, row] = low(gn[slot, PAD - WINDOW : PAD, there])

    def send_edge():
        out_copy(2).start()

        @pl.when(c == 1)
        def _():
            edge_copy(0).start()

        @pl.when(c == 0)
        def _():
            edge_copy(1).start()

        @pl.when((c == 0) & (k == 1))
        def _():
            edge_copy(2).start()

    def close_edge():
        @pl.when(c == 1)
        def _():
            edge_copy(0).wait_send()
            edge_copy(1).wait_recv()

        @pl.when(c == 0)
        def _():
            edge_copy(0).wait_recv()
            edge_copy(1).wait_send()

        @pl.when((c == 0) & (k == 1))
        def _():
            edge_copy(2).wait_send()

        @pl.when((c == 1) & (k == 0))
        def _():
            edge_copy(2).wait_recv()

        inside = piece - WINDOW
        for m, source in ((0, acc), (1, gn)):
            for slot in range(2):
                for row in range(2):
                    there = slice(row * HALF, (row + 1) * HALF)
                    first = row * piece
                    outs[m, slot, first : first + inside, :] = low(source[slot, PAD : PAD + inside, there])
                    outs[m, slot, first + inside : first + piece, :] = low(
                        source[slot, PAD + inside : PAD + piece, there] + wide(edge_in[m, slot, row])
                    )
            out_copy(m).start()

    def to_input(slot):
        grad = nt_dot(outs[0, slot], flat(wa[0]))
        for m in (1, 2):
            grad = grad + nt_dot(outs[m, slot], flat(wa[m]))
        return grad

    def inverse_rms(value):
        return lax.rsqrt(jnp.mean(value * value, axis=-1, keepdims=True) + 1e-05)

    def send_input():
        x = wide(xm[...])
        part = to_input(1 - h)
        swap[0] = low(part)
        swap_copy(2).start()
        one = jnp.sum(part * x * inverse_rms(x), axis=0, keepdims=True)
        part = to_input(h)
        acc[0] = part
        for i in range(2):
            x_again(i).wait()
        x = wide(jnp.concatenate([gat[0], gat[1]], axis=1))
        one = one + jnp.sum(part * x * inverse_rms(x), axis=0, keepdims=True)
        width = one.shape[1]
        stacked = jnp.concatenate(
            [
                jnp.broadcast_to(one, (LANES // 2, width)),
                jnp.broadcast_to(gain[8:9, :], (LANES // 2, width)),
            ],
            axis=0,
        )
        nb[...] = low(stacked.T).reshape(nb.shape)
        pair_side().start()

    def close_input():
        swap_copy(2).wait()
        grad_normed = acc[0] + wide(swap_in[2])
        x = wide(jnp.concatenate([gat[0], gat[1]], axis=1))
        factor = inverse_rms(x)
        through = grad_normed * gain[0:1, :]
        shift = jnp.mean(through * x, axis=-1, keepdims=True) * factor * factor * factor
        gi_ref[...] += factor * through - x * shift

    def close_norm():
        pair_side().wait()
        nb_sum[...] = low(wide(nb[:, c]) + wide(nb_peer[...]))

    def turn_normed():
        no_side().wait()
        turned(lambda i: flat(no8[i, c]), lambda i: flat(no_peer[i]), no_t)

    def wout_grads():
        at_side().wait()
        turned(lambda i: at8[i, c], lambda i: at_peer[i], og_t)
        gb_side().wait()
        for n in range(2):
            cols = slice(n * HALF, (n + 1) * HALF)
            grad = mm(og_t[:, 0:tokens], gb[:, cols]) + mm(og_t[:, tokens : 2 * tokens], gb_peer[:, cols])
            k_ref[:, 4 * n : 4 * n + 4] = low(grad).reshape(4, 4, -1, HALF)

    def attn_grads(m):
        out_copy(m).wait()
        grad = mm(no_t[:, 0:n_tokens], flat(outs[m])) + mm(no_t[:, n_tokens:], flat(outs_peer[m]))
        if m == 2:
            mga[...] = low(grad).reshape(mga.shape)
        else:
            v_ref[:, 4 * m : 4 * m + 4] = low(grad).reshape(4, 4, -1, HALF)

    def ticks(first, last):
        for t in range(first, last):
            sum_tick(t)

    ticks(0, 2)
    close_middle()
    to_attended()
    keep_out()
    ticks(2, 4)
    attend_back(h)
    ga_copy().wait()
    attend_back(1 - h)
    send_edge()
    for i in range(2):
        x_again(i).start()
    ticks(4, 7)
    turn_normed()
    attn_grads(2)
    wout_grads()
    launch(tiles)
    launch(tiles + 1)
    launch(tiles + 2)
    ticks(7, 9)
    close_edge()
    ticks(9, 10)
    send_input()
    for m in range(2):
        attn_grads(m)
        launch(tiles + 3 + m)
    close_norm()
    launch(tiles + 5)
    ticks(10, 14)
    close_out()
    close_input()
    ticks(14, chunks + SUM_LAGS[-1])
    out_store().wait()


def deliver_kernel(count, *refs):
    sources, targets, refs = refs[:count], refs[count : 2 * count + 1], refs[2 * count + 1 :]
    held, vectors, (in_sem, out_sem) = refs[:count], refs[count : count + 2], refs[count + 2 :]
    ins = [pltpu.make_async_copy(s, v, in_sem.at[i]) for i, (s, v) in enumerate(zip(sources, held))]
    leave = (*vectors, *held[1:])
    outs = [pltpu.make_async_copy(v, t, out_sem.at[i]) for i, (v, t) in enumerate(zip(leave, targets))]
    for copy in ins:
        copy.start()
    ins[0].wait()
    turned = held[0][...].T
    for i in range(2):
        vectors[i][...] = turned[i * LANES // 2, :]
        outs[i].start()
    for arrived, leaving in zip(ins[1:], outs[2:]):
        arrived.wait()
        leaving.start()
    for copy in outs:
        copy.wait()


def delivered(norms, arrays):
    anywhere = pl.BlockSpec(memory_space=pl.ANY)
    count = len(arrays) + 1
    vector = (norms.shape[:1], norms.dtype)
    return pl.pallas_call(
        functools.partial(deliver_kernel, count),
        out_shape=[jax.ShapeDtypeStruct(*vector)] * 2 + [jax.ShapeDtypeStruct(a.shape, a.dtype) for a in arrays],
        in_specs=[anywhere] * count,
        out_specs=[anywhere] * (count + 1),
        scratch_shapes=[pltpu.VMEM(a.shape, a.dtype) for a in (norms, *arrays)]
        + [pltpu.VMEM(*vector)] * 2
        + [pltpu.SemaphoreType.DMA((count,)), pltpu.SemaphoreType.DMA((count + 1,))],
        compiler_params=pltpu.CompilerParams(vmem_limit_bytes=60 * 2**20),
        name="deliver",
    )(norms, *arrays)


def fused(hidden_in, lengths, out_grad, gain_shards, weight_shards):
    hidden = hidden_in.reshape(-1, hidden_in.shape[-1])
    tokens, width = hidden.shape
    rows = weight_shards[0].shape[0]
    tiles = weight_shards[4].shape[1] // (2 * PART)
    bf, fl = jnp.bfloat16, jnp.float32
    every, mine = (4, 2, 2, 2, rows), (4, 2, 2, rows)
    part = 3 * PART
    dma = pltpu.SemaphoreType.DMA
    vmem, anywhere = pl.BlockSpec(memory_space=pltpu.VMEM), pl.BlockSpec(memory_space=pl.ANY)
    shape = jax.ShapeDtypeStruct
    piece = tokens // 2
    keys = (4, (PAD + piece) // rows, rows, HALF)
    scratch = [
        ((*every, LANES), bf), ((3, *every, HALF), bf), ((2, *every, HALF), bf), ((tiles, *every, part), bf),
        ((3, rows, HALF), bf), ((tiles, rows, part), bf), ((tokens, width), bf),
        *[((4, 2, 2, tokens, PART), bf)] * 3, ((4, 2, tokens, PART), bf), ((2, 2, 2, tokens, PART), bf),
        *[((4, 2, tokens, PART), bf)] * 3, ((4, tokens, PART), bf),
        *[((width // 2, 4 * tokens), bf)] * 2,
        ((2, tokens, HALF), bf), (keys, bf), (keys, bf), ((2, 2, HEADS // 2, piece, PAD + piece), fl),
        ((tokens, width), fl), ((2, tokens, width), fl), ((2, tokens, width), fl),
        ((16, width), fl), ((tiles, 3, 2, tokens, PART), bf), ((tiles, 3, 2, tokens, PART), bf),
        ((2, tokens, width), bf), ((3, tokens, width), bf), ((2, tokens, HALF), bf),
        ((2, 2, 2, WINDOW, HALF), bf), ((2, 2, 2, WINDOW, HALF), bf),
        ((3, 2, tokens, HALF), bf), ((3, 2, tokens, HALF), bf), ((tokens, width), bf), ((tokens, width), bf),
        ((*mine, HALF), bf),
        ((*mine, LANES), bf), ((*mine, LANES), bf),
        ((tiles, 3, 4, rows, part), bf), ((tiles, 3, rows, part), bf),
        ((3, 3, 4, rows, HALF), bf), ((3, 3, rows, HALF), bf),
        ((2, 3, 4, rows, HALF), bf), ((2, 3, rows, HALF), bf),
        ((3, 4, rows, LANES), bf), ((3, rows, LANES), bf),
    ]
    count, chunks = 6 + tiles, 6 + tiles
    results = pl.pallas_call(
        layer_kernel,
        out_shape=[shape((tokens, width), bf), shape((tokens, width), fl)]
        + [shape((rows, width), fl)] * 4 + [shape((rows, 2 * tiles * PART), fl)] * 3
        + [shape((rows, LANES), fl)],
        in_specs=[anywhere, anywhere, pl.BlockSpec(memory_space=pltpu.SMEM), vmem, vmem] + [anywhere] * 7,
        out_specs=[anywhere] + [vmem] * 9,
        scratch_shapes=[pltpu.VMEM(*s) for s in scratch]
        + [
            dma((count, 2)), dma((count, 4)), dma((count, 4)), dma((chunks, 4)), dma((chunks, 4)),
            dma((2, 2)), dma((2, 2)), dma((2,)), dma((2,)), dma((8,)), dma((8,)),
            dma((tiles,)), dma((tiles,)), dma((8,)), dma((8,)), dma((3,)), dma((3,)), dma((12,)),
        ],
        compiler_params=pltpu.CompilerParams(
            collective_id=0, has_side_effects=True, vmem_limit_bytes=63 * 2**20
        ),
        name="layer",
    )(hidden, out_grad.reshape(hidden.shape), lengths, *gain_shards, *weight_shards)
    one, two, block_out, grad_in, query, key, value, wout, gate, up, down = delivered(results[9], results[:9])
    return (
        block_out.reshape(hidden_in.shape), grad_in.reshape(hidden_in.shape),
        one, query, key, value, wout, two, gate, up, down,
    )


def layer(hidden_in, lengths, out_grad, gains, weights):
    score_scale = 1.0 / math.sqrt(HEAD_DIM)
    tokens = hidden_in.shape[1]
    gain_one, gain_two = gains
    w_query, w_key, w_value, w_out, w_gate, w_up, w_down = weights
    inputs = hidden_in.astype(jnp.float32)
    normed_one = rms_scale(inputs, gain_one).astype(jnp.bfloat16)
    queries = project(normed_one, w_query).astype(jnp.bfloat16)
    keys = project(normed_one, w_key).astype(jnp.bfloat16)
    values = project(normed_one, w_value).astype(jnp.bfloat16)
    tails = jnp.stack([keys[:, tokens - WINDOW :], values[:, tokens - WINDOW :]])
    received = passed_along(tails, "seq", 1)
    keys_all = jnp.concatenate([received[0], keys], axis=1)
    values_all = jnp.concatenate([received[1], values], axis=1)
    allowed = window_mask(lengths, lax.axis_index("seq"), tokens)
    scores = scores_of(queries, keys_all, allowed)
    top = jnp.max(scores, axis=-1, keepdims=True)
    exps = jnp.exp(scores - top)
    probs = exps / jnp.sum(exps, axis=-1, keepdims=True)
    probs_low = probs.astype(jnp.bfloat16)
    mixed = jnp.einsum(
        "rhqk,rkhd->rqhd", probs_low, split_heads(values_all), preferred_element_type=jnp.float32
    )
    attended = merge_heads(mixed).astype(jnp.bfloat16)
    middle = inputs + project(attended, w_out)
    normed_two = rms_scale(middle, gain_two).astype(jnp.bfloat16)
    gates = project(normed_two, w_gate)
    ups = project(normed_two, w_up)
    hidden_act = swiglu(gates, ups).astype(jnp.bfloat16)
    block_out = (middle + project_back(hidden_act, w_down)).astype(jnp.bfloat16)
    grad_hidden = project(out_grad, w_down)
    unused, swiglu_back = jax.vjp(swiglu, gates, ups)
    grad_gates, grad_ups = swiglu_back(grad_hidden)
    grad_gates = grad_gates.astype(jnp.bfloat16)
    grad_ups = grad_ups.astype(jnp.bfloat16)
    grad_down = weight_grad(out_grad, hidden_act)
    grad_gate = weight_grad(normed_two, grad_gates)
    grad_up = weight_grad(normed_two, grad_ups)
    grad_normed_two = project_back(grad_gates, w_gate) + project_back(grad_ups, w_up)
    unused, norm_two_back = jax.vjp(rms_scale, middle, gain_two)
    grad_middle_part, grad_norm2 = norm_two_back(grad_normed_two)
    grad_middle = out_grad.astype(jnp.float32) + grad_middle_part
    grad_branch = grad_middle.astype(jnp.bfloat16)
    grad_wout = weight_grad(attended, grad_branch)
    grad_attended = project_back(grad_branch, w_out).astype(jnp.bfloat16)
    grad_heads = split_heads(grad_attended)
    grad_values_all = jnp.einsum(
        "rhqk,rqhd->rkhd", probs_low, grad_heads, preferred_element_type=jnp.float32
    )
    grad_probs = jnp.einsum(
        "rqhd,rkhd->rhqk", grad_heads, split_heads(values_all), preferred_element_type=jnp.float32
    )
    grad_scores = (
        probs * (grad_probs - jnp.sum(grad_probs * probs, axis=-1, keepdims=True))
    ).astype(jnp.bfloat16)
    grad_queries = score_scale * merge_heads(
        jnp.einsum(
            "rhqk,rkhd->rqhd", grad_scores, split_heads(keys_all),
            preferred_element_type=jnp.float32,
        )
    )
    grad_keys_all = score_scale * merge_heads(
        jnp.einsum(
            "rhqk,rqhd->rkhd", grad_scores, split_heads(queries),
            preferred_element_type=jnp.float32,
        )
    )
    grad_values_all = merge_heads(grad_values_all)
    halo_grads = jnp.stack([grad_keys_all[:, :WINDOW], grad_values_all[:, :WINDOW]])
    returned = passed_along(halo_grads.astype(jnp.bfloat16), "seq", -1).astype(halo_grads.dtype)
    grad_keys = (
        grad_keys_all[:, WINDOW:].at[:, tokens - WINDOW :].add(returned[0]).astype(jnp.bfloat16)
    )
    grad_values = (
        grad_values_all[:, WINDOW:].at[:, tokens - WINDOW :].add(returned[1]).astype(jnp.bfloat16)
    )
    grad_queries = grad_queries.astype(jnp.bfloat16)
    grad_query = weight_grad(normed_one, grad_queries)
    grad_key = weight_grad(normed_one, grad_keys)
    grad_value = weight_grad(normed_one, grad_values)
    grad_normed_one = (
        project_back(grad_queries, w_query)
        + project_back(grad_keys, w_key)
        + project_back(grad_values, w_value)
    )
    unused, norm_one_back = jax.vjp(rms_scale, inputs, gain_one)
    grad_inputs_part, grad_norm1 = norm_one_back(grad_normed_one)
    grad_in = grad_middle + grad_inputs_part
    grads = (grad_query, grad_key, grad_value, grad_wout, grad_gate, grad_up, grad_down)
    return block_out, grad_in, (grad_norm1, grad_norm2), grads


def shards(
    hidden_in, lengths, norm1_gain, w_query, w_key, w_value, w_out,
    norm2_gain, w_gate, w_up, w_down, out_grad,
):
    gain_shards = (norm1_gain, norm2_gain)
    weight_shards = (w_query, w_key, w_value, w_out, w_gate, w_up, w_down)
    if (lax.axis_size("seq"), lax.axis_size("rows")) == (SEQ_PIECES, ROW_GROUPS):
        return fused(hidden_in, lengths, out_grad, gain_shards, weight_shards)
    gains = [g.astype(jnp.float32) for g in gathered_by_xla(gain_shards)]
    weights = gathered_by_xla(weight_shards)
    block_out, grad_in, norms, grads = layer(hidden_in, lengths, out_grad, gains, weights)
    norms, grads = scattered_by_xla(norms), scattered_by_xla(grads)
    return (
        block_out, grad_in, norms[0], grads[0], grads[1], grads[2], grads[3],
        norms[1], grads[4], grads[5], grads[6],
    )


def solution(mesh):
    tokens = P("rows", "seq", None)
    vector = P(("seq", "rows"))
    matrix = P(("seq", "rows"), None)
    in_specs = (
        tokens, P("rows", None), vector, matrix, matrix, matrix, matrix,
        vector, matrix, matrix, matrix, tokens,
    )
    out_specs = (
        tokens, tokens, vector, matrix, matrix, matrix, matrix,
        vector, matrix, matrix, matrix,
    )
    return jax.shard_map(shards, mesh=mesh, in_specs=in_specs, out_specs=out_specs, check_vma=False)
```

```python
import functools
import math

import jax
import jax.numpy as jnp
from jax import lax
from jax.experimental import pallas as pl
from jax.experimental.pallas import tpu as pltpu
from jax.sharding import PartitionSpec as P

HEADS = 8
HEAD_DIM = 128
WINDOW = 64
LANES = 128
MESH = pl.DeviceIdType.MESH


def passed_along(block, axis, distance):
    devices = range(lax.axis_size(axis))
    route = [(i - distance, i) for i in devices if i - distance in devices]
    return lax.ppermute(block, axis, route)


def rms_scale(values, gain):
    factor = lax.rsqrt(jnp.mean(values * values, axis=-1, keepdims=True) + 1e-05)
    return values * factor * gain


def swiglu(gates, ups):
    return jax.nn.silu(gates) * ups


def project(left, weight):
    return jnp.dot(left, weight, preferred_element_type=jnp.float32)


def project_back(grad, weight):
    return lax.dot_general(
        grad, weight, (((2,), (1,)), ((), ())), preferred_element_type=jnp.float32
    )


def weight_grad(left, grad):
    return jnp.einsum("rtd,rtf->df", left, grad, preferred_element_type=jnp.float32)


def split_heads(values):
    return values.reshape(values.shape[0], values.shape[1], HEADS, HEAD_DIM)


def merge_heads(values):
    return values.reshape(values.shape[0], values.shape[1], HEADS * HEAD_DIM)


def window_mask(lengths, seq_index, tokens):
    docs = lengths.shape[1]
    upto = jnp.arange(docs)[:, None] >= jnp.arange(docs)[None, :]
    ends = jnp.sum(jnp.where(upto[None], lengths[:, None, :], 0), axis=2)
    query_pos = seq_index * tokens + jnp.arange(tokens, dtype=jnp.int32)
    key_pos = seq_index * tokens - WINDOW + jnp.arange(tokens + WINDOW, dtype=jnp.int32)
    starts = jnp.max(
        jnp.where(
            ends[:, None, :] <= query_pos[None, :, None],
            ends[:, None, :],
            jnp.zeros_like(ends[:, None, :]),
        ),
        axis=2,
    )
    allowed = (
        (key_pos[None, None, :] >= starts[:, :, None])
        & (key_pos[None, None, :] <= query_pos[None, :, None])
        & (query_pos[None, :, None] - key_pos[None, None, :] < WINDOW)
    )
    return allowed[:, None]


def scores_of(queries, keys_all, allowed):
    score_scale = 1.0 / math.sqrt(HEAD_DIM)
    scores = (
        jnp.einsum(
            "rqhd,rkhd->rhqk",
            split_heads(queries),
            split_heads(keys_all),
            preferred_element_type=jnp.float32,
        )
        * score_scale
    )
    return jnp.where(allowed, scores, -1e30)


def gathered_by_xla(shards):
    return [lax.all_gather(s, ("seq", "rows"), axis=0, tiled=True) for s in shards]


def scattered_by_xla(totals):
    return [
        lax.psum_scatter(t.astype(jnp.float32), ("seq", "rows"), scatter_dimension=0, tiled=True)
        for t in totals
    ]


SEQ_PIECES = 8
ROW_GROUPS = 4
PART = 128
HALF = 512
PAD = 128
AHEAD = (11, 6, 4, 2)
FIRST_TILES = 7
SUM_LAGS = (0, 4, 8)


class Place:
    def __init__(self):
        seq, rows = lax.axis_index("seq"), lax.axis_index("rows")
        self.z, self.c = seq // 2, seq % 2
        self.k, self.h = self.z // 2, self.z % 2
        self.y, self.x = rows // 2, rows % 2
        self.turn_y, self.turn_x = 1 - 2 * self.y, 1 - 2 * self.x

    def column(self, near, far):
        y, x, c = self.y, self.x, self.c
        if near:
            y, x = y + c * self.turn_y, x + (1 - c) * self.turn_x
        if far:
            y, x = y + (1 - c) * self.turn_y, x + c * self.turn_x
        return y, x

    def device(self, z, c, column):
        return (2 * z + c, 2 * column[0] + column[1])

    def near(self):
        return self.device(self.z, self.c, self.column(True, False))

    def far(self):
        return self.device(self.z, self.c, self.column(False, True))

    def peer(self):
        return self.device(self.z, 1 - self.c, (self.y, self.x))

    def mate(self):
        return self.device(2 * self.k + 1 - self.h, self.c, (self.y, self.x))

    def across(self):
        return self.device(2 * (1 - self.k) + self.h, self.c, (self.y, self.x))

    def cross(self):
        return self.device(2 * (1 - self.k) + self.h, 1 - self.c, (self.y, self.x))

    def along_z(self, step):
        return self.device((self.z + step) % 4, self.c, (self.y, self.x))

    def partners(self):
        return [self.near(), self.far(), self.peer(), self.cross()] + [self.along_z(i) for i in (1, 2, 3)]


def greet(partners):
    barrier = pltpu.get_barrier_semaphore()
    for partner in partners:
        pl.semaphore_signal(barrier, inc=1, device_id=partner, device_id_type=MESH)
    pl.semaphore_wait(barrier, len(partners))


def remote(source, target, send, recv, device):
    return pltpu.make_async_remote_copy(
        src_ref=source, dst_ref=target, send_sem=send, recv_sem=recv,
        device_id=device, device_id_type=MESH,
    )


def nt_dot(left, right):
    return lax.dot_general(left, right, (((1,), (1,)), ((), ())), preferred_element_type=jnp.float32)


def tn_dot(left, right):
    return lax.dot_general(left, right, (((0,), (0,)), ((), ())), preferred_element_type=jnp.float32)


def mm(left, right):
    return jnp.dot(left, right, preferred_element_type=jnp.float32)


def flat(value):
    return value.reshape(-1, value.shape[-1])


def low(value):
    return value.astype(jnp.bfloat16)


def wide(value):
    return value.astype(jnp.float32)


def lanes_at(first, width):
    return pl.ds(pl.multiple_of(first, PART), width)


class Gather:
    def __init__(self, here, own_sem, send, recv):
        self.here, self.own_sem, self.send, self.recv = here, own_sem, send, recv
        self.own, self.near = here.column(False, False), here.column(True, False)
        self.far, self.both = here.column(False, True), here.column(True, True)

    def slot(self, whole):
        return whole.at[self.here.z, self.here.c, self.own[0], self.own[1]]

    def block(self, whole, core, column):
        return whole.at[:, core, column[0], column[1]]

    def copy(self, n, number, source, target, device):
        return remote(source, target, self.send.at[n, number], self.recv.at[n, number], device)

    def wait(self, n, number, view, device):
        self.copy(n, number, view, view, device).wait()

    def begin(self, n, parts, whole, pack):
        slot = self.slot(whole)
        for kept, given, first, width in parts:
            pltpu.make_async_copy(kept, slot.at[:, pl.ds(first, width)], self.own_sem.at[n, 0]).start()
            if pack is not None:
                pltpu.make_async_copy(given, pack.at[:, pl.ds(first, width)], self.own_sem.at[n, 1]).start()

    def first(self, n, whole, pack, fetched=True):
        slot = self.slot(whole)
        if fetched:
            pltpu.make_async_copy(slot, slot, self.own_sem.at[n, 0]).wait()
        if pack is not None:
            pltpu.make_async_copy(pack, pack, self.own_sem.at[n, 1]).wait()
        for step in (1, 2, 3):
            source = slot if pack is None or step == 2 else pack
            self.copy(n, 0, source, slot, self.here.along_z(step)).start()

    def second(self, n, whole):
        here = self.here
        self.wait(n, 0, whole.at[pl.ds(0, 3), here.c, self.own[0], self.own[1]], here.along_z(1))
        block = self.block(whole, here.c, self.own)
        self.copy(n, 1, block, block, here.near()).start()
        self.copy(n, 2, block, block, here.far()).start()
        self.copy(n, 3, block, block, here.peer()).start()

    def third(self, n, whole):
        here = self.here
        block = self.block(whole, here.c, self.near)
        self.wait(n, 1, block, here.near())
        self.copy(n, 2, block, block, here.far()).start()
        self.copy(n, 3, block, block, here.peer()).start()

    def fourth(self, n, whole):
        here = self.here
        self.wait(n, 2, whole.at[:, here.c, 0], here.far())
        for column in (self.far, self.both):
            block = self.block(whole, here.c, column)
            self.copy(n, 3, block, block, here.peer()).start()

    def fifth(self, n, whole):
        self.wait(n, 3, whole.at[:, 1 - self.here.c], self.here.peer())


class Scatter:
    def __init__(self, here, send, recv):
        self.here, self.send, self.recv = here, send, recv
        self.own, self.near = here.column(False, False), here.column(True, False)
        self.far, self.both = here.column(False, True), here.column(True, True)

    def copy(self, n, number, source, target, device):
        return remote(source, target, self.send.at[n, number], self.recv.at[n, number], device)

    def view(self, source, column):
        if len(source.shape) == 5:
            return source.at[:, column[0], column[1]]
        return source.at[:, 2 * column[0] + column[1]]

    def to_far(self, n, source, twos):
        return [
            self.copy(n, i, self.view(source, column), twos.at[i], self.here.far())
            for i, column in enumerate((self.both, self.far))
        ]

    def to_near(self, n, source, twos):
        return self.copy(n, 2, self.view(source, self.near), twos.at[2], self.here.near())

    def first(self, n, source, twos):
        for copy in self.to_far(n, source, twos):
            copy.start()

    def add(self, target, other):
        @pl.loop(0, 4)
        def _(level):
            target[level] = low(wide(target[level]) + wide(other[level]))

    def second(self, n, source, twos):
        both, far = self.to_far(n, source, twos)
        both.wait()
        self.add(self.view(source, self.near), twos.at[0])
        self.to_near(n, source, twos).start()
        far.wait()
        self.add(self.view(source, self.own), twos.at[1])

    def third(self, n, source, twos, ends):
        self.to_near(n, source, twos).wait()
        own = self.view(source, self.own)
        self.add(own, twos.at[2])
        for step in (1, 2, 3):
            block = own.at[(self.here.z + step) % 4]
            self.copy(n, 3, block, ends.at[step - 1], self.here.along_z(step)).start()

    def fourth(self, n, source, ends):
        self.copy(n, 3, ends, ends, self.here.along_z(1)).wait()
        own = self.view(source, self.own)
        return wide(own[self.here.z]), [wide(ends[i]) for i in range(3)]


def layer_kernel(
    x_in, og_in, lengths_ref, one_in, two_in, wq_in, wk_in, wv_in, wo_in, wg_in, wu_in, wd_in,
    out_ref, gi_to, oq_to, ok_to, ov_to, oo_to, og_to, ou_to, od_to, on_to,
    gi_ref, oq_ref, ok_ref, ov_ref, oo_ref, og_out, ou_out, od_out, on_ref,
    wn, wa, wo, wm, pack_a, pack_m, xm, og8, nt8, no8, at8, atb, og_peer, nt_peer, no_peer, at_peer,
    og_t, nt_t, q_ref, k_ref, v_ref, p_ref, mid, acc, gn, gain, tri, tri_peer,
    swap, swap_in, gat, edge, edge_in, outs, outs_peer, gb, gb_peer, mga,
    nb_peer, nb_sum, mlp_twos, mlp_ends, mga_twos, mga_ends, mgo_twos, mgo_ends, nb_twos, nb_ends,
    own_sem, g_send, g_recv, s_send, s_recv, halo_send, halo_recv, edge_send, edge_recv,
    side_send, side_recv, tri_send, tri_recv, swap_send, swap_recv, out_send, out_recv, host_sem, row_send, row_recv,
):
    nb, no_t = wn, nt_t
    here = Place()
    z, c, k, h = here.z, here.c, here.k, here.h
    tiles = wm.shape[0]
    span = tiles * PART
    scale = 1.0 / math.sqrt(HEAD_DIM)
    tokens = x_in.shape[0]
    piece = tokens // 2
    rows = wn.shape[4]
    gather = Gather(here, own_sem, g_send, g_recv)
    scatter = Scatter(here, s_send, s_recv)
    early = 6
    total = early + tiles

    def whole_of(n):
        if n == 0:
            return wn
        return wa.at[n - 1] if n < 4 else wo.at[n - 4]

    def pack_of(n):
        return pack_a.at[n - 1] if 1 <= n < 4 else None

    def parts_of(n):
        if n == 0:
            return []
        if n < 4:
            source = (wk_in, wv_in, wq_in)[n - 1]
            return [(source.at[:, lanes_at(h * HALF, HALF)], source.at[:, lanes_at((1 - h) * HALF, HALF)], 0, HALF)]
        return [(wo_in.at[:, pl.ds((n - 4) * HALF, HALF)], None, 0, HALF)]

    def mlp_parts(f):
        return [
            (
                w.at[:, lanes_at(h * span + f * PART, PART)],
                w.at[:, lanes_at((1 - h) * span + f * PART, PART)],
                i * PART, PART,
            )
            for i, w in enumerate((wg_in, wu_in, wd_in))
        ]

    def step(stage, n):
        late = n >= early
        whole = wm.at[n - early] if late else whole_of(n)
        if stage == 0:
            gather.first(n, whole, pack_m.at[n - early] if late else pack_of(n), n != 0)
        else:
            (gather.second, gather.third, gather.fourth, gather.fifth)[stage - 1](n, whole)

    def steps(stage, *chunks_of):
        for n in chunks_of:
            step(stage, n)

    def tile_steps(f):
        for stage, ahead in enumerate(AHEAD):
            tile = f + ahead

            @pl.when(tile < tiles)
            def _(stage=stage, tile=tile):
                if stage == 0:
                    gather.first(early + tile, wm.at[tile], pack_m.at[tile])
                else:
                    (gather.second, gather.third, gather.fourth)[stage - 1](early + tile, wm.at[tile])

    def halo(which, kind):
        ref = (k_ref, v_ref)[which]
        tail, head = pl.ds((PAD + piece - WINDOW) // rows, WINDOW // rows), pl.ds((PAD - WINDOW) // rows, WINDOW // rows)
        if kind == 0:
            source, target, device = ref.at[:, tail], ref.at[:, head], here.peer()
        elif kind == 1:
            source, target, device = ref.at[pl.ds(0, 2), tail], ref.at[pl.ds(2, 2), head], here.peer()
        else:
            source, target, device = ref.at[pl.ds(2, 2), tail], ref.at[pl.ds(0, 2), head], here.cross()
        return remote(source, target, halo_send.at[which, kind // 2], halo_recv.at[which, kind // 2], device)

    def edge_copy(kind):
        if kind == 0:
            source, target, device = edge, edge_in, here.peer()
        elif kind == 1:
            source, target, device = edge.at[:, 1], edge_in.at[:, 0], here.peer()
        else:
            source, target, device = edge.at[:, 0], edge_in.at[:, 1], here.cross()
        return remote(source, target, edge_send.at[kind // 2], edge_recv.at[kind // 2], device)

    def x_copy():
        return remote(x_in, xm, swap_send.at[0], swap_recv.at[0], here.mate())

    def og_copy(slot):
        view = og8.at[:, :, slot]
        return remote(view, view, swap_send.at[1], swap_recv.at[1], here.mate())

    def nt_copy(slot):
        view = nt8.at[:, :, slot]
        return remote(view, view, swap_send.at[2], swap_recv.at[2], here.mate())

    def at_copy():
        return remote(atb.at[1 - h], at8.at[pl.ds(2 * h, 2)], swap_send.at[3], swap_recv.at[3], here.mate())

    def ga_copy(row):
        there = pl.ds(row * piece, piece)
        return remote(
            swap.at[0, there, pl.ds(0, HALF)], gat.at[h, there], row_send.at[2 + row], row_recv.at[2 + row], here.mate()
        )

    def gn_copy(row):
        there = pl.ds(row * piece, piece)
        return remote(swap.at[0, there], swap_in.at[0, there], row_send.at[row], row_recv.at[row], here.mate())

    def swap_copy(number):
        return remote(
            swap.at[number % 2], swap_in.at[number], swap_send.at[5 + number], swap_recv.at[5 + number], here.mate()
        )

    def out_store():
        return pltpu.make_async_copy(swap.at[1], out_ref, host_sem.at[8])

    def x_again(i):
        return pltpu.make_async_copy(x_in.at[:, pl.ds(i * HALF, HALF)], gat.at[i], host_sem.at[9 + i])

    def side_copy(number, source, target):
        return remote(source, target, side_send.at[number], side_recv.at[number], here.peer())

    def og_side(number, slot):
        return side_copy(number, og8.at[:, 1 - c, slot], og_peer.at[:, slot])

    def nt_side(number, slot):
        return side_copy(number, nt8.at[:, 1 - c, slot], nt_peer.at[:, slot])

    def no_side():
        return side_copy(4, no8.at[:, 1 - c], no_peer)

    def at_side():
        return side_copy(5, at8.at[:, 1 - c], at_peer)

    def gb_side():
        return side_copy(6, gb, gb_peer)

    def pair_side():
        return side_copy(7, nb.at[:, 1 - c], nb_peer)

    def out_copy(m):
        return remote(outs.at[m], outs_peer.at[m], out_send.at[m], out_recv.at[m], here.peer())

    def tri_copy(f, slot):
        return remote(
            tri.at[f, :, slot], tri_peer.at[f, :, slot], tri_send.at[f], tri_recv.at[f], here.peer()
        )

    def spread(value, target, slot):
        for i in range(8):
            target[i // 2, i % 2, slot] = value[:, i * PART : (i + 1) * PART]

    def joined(source, slot):
        return jnp.concatenate([source[i // 2, i % 2, slot] for i in range(8)], axis=1)

    def turned(own_part, peer_part, target):
        for level in range(4):
            rows = slice(level * PART, (level + 1) * PART)
            left, right = own_part(level), peer_part(level)
            target[rows, 0 : left.shape[0]] = low(wide(left).T)
            target[rows, left.shape[0] : 2 * left.shape[0]] = low(wide(right).T)

    def turned_slot(source, peer, target, slot):
        for level in range(4):
            rows = slice(level * PART, (level + 1) * PART)
            target[rows, lanes_at(slot * tokens, tokens)] = low(wide(source[level, c, slot]).T)
            target[rows, lanes_at((2 + slot) * tokens, tokens)] = low(wide(peer[level, slot]).T)

    og_fetches = [
        pltpu.make_async_copy(og_in.at[:, pl.ds(i * PART, PART)], og8.at[i // 2, i % 2, h], host_sem.at[i])
        for i in range(8)
    ]
    x_fetches = [
        pltpu.make_async_copy(x_in.at[:, pl.ds(i * HALF, HALF)], outs.at[0, i], host_sem.at[9 + i]) for i in range(2)
    ]
    for n in range(early):
        gather.begin(n, parts_of(n), whole_of(n), pack_of(n))
    gain_columns = [jnp.broadcast_to(wide(g[...])[None, :], (LANES // 2, rows)) for g in (one_in, two_in)]
    gather.slot(wn)[...] = low(jnp.concatenate(gain_columns, axis=0).T)
    for copy in og_fetches + x_fetches:
        copy.start()

    @pl.loop(0, tiles)
    def _(f):
        gather.begin(early + f, mlp_parts(f), wm.at[f], pack_m.at[f])

    skipped, begun = (PAD - WINDOW) // rows, PAD // rows
    nothing = jnp.zeros((4, skipped, rows, HALF), jnp.bfloat16)
    for ref in (k_ref, v_ref):
        ref[:, 0:skipped] = nothing

    @pl.when((c == 0) & (k == 0))
    def _():
        for ref in (k_ref, v_ref):
            ref[0:2, skipped:begun] = nothing[0:2]

    @pl.when((c == 1) & (k == 1))
    def _():
        edge_in[:, 1] = jnp.zeros((2, 2, WINDOW, HALF), jnp.bfloat16)

    greet(here.partners())

    steps(0, 0, 1, 2, 3)
    x_copy().start()
    steps(0, 4, 5, 6, 7)
    steps(1, 0, 1, 2, 3)
    steps(2, 0, 1, 2, 3)
    steps(1, 4, 5)
    steps(3, 0, 1, 2, 3)
    for copy in og_fetches:
        copy.wait()
    og_side(0, h).start()
    steps(4, 0)

    gain_rows = wide(flat(wn[...])).T
    gain[0:8, :] = jnp.broadcast_to(gain_rows[0:1, :], (8, gain_rows.shape[1]))
    gain[8:16, :] = jnp.broadcast_to(gain_rows[64:65, :], (8, gain_rows.shape[1]))

    def normed_of(value, row):
        factor = lax.rsqrt(jnp.mean(value * value, axis=-1, keepdims=True) + 1e-05)
        return low(value * factor * gain[row : row + 1, :])

    for copy in x_fetches:
        copy.wait()
    spread(normed_of(wide(jnp.concatenate([outs[0, 0], outs[0, 1]], axis=1)), 0), no8, h)
    x_copy().wait()
    spread(normed_of(wide(xm[...]), 0), no8, 1 - h)
    no_side().start()

    def projected(n, slot):
        return low(mm(joined(no8, slot), flat(wa[n])))

    steps(1, 6)
    for n, ref in ((0, k_ref), (1, v_ref)):
        steps(4, 1 + n)
        for slot in range(2):
            ref[2 * slot : 2 * slot + 2, begun:] = projected(n, slot).reshape(2, piece // rows, rows, HALF)

        @pl.when(c == 0)
        def _(n=n):
            halo(n, 0).start()

        @pl.when(c == 1)
        def _(n=n):
            halo(n, 1).start()

        @pl.when((c == 1) & (k == 0))
        def _(n=n):
            halo(n, 2).start()

        if n == 1:
            steps(0, 8, 9)
            steps(1, 7)
            steps(2, 4)

    steps(4, 3)
    for slot in range(2):
        q_ref[slot] = projected(2, slot)

    for n in range(2):

        @pl.when(c == 0)
        def _(n=n):
            halo(n, 0).wait_send()
            halo(n, 1).wait_recv()

        @pl.when(c == 1)
        def _(n=n):
            halo(n, 0).wait_recv()
            halo(n, 1).wait_send()

        @pl.when((c == 1) & (k == 0))
        def _(n=n):
            halo(n, 2).wait_send()

        @pl.when((c == 0) & (k == 1))
        def _(n=n):
            halo(n, 2).wait_recv()

    def mask_of(slot, row):
        first = (4 * k + 2 * slot + c) * piece
        query_pos = first + lax.broadcasted_iota(jnp.int32, (piece, PAD + piece), 0)
        key_pos = first - PAD + lax.broadcasted_iota(jnp.int32, (piece, PAD + piece), 1)
        start = jnp.zeros((piece, PAD + piece), jnp.int32)
        reached = 0
        for doc in range(lengths_ref.shape[1]):
            reached = reached + lengths_ref[row, doc]
            start = jnp.maximum(start, jnp.where(query_pos >= reached, reached, 0))
        return (key_pos >= start) & (key_pos <= query_pos) & (query_pos - key_pos < WINDOW)

    def attend(slot, row):
        allowed = mask_of(slot, row)
        span_rows = slice(row * piece, (row + 1) * piece)
        for head in range(HEADS // 2):
            cols = slice(head * HEAD_DIM, (head + 1) * HEAD_DIM)
            scores = nt_dot(q_ref[slot, span_rows, cols], flat(k_ref[2 * slot + row, :, :, cols])) * scale
            scores = jnp.where(allowed, scores, -1e30)
            exps = jnp.exp(scores - jnp.max(scores, axis=-1, keepdims=True))
            probs = exps / jnp.sum(exps, axis=-1, keepdims=True)
            p_ref[slot, row, head] = probs
            atb[slot, head // 2, head % 2, span_rows, :] = low(mm(low(probs), flat(v_ref[2 * slot + row, :, :, cols])))

    attend(1 - h, 0)
    attend(1 - h, 1)
    at_copy().start()
    steps(0, 10, 11, 12, 13, 14, 15, 16)
    steps(2, 5)
    steps(1, 8)
    attend(h, 0)
    attend(h, 1)
    at8[pl.ds(2 * h, 2)] = atb[h]
    steps(3, 4)
    steps(2, 6)
    steps(3, 5)
    steps(4, 4, 5)
    steps(1, 9)
    steps(2, 7)
    at_copy().wait()
    at_side().start()
    attended = jnp.concatenate([at8[i // 2, i % 2] for i in range(8)], axis=1)
    for n in range(2):
        cols = slice(n * HALF, (n + 1) * HALF)
        mid[:, cols] = wide(outs[0, n]) + mm(attended, flat(wo[n]))
    middle = mid[...]
    spread(normed_of(middle, 8), nt8, h)
    nt_copy(h).start()
    nt_side(2, h).start()
    og_copy(h).start()
    steps(1, 10, 11)
    steps(2, 8)
    steps(3, 6)
    steps(2, 9)
    steps(3, 7)
    acc[h] = middle
    acc[1 - h] = jnp.zeros(middle.shape, jnp.float32)
    gn[...] = jnp.zeros(gn.shape, jnp.float32)

    def feed(slot, *numbers):
        left, out_grad = joined(nt8, slot), joined(og8, slot)
        w_pairs = [flat(wm[f, :, :, :, :, :, 0 : 2 * PART]) for f in numbers]
        w_down = jnp.concatenate([flat(wm[f, :, :, :, :, :, 2 * PART : 3 * PART]) for f in numbers], axis=1)
        grads_hidden = mm(out_grad, w_down)
        hidden_acts, grads = [], []
        for i, f in enumerate(numbers):
            both = mm(left, w_pairs[i])
            gates, ups = both[:, 0:PART], both[:, PART:]
            grad_hidden = grads_hidden[:, i * PART : (i + 1) * PART]
            sigmoid = 1.0 / (1.0 + jnp.exp(-gates))
            silu = gates * sigmoid
            hidden = low(silu * ups)
            grad_gates = low(grad_hidden * ups * sigmoid * (1.0 + gates * (1.0 - sigmoid)))
            grad_ups = low(grad_hidden * silu)
            tri[f, 0, slot] = grad_gates
            tri[f, 1, slot] = grad_ups
            tri[f, 2, slot] = hidden
            tri_copy(f, slot).start()
            hidden_acts.append(hidden)
            grads += [grad_gates, grad_ups]
        acc[slot] += nt_dot(jnp.concatenate(hidden_acts, axis=1), w_down)
        gn[slot] += nt_dot(jnp.concatenate(grads, axis=1), jnp.concatenate(w_pairs, axis=1))

    og_side(0, h).wait()
    turned_slot(og8, og_peer, og_t, h)
    nt_side(2, h).wait()
    turned_slot(nt8, nt_peer, nt_t, h)
    n_tokens = 2 * tokens

    def ff_grads(f):
        remote(tri.at[f], tri_peer.at[f], tri_send.at[f], tri_recv.at[f], here.peer()).wait()
        pair = mm(nt_t[:, 0:n_tokens], jnp.concatenate([flat(tri[f, 0]), flat(tri[f, 1])], axis=1)) + mm(
            nt_t[:, n_tokens:], jnp.concatenate([flat(tri_peer[f, 0]), flat(tri_peer[f, 1])], axis=1)
        )
        down = mm(og_t[:, 0:n_tokens], flat(tri[f, 2])) + mm(og_t[:, n_tokens:], flat(tri_peer[f, 2]))
        wm[f, :, 0, :, :, :, 0 : 2 * PART] = low(pair).reshape(4, 2, 2, -1, 2 * PART)
        wm[f, :, 0, :, :, :, 2 * PART : 3 * PART] = low(down).reshape(4, 2, 2, -1, PART)

    chunks = tiles + 6

    def chunk(n):
        if n < tiles:
            return wm.at[n, :, 0], mlp_twos.at[n], mlp_ends.at[n]
        n -= tiles
        if n < 2:
            return k_ref.at[:, pl.ds(4 * n, 4)], mgo_twos.at[n], mgo_ends.at[n]
        if n < 5:
            source = mga if n == 2 else v_ref.at[:, pl.ds(4 * (n - 3), 4)]
            return source, mga_twos.at[n - 2], mga_ends.at[n - 2]
        return nb_sum, nb_twos, nb_ends

    def store_tile(n, mine, others):
        back, across, on = others
        for half, value in ((h, mine + across), (1 - h, back + on)):
            for i, ref in enumerate((og_out, ou_out, od_out)):
                ref[:, lanes_at(half * span + n * PART, PART)] = value[:, i * PART : (i + 1) * PART]

    def store(n, mine, others):
        if n < tiles:
            store_tile(n, mine, others)
            return
        back, across, on = others
        n -= tiles
        if 2 <= n < 5:
            for half, value in ((h, mine + across), (1 - h, back + on)):
                (oq_ref, ok_ref, ov_ref)[n - 2][:, lanes_at(half * HALF, HALF)] = value
            return
        value = mine + back + across + on
        if n < 2:
            oo_ref[:, n * HALF : (n + 1) * HALF] = value
        else:
            on_ref[...] = value

    def sum_tick(t):
        for stage, lag in enumerate(SUM_LAGS):
            n = t - lag
            if not 0 <= n < chunks:
                continue
            source, twos, ends = chunk(n)
            if stage == 0:
                scatter.second(n, source, twos)
            elif stage == 1:
                scatter.third(n, source, twos, ends)
            else:
                store(n, *scatter.fourth(n, source, ends))

    def launch_tile(f):
        scatter.first(f, wm.at[f, :, 0], mlp_twos.at[f])

    def launch(n):
        source, twos, _ = chunk(n)
        scatter.first(n, source, twos)

    @pl.loop(0, FIRST_TILES)
    def _(f):
        tile_steps(f)
        gather.fifth(early + f, wm.at[f])
        feed(h, f)

    og_copy(1 - h).wait()
    og_side(1, 1 - h).start()
    nt_copy(1 - h).wait()
    nt_side(3, 1 - h).start()

    @pl.loop(0, FIRST_TILES // 2)
    def _(i):
        for f in (FIRST_TILES + 2 * i, FIRST_TILES + 2 * i + 1):

            @pl.when(f < tiles)
            def _(f=f):
                tile_steps(f)

        feed(1 - h, 2 * i, 2 * i + 1)

    feed(1 - h, FIRST_TILES - 1)

    @pl.loop(0, (tiles - FIRST_TILES) // 2)
    def _(i):
        f = FIRST_TILES + 2 * i
        for tile in (f, f + 1):
            gather.fifth(early + tile, wm.at[tile])

        @pl.loop(0, 2)
        def _(slot):
            feed(slot, f, f + 1)

    for row in range(2):
        there = slice(row * piece, (row + 1) * piece)
        swap[0, there, :] = low(gn[1 - h, there, :])
        gn_copy(row).start()
    og_side(1, 1 - h).wait()
    turned_slot(og8, og_peer, og_t, 1 - h)
    nt_side(3, 1 - h).wait()
    turned_slot(nt8, nt_peer, nt_t, 1 - h)

    @pl.loop(0, tiles)
    def _(f):
        ff_grads(f)
        launch_tile(f)


    def close_middle(row):
        gn_copy(row).wait()
        there = slice(row * piece, (row + 1) * piece)
        middle = mid[there, :]
        factor = lax.rsqrt(jnp.mean(middle * middle, axis=-1, keepdims=True) + 1e-05)
        grad_normed = gn[h, there, :] + wide(swap_in[0, there, :])
        through = grad_normed * gain[8:9, :]
        shift = jnp.mean(through * middle, axis=-1, keepdims=True) * factor * factor * factor
        out_grad = jnp.concatenate([og8[i // 2, i % 2, h, there, :] for i in range(8)], axis=1)
        grad_middle = wide(out_grad) + factor * through - middle * shift
        gi_ref[there, :] = grad_middle
        gb[there, :] = low(grad_middle)
        return jnp.sum(grad_normed * middle * factor, axis=0, keepdims=True)

    def to_attended(row):
        there = slice(row * piece, (row + 1) * piece)

        def part(half):
            rows = pl.ds(2 * half, 2)
            return low(
                nt_dot(gb[there, 0:HALF], flat(wo[0, rows])) + nt_dot(gb[there, HALF:], flat(wo[1, rows]))
            )

        swap[0, there, 0:HALF] = part(1 - h)
        ga_copy(row).start()
        gat[h, there, :] = part(h)

    def send_out(ones):
        gb_side().start()
        swap[1] = low(acc[1 - h])
        swap_copy(1).start()
        gain[8:16, :] = jnp.broadcast_to(ones[0] + ones[1], (8, gain.shape[1]))

    def keep_out():
        mid[...] = acc[h]

    def close_out():
        swap_copy(1).wait()
        swap[1] = low(mid[...] + wide(swap_in[1]))
        out_store().start()

    def attend_back(slot, row):
        span_rows = slice(row * piece, (row + 1) * piece)
        for head in range(HEADS // 2):
            cols = slice(head * HEAD_DIM, (head + 1) * HEAD_DIM)
            there = slice(row * HALF + head * HEAD_DIM, row * HALF + (head + 1) * HEAD_DIM)
            grad = gat[slot, span_rows, cols]
            probs = p_ref[slot, row, head]
            gn[slot, :, there] = tn_dot(low(probs), grad)
            grad_probs = nt_dot(grad, flat(v_ref[2 * slot + row, :, :, cols]))
            inner = jnp.sum(grad_probs * probs, axis=-1, keepdims=True)
            grad_scores = low(probs * (grad_probs - inner))
            outs[2, slot, span_rows, cols] = low(mm(grad_scores, flat(k_ref[2 * slot + row, :, :, cols])) * scale)
            acc[slot, :, there] = tn_dot(grad_scores, q_ref[slot, span_rows, cols]) * scale
        there = slice(row * HALF, (row + 1) * HALF)
        edge[0, slot, row] = low(acc[slot, PAD - WINDOW : PAD, there])
        edge[1, slot, row] = low(gn[slot, PAD - WINDOW : PAD, there])

    def send_edge():
        out_copy(2).start()

        @pl.when(c == 1)
        def _():
            edge_copy(0).start()

        @pl.when(c == 0)
        def _():
            edge_copy(1).start()

        @pl.when((c == 0) & (k == 1))
        def _():
            edge_copy(2).start()

    def close_edge():
        @pl.when(c == 1)
        def _():
            edge_copy(0).wait_send()
            edge_copy(1).wait_recv()

        @pl.when(c == 0)
        def _():
            edge_copy(0).wait_recv()
            edge_copy(1).wait_send()

        @pl.when((c == 0) & (k == 1))
        def _():
            edge_copy(2).wait_send()

        @pl.when((c == 1) & (k == 0))
        def _():
            edge_copy(2).wait_recv()

        inside = piece - WINDOW
        for m, source in ((0, acc), (1, gn)):
            for slot in range(2):
                for row in range(2):
                    there = slice(row * HALF, (row + 1) * HALF)
                    first = row * piece
                    outs[m, slot, first : first + inside, :] = low(source[slot, PAD : PAD + inside, there])
                    outs[m, slot, first + inside : first + piece, :] = low(
                        source[slot, PAD + inside : PAD + piece, there] + wide(edge_in[m, slot, row])
                    )
            out_copy(m).start()

    def to_input(slot):
        grad = nt_dot(outs[0, slot], flat(wa[0]))
        for m in (1, 2):
            grad = grad + nt_dot(outs[m, slot], flat(wa[m]))
        return grad

    def inverse_rms(value):
        return lax.rsqrt(jnp.mean(value * value, axis=-1, keepdims=True) + 1e-05)

    def send_input():
        part = to_input(1 - h)
        swap[0] = low(part)
        swap_copy(2).start()
        x = wide(xm[...])
        return jnp.sum(part * x * inverse_rms(x), axis=0, keepdims=True)

    def send_norm(one):
        part = to_input(h)
        acc[0] = part
        for i in range(2):
            x_again(i).wait()
        x = wide(jnp.concatenate([gat[0], gat[1]], axis=1))
        one = one + jnp.sum(part * x * inverse_rms(x), axis=0, keepdims=True)
        width = one.shape[1]
        stacked = jnp.concatenate(
            [
                jnp.broadcast_to(one, (LANES // 2, width)),
                jnp.broadcast_to(gain[8:9, :], (LANES // 2, width)),
            ],
            axis=0,
        )
        nb[...] = low(stacked.T).reshape(nb.shape)
        pair_side().start()

    def close_input():
        swap_copy(2).wait()
        grad_normed = acc[0] + wide(swap_in[2])
        x = wide(jnp.concatenate([gat[0], gat[1]], axis=1))
        factor = inverse_rms(x)
        through = grad_normed * gain[0:1, :]
        shift = jnp.mean(through * x, axis=-1, keepdims=True) * factor * factor * factor
        gi_ref[...] += factor * through - x * shift

    def close_norm():
        pair_side().wait()
        nb_sum[...] = low(wide(nb[:, c]) + wide(nb_peer[...]))

    def turn_normed():
        no_side().wait()
        turned(lambda i: flat(no8[i, c]), lambda i: flat(no_peer[i]), no_t)

    def wout_grads():
        at_side().wait()
        turned(lambda i: at8[i, c], lambda i: at_peer[i], og_t)
        gb_side().wait()
        for n in range(2):
            cols = slice(n * HALF, (n + 1) * HALF)
            grad = mm(og_t[:, 0:tokens], gb[:, cols]) + mm(og_t[:, tokens : 2 * tokens], gb_peer[:, cols])
            k_ref[:, 4 * n : 4 * n + 4] = low(grad).reshape(4, 4, -1, HALF)

    def attn_grads(m):
        out_copy(m).wait()
        grad = mm(no_t[:, 0:n_tokens], flat(outs[m])) + mm(no_t[:, n_tokens:], flat(outs_peer[m]))
        if m == 2:
            mga[...] = low(grad).reshape(mga.shape)
        else:
            v_ref[:, 4 * m : 4 * m + 4] = low(grad).reshape(4, 4, -1, HALF)

    def ticks(first, last):
        for t in range(first, last):
            sum_tick(t)

    ticks(0, 2)
    ones = []
    for row in range(2):
        ones.append(close_middle(row))
        to_attended(row)
    send_out(ones)
    keep_out()
    ticks(2, 4)
    attend_back(h, 0)
    attend_back(h, 1)
    for row in range(2):
        ga_copy(row).wait()
        attend_back(1 - h, row)
    send_edge()
    for i in range(2):
        x_again(i).start()
    turn_normed()
    wout_grads()
    launch(tiles)
    launch(tiles + 1)
    attn_grads(2)
    launch(tiles + 2)
    ticks(4, 7)
    close_edge()
    one = send_input()
    for m in range(2):
        attn_grads(m)
        launch(tiles + 3 + m)
    send_norm(one)
    ticks(7, 9)
    close_norm()
    launch(tiles + 5)
    ticks(9, 11)
    close_out()
    ticks(11, 14)
    close_input()
    stores = [
        pltpu.make_async_copy(source, target, host_sem.at[12 + i])
        for i, (source, target) in enumerate(
            zip(
                (gi_ref, og_out, ou_out, od_out, oo_ref, oq_ref, ok_ref, ov_ref, on_ref),
                (gi_to, og_to, ou_to, od_to, oo_to, oq_to, ok_to, ov_to, on_to),
            )
        )
    ]
    stores[0].start()
    ticks(14, tiles + SUM_LAGS[-1])
    for store_out in stores[1:4]:
        store_out.start()
    ticks(tiles + SUM_LAGS[-1], tiles + SUM_LAGS[-1] + 2)
    stores[4].start()
    ticks(tiles + SUM_LAGS[-1] + 2, chunks + SUM_LAGS[-1])
    for store_out in stores[5:]:
        store_out.start()
    out_store().wait()
    for store_out in stores:
        store_out.wait()


def deliver_kernel(count, *refs):
    sources, targets, refs = refs[:count], refs[count : 2 * count + 1], refs[2 * count + 1 :]
    held, vectors, (in_sem, out_sem) = refs[:count], refs[count : count + 2], refs[count + 2 :]
    ins = [pltpu.make_async_copy(s, v, in_sem.at[i]) for i, (s, v) in enumerate(zip(sources, held))]
    leave = (*vectors, *held[1:])
    outs = [pltpu.make_async_copy(v, t, out_sem.at[i]) for i, (v, t) in enumerate(zip(leave, targets))]
    for copy in ins:
        copy.start()
    ins[0].wait()
    turned = held[0][...].T
    for i in range(2):
        vectors[i][...] = turned[i * LANES // 2, :]
        outs[i].start()
    for arrived, leaving in zip(ins[1:], outs[2:]):
        arrived.wait()
        leaving.start()
    for copy in outs:
        copy.wait()


def delivered(norms, arrays):
    anywhere = pl.BlockSpec(memory_space=pl.ANY)
    count = len(arrays) + 1
    vector = (norms.shape[:1], norms.dtype)
    return pl.pallas_call(
        functools.partial(deliver_kernel, count),
        out_shape=[jax.ShapeDtypeStruct(*vector)] * 2 + [jax.ShapeDtypeStruct(a.shape, a.dtype) for a in arrays],
        in_specs=[anywhere] * count,
        out_specs=[anywhere] * (count + 1),
        scratch_shapes=[pltpu.VMEM(a.shape, a.dtype) for a in (norms, *arrays)]
        + [pltpu.VMEM(*vector)] * 2
        + [pltpu.SemaphoreType.DMA((count,)), pltpu.SemaphoreType.DMA((count + 1,))],
        compiler_params=pltpu.CompilerParams(vmem_limit_bytes=60 * 2**20),
        name="deliver",
    )(norms, *arrays)


def fused(hidden_in, lengths, out_grad, gain_shards, weight_shards):
    hidden = hidden_in.reshape(-1, hidden_in.shape[-1])
    tokens, width = hidden.shape
    rows = weight_shards[0].shape[0]
    tiles = weight_shards[4].shape[1] // (2 * PART)
    bf, fl = jnp.bfloat16, jnp.float32
    every, mine = (4, 2, 2, 2, rows), (4, 2, 2, rows)
    part = 3 * PART
    dma = pltpu.SemaphoreType.DMA
    vmem, anywhere = pl.BlockSpec(memory_space=pltpu.VMEM), pl.BlockSpec(memory_space=pl.ANY)
    shape = jax.ShapeDtypeStruct
    piece = tokens // 2
    keys = (4, (PAD + piece) // rows, rows, HALF)
    scratch = [
        ((*every, LANES), bf), ((3, *every, HALF), bf), ((2, *every, HALF), bf), ((tiles, *every, part), bf),
        ((3, rows, HALF), bf), ((tiles, rows, part), bf), ((tokens, width), bf),
        *[((4, 2, 2, tokens, PART), bf)] * 3, ((4, 2, tokens, PART), bf), ((2, 2, 2, tokens, PART), bf),
        *[((4, 2, tokens, PART), bf)] * 3, ((4, tokens, PART), bf),
        *[((width // 2, 4 * tokens), bf)] * 2,
        ((2, tokens, HALF), bf), (keys, bf), (keys, bf), ((2, 2, HEADS // 2, piece, PAD + piece), fl),
        ((tokens, width), fl), ((2, tokens, width), fl), ((2, tokens, width), fl),
        ((16, width), fl), ((tiles, 3, 2, tokens, PART), bf), ((tiles, 3, 2, tokens, PART), bf),
        ((2, tokens, width), bf), ((3, tokens, width), bf), ((2, tokens, HALF), bf),
        ((2, 2, 2, WINDOW, HALF), bf), ((2, 2, 2, WINDOW, HALF), bf),
        ((3, 2, tokens, HALF), bf), ((3, 2, tokens, HALF), bf), ((tokens, width), bf), ((tokens, width), bf),
        ((*mine, HALF), bf),
        ((*mine, LANES), bf), ((*mine, LANES), bf),
        ((tiles, 3, 4, rows, part), bf), ((tiles, 3, rows, part), bf),
        ((3, 3, 4, rows, HALF), bf), ((3, 3, rows, HALF), bf),
        ((2, 3, 4, rows, HALF), bf), ((2, 3, rows, HALF), bf),
        ((3, 4, rows, LANES), bf), ((3, rows, LANES), bf),
    ]
    count, chunks = 6 + tiles, 6 + tiles
    sums = [((tokens, width), fl)] + [((rows, width), fl)] * 4
    sums += [((rows, 2 * tiles * PART), fl)] * 3 + [((rows, LANES), fl)]
    results = pl.pallas_call(
        layer_kernel,
        out_shape=[shape((tokens, width), bf)] + [shape(*s) for s in sums],
        in_specs=[anywhere, anywhere, pl.BlockSpec(memory_space=pltpu.SMEM), vmem, vmem] + [anywhere] * 7,
        out_specs=[anywhere] * 10,
        scratch_shapes=[pltpu.VMEM(*s) for s in sums + scratch]
        + [
            dma((count, 2)), dma((count, 4)), dma((count, 4)), dma((chunks, 4)), dma((chunks, 4)),
            dma((2, 2)), dma((2, 2)), dma((2,)), dma((2,)), dma((8,)), dma((8,)),
            dma((tiles,)), dma((tiles,)), dma((8,)), dma((8,)), dma((3,)), dma((3,)), dma((21,)), dma((4,)), dma((4,)),
        ],
        compiler_params=pltpu.CompilerParams(
            collective_id=0, has_side_effects=True, vmem_limit_bytes=63 * 2**20
        ),
        name="layer",
    )(hidden, out_grad.reshape(hidden.shape), lengths, *gain_shards, *weight_shards)
    one, two, block_out, grad_in, query, key, value, wout, gate, up, down = delivered(results[9], results[:9])
    return (
        block_out.reshape(hidden_in.shape), grad_in.reshape(hidden_in.shape),
        one, query, key, value, wout, two, gate, up, down,
    )


def layer(hidden_in, lengths, out_grad, gains, weights):
    score_scale = 1.0 / math.sqrt(HEAD_DIM)
    tokens = hidden_in.shape[1]
    gain_one, gain_two = gains
    w_query, w_key, w_value, w_out, w_gate, w_up, w_down = weights
    inputs = hidden_in.astype(jnp.float32)
    normed_one = rms_scale(inputs, gain_one).astype(jnp.bfloat16)
    queries = project(normed_one, w_query).astype(jnp.bfloat16)
    keys = project(normed_one, w_key).astype(jnp.bfloat16)
    values = project(normed_one, w_value).astype(jnp.bfloat16)
    tails = jnp.stack([keys[:, tokens - WINDOW :], values[:, tokens - WINDOW :]])
    received = passed_along(tails, "seq", 1)
    keys_all = jnp.concatenate([received[0], keys], axis=1)
    values_all = jnp.concatenate([received[1], values], axis=1)
    allowed = window_mask(lengths, lax.axis_index("seq"), tokens)
    scores = scores_of(queries, keys_all, allowed)
    top = jnp.max(scores, axis=-1, keepdims=True)
    exps = jnp.exp(scores - top)
    probs = exps / jnp.sum(exps, axis=-1, keepdims=True)
    probs_low = probs.astype(jnp.bfloat16)
    mixed = jnp.einsum(
        "rhqk,rkhd->rqhd", probs_low, split_heads(values_all), preferred_element_type=jnp.float32
    )
    attended = merge_heads(mixed).astype(jnp.bfloat16)
    middle = inputs + project(attended, w_out)
    normed_two = rms_scale(middle, gain_two).astype(jnp.bfloat16)
    gates = project(normed_two, w_gate)
    ups = project(normed_two, w_up)
    hidden_act = swiglu(gates, ups).astype(jnp.bfloat16)
    block_out = (middle + project_back(hidden_act, w_down)).astype(jnp.bfloat16)
    grad_hidden = project(out_grad, w_down)
    unused, swiglu_back = jax.vjp(swiglu, gates, ups)
    grad_gates, grad_ups = swiglu_back(grad_hidden)
    grad_gates = grad_gates.astype(jnp.bfloat16)
    grad_ups = grad_ups.astype(jnp.bfloat16)
    grad_down = weight_grad(out_grad, hidden_act)
    grad_gate = weight_grad(normed_two, grad_gates)
    grad_up = weight_grad(normed_two, grad_ups)
    grad_normed_two = project_back(grad_gates, w_gate) + project_back(grad_ups, w_up)
    unused, norm_two_back = jax.vjp(rms_scale, middle, gain_two)
    grad_middle_part, grad_norm2 = norm_two_back(grad_normed_two)
    grad_middle = out_grad.astype(jnp.float32) + grad_middle_part
    grad_branch = grad_middle.astype(jnp.bfloat16)
    grad_wout = weight_grad(attended, grad_branch)
    grad_attended = project_back(grad_branch, w_out).astype(jnp.bfloat16)
    grad_heads = split_heads(grad_attended)
    grad_values_all = jnp.einsum(
        "rhqk,rqhd->rkhd", probs_low, grad_heads, preferred_element_type=jnp.float32
    )
    grad_probs = jnp.einsum(
        "rqhd,rkhd->rhqk", grad_heads, split_heads(values_all), preferred_element_type=jnp.float32
    )
    grad_scores = (
        probs * (grad_probs - jnp.sum(grad_probs * probs, axis=-1, keepdims=True))
    ).astype(jnp.bfloat16)
    grad_queries = score_scale * merge_heads(
        jnp.einsum(
            "rhqk,rkhd->rqhd", grad_scores, split_heads(keys_all),
            preferred_element_type=jnp.float32,
        )
    )
    grad_keys_all = score_scale * merge_heads(
        jnp.einsum(
            "rhqk,rqhd->rkhd", grad_scores, split_heads(queries),
            preferred_element_type=jnp.float32,
        )
    )
    grad_values_all = merge_heads(grad_values_all)
    halo_grads = jnp.stack([grad_keys_all[:, :WINDOW], grad_values_all[:, :WINDOW]])
    returned = passed_along(halo_grads.astype(jnp.bfloat16), "seq", -1).astype(halo_grads.dtype)
    grad_keys = (
        grad_keys_all[:, WINDOW:].at[:, tokens - WINDOW :].add(returned[0]).astype(jnp.bfloat16)
    )
    grad_values = (
        grad_values_all[:, WINDOW:].at[:, tokens - WINDOW :].add(returned[1]).astype(jnp.bfloat16)
    )
    grad_queries = grad_queries.astype(jnp.bfloat16)
    grad_query = weight_grad(normed_one, grad_queries)
    grad_key = weight_grad(normed_one, grad_keys)
    grad_value = weight_grad(normed_one, grad_values)
    grad_normed_one = (
        project_back(grad_queries, w_query)
        + project_back(grad_keys, w_key)
        + project_back(grad_values, w_value)
    )
    unused, norm_one_back = jax.vjp(rms_scale, inputs, gain_one)
    grad_inputs_part, grad_norm1 = norm_one_back(grad_normed_one)
    grad_in = grad_middle + grad_inputs_part
    grads = (grad_query, grad_key, grad_value, grad_wout, grad_gate, grad_up, grad_down)
    return block_out, grad_in, (grad_norm1, grad_norm2), grads


def shards(
    hidden_in, lengths, norm1_gain, w_query, w_key, w_value, w_out,
    norm2_gain, w_gate, w_up, w_down, out_grad,
):
    gain_shards = (norm1_gain, norm2_gain)
    weight_shards = (w_query, w_key, w_value, w_out, w_gate, w_up, w_down)
    if (lax.axis_size("seq"), lax.axis_size("rows")) == (SEQ_PIECES, ROW_GROUPS):
        return fused(hidden_in, lengths, out_grad, gain_shards, weight_shards)
    gains = [g.astype(jnp.float32) for g in gathered_by_xla(gain_shards)]
    weights = gathered_by_xla(weight_shards)
    block_out, grad_in, norms, grads = layer(hidden_in, lengths, out_grad, gains, weights)
    norms, grads = scattered_by_xla(norms), scattered_by_xla(grads)
    return (
        block_out, grad_in, norms[0], grads[0], grads[1], grads[2], grads[3],
        norms[1], grads[4], grads[5], grads[6],
    )


def solution(mesh):
    tokens = P("rows", "seq", None)
    vector = P(("seq", "rows"))
    matrix = P(("seq", "rows"), None)
    in_specs = (
        tokens, P("rows", None), vector, matrix, matrix, matrix, matrix,
        vector, matrix, matrix, matrix, tokens,
    )
    out_specs = (
        tokens, tokens, vector, matrix, matrix, matrix, matrix,
        vector, matrix, matrix, matrix,
    )
    return jax.shard_map(shards, mesh=mesh, in_specs=in_specs, out_specs=out_specs, check_vma=False)
```

```python
import functools
import math

import jax
import jax.numpy as jnp
from jax import lax
from jax.experimental import pallas as pl
from jax.experimental.pallas import tpu as pltpu
from jax.sharding import PartitionSpec as P

HEADS = 8
HEAD_DIM = 128
WINDOW = 64
LANES = 128
MESH = pl.DeviceIdType.MESH


def passed_along(block, axis, distance):
    devices = range(lax.axis_size(axis))
    route = [(i - distance, i) for i in devices if i - distance in devices]
    return lax.ppermute(block, axis, route)


def rms_scale(values, gain):
    factor = lax.rsqrt(jnp.mean(values * values, axis=-1, keepdims=True) + 1e-05)
    return values * factor * gain


def swiglu(gates, ups):
    return jax.nn.silu(gates) * ups


def project(left, weight):
    return jnp.dot(left, weight, preferred_element_type=jnp.float32)


def project_back(grad, weight):
    return lax.dot_general(
        grad, weight, (((2,), (1,)), ((), ())), preferred_element_type=jnp.float32
    )


def weight_grad(left, grad):
    return jnp.einsum("rtd,rtf->df", left, grad, preferred_element_type=jnp.float32)


def split_heads(values):
    return values.reshape(values.shape[0], values.shape[1], HEADS, HEAD_DIM)


def merge_heads(values):
    return values.reshape(values.shape[0], values.shape[1], HEADS * HEAD_DIM)


def window_mask(lengths, seq_index, tokens):
    docs = lengths.shape[1]
    upto = jnp.arange(docs)[:, None] >= jnp.arange(docs)[None, :]
    ends = jnp.sum(jnp.where(upto[None], lengths[:, None, :], 0), axis=2)
    query_pos = seq_index * tokens + jnp.arange(tokens, dtype=jnp.int32)
    key_pos = seq_index * tokens - WINDOW + jnp.arange(tokens + WINDOW, dtype=jnp.int32)
    starts = jnp.max(
        jnp.where(
            ends[:, None, :] <= query_pos[None, :, None],
            ends[:, None, :],
            jnp.zeros_like(ends[:, None, :]),
        ),
        axis=2,
    )
    allowed = (
        (key_pos[None, None, :] >= starts[:, :, None])
        & (key_pos[None, None, :] <= query_pos[None, :, None])
        & (query_pos[None, :, None] - key_pos[None, None, :] < WINDOW)
    )
    return allowed[:, None]


def scores_of(queries, keys_all, allowed):
    score_scale = 1.0 / math.sqrt(HEAD_DIM)
    scores = (
        jnp.einsum(
            "rqhd,rkhd->rhqk",
            split_heads(queries),
            split_heads(keys_all),
            preferred_element_type=jnp.float32,
        )
        * score_scale
    )
    return jnp.where(allowed, scores, -1e30)


def gathered_by_xla(shards):
    return [lax.all_gather(s, ("seq", "rows"), axis=0, tiled=True) for s in shards]


def scattered_by_xla(totals):
    return [
        lax.psum_scatter(t.astype(jnp.float32), ("seq", "rows"), scatter_dimension=0, tiled=True)
        for t in totals
    ]


SEQ_PIECES = 8
ROW_GROUPS = 4
PART = 128
HALF = 512
PAD = 128
AHEAD = (11, 6, 4, 2)
FIRST_TILES = 9
SUM_LAGS = (0, 4, 8)


class Place:
    def __init__(self):
        seq, rows = lax.axis_index("seq"), lax.axis_index("rows")
        self.z, self.c = seq // 2, seq % 2
        self.k, self.h = self.z // 2, self.z % 2
        self.y, self.x = rows // 2, rows % 2
        self.turn_y, self.turn_x = 1 - 2 * self.y, 1 - 2 * self.x

    def column(self, near, far):
        y, x, c = self.y, self.x, self.c
        if near:
            y, x = y + c * self.turn_y, x + (1 - c) * self.turn_x
        if far:
            y, x = y + (1 - c) * self.turn_y, x + c * self.turn_x
        return y, x

    def device(self, z, c, column):
        return (2 * z + c, 2 * column[0] + column[1])

    def near(self):
        return self.device(self.z, self.c, self.column(True, False))

    def far(self):
        return self.device(self.z, self.c, self.column(False, True))

    def peer(self):
        return self.device(self.z, 1 - self.c, (self.y, self.x))

    def mate(self):
        return self.device(2 * self.k + 1 - self.h, self.c, (self.y, self.x))

    def across(self):
        return self.device(2 * (1 - self.k) + self.h, self.c, (self.y, self.x))

    def cross(self):
        return self.device(2 * (1 - self.k) + self.h, 1 - self.c, (self.y, self.x))

    def along_z(self, step):
        return self.device((self.z + step) % 4, self.c, (self.y, self.x))

    def partners(self):
        return [self.near(), self.far(), self.peer(), self.cross()] + [self.along_z(i) for i in (1, 2, 3)]


def greet(partners):
    barrier = pltpu.get_barrier_semaphore()
    for partner in partners:
        pl.semaphore_signal(barrier, inc=1, device_id=partner, device_id_type=MESH)
    pl.semaphore_wait(barrier, len(partners))


def remote(source, target, send, recv, device):
    return pltpu.make_async_remote_copy(
        src_ref=source, dst_ref=target, send_sem=send, recv_sem=recv,
        device_id=device, device_id_type=MESH,
    )


def nt_dot(left, right):
    return lax.dot_general(left, right, (((1,), (1,)), ((), ())), preferred_element_type=jnp.float32)


def tn_dot(left, right):
    return lax.dot_general(left, right, (((0,), (0,)), ((), ())), preferred_element_type=jnp.float32)


def mm(left, right):
    return jnp.dot(left, right, preferred_element_type=jnp.float32)


def flat(value):
    return value.reshape(-1, value.shape[-1])


def low(value):
    return value.astype(jnp.bfloat16)


def wide(value):
    return value.astype(jnp.float32)


def lanes_at(first, width):
    return pl.ds(pl.multiple_of(first, PART), width)


class Gather:
    def __init__(self, here, own_sem, send, recv):
        self.here, self.own_sem, self.send, self.recv = here, own_sem, send, recv
        self.own, self.near = here.column(False, False), here.column(True, False)
        self.far, self.both = here.column(False, True), here.column(True, True)

    def slot(self, whole):
        return whole.at[self.here.z, self.here.c, self.own[0], self.own[1]]

    def block(self, whole, core, column):
        return whole.at[:, core, column[0], column[1]]

    def copy(self, n, number, source, target, device):
        return remote(source, target, self.send.at[n, number], self.recv.at[n, number], device)

    def wait(self, n, number, view, device):
        self.copy(n, number, view, view, device).wait()

    def begin(self, n, parts, whole, pack):
        slot = self.slot(whole)
        for kept, given, first, width in parts:
            pltpu.make_async_copy(kept, slot.at[:, pl.ds(first, width)], self.own_sem.at[n, 0]).start()
            if pack is not None:
                pltpu.make_async_copy(given, pack.at[:, pl.ds(first, width)], self.own_sem.at[n, 1]).start()

    def first(self, n, whole, pack, fetched=True):
        slot = self.slot(whole)
        if fetched:
            pltpu.make_async_copy(slot, slot, self.own_sem.at[n, 0]).wait()
        if pack is not None:
            pltpu.make_async_copy(pack, pack, self.own_sem.at[n, 1]).wait()
        for step in (1, 2, 3):
            source = slot if pack is None or step == 2 else pack
            self.copy(n, 0, source, slot, self.here.along_z(step)).start()

    def second(self, n, whole):
        here = self.here
        self.wait(n, 0, whole.at[pl.ds(0, 3), here.c, self.own[0], self.own[1]], here.along_z(1))
        block = self.block(whole, here.c, self.own)
        self.copy(n, 1, block, block, here.near()).start()
        self.copy(n, 2, block, block, here.far()).start()
        self.copy(n, 3, block, block, here.peer()).start()

    def third(self, n, whole):
        here = self.here
        block = self.block(whole, here.c, self.near)
        self.wait(n, 1, block, here.near())
        self.copy(n, 2, block, block, here.far()).start()
        self.copy(n, 3, block, block, here.peer()).start()

    def fourth(self, n, whole):
        here = self.here
        self.wait(n, 2, whole.at[:, here.c, 0], here.far())
        for column in (self.far, self.both):
            block = self.block(whole, here.c, column)
            self.copy(n, 3, block, block, here.peer()).start()

    def fifth(self, n, whole):
        self.wait(n, 3, whole.at[:, 1 - self.here.c], self.here.peer())


class Scatter:
    def __init__(self, here, send, recv):
        self.here, self.send, self.recv = here, send, recv
        self.own, self.near = here.column(False, False), here.column(True, False)
        self.far, self.both = here.column(False, True), here.column(True, True)

    def copy(self, n, number, source, target, device):
        return remote(source, target, self.send.at[n, number], self.recv.at[n, number], device)

    def view(self, source, column):
        if len(source.shape) == 5:
            return source.at[:, column[0], column[1]]
        return source.at[:, 2 * column[0] + column[1]]

    def to_far(self, n, source, twos):
        return [
            self.copy(n, i, self.view(source, column), twos.at[i], self.here.far())
            for i, column in enumerate((self.both, self.far))
        ]

    def to_near(self, n, source, twos):
        return self.copy(n, 2, self.view(source, self.near), twos.at[2], self.here.near())

    def first(self, n, source, twos):
        for copy in self.to_far(n, source, twos):
            copy.start()

    def add(self, target, other):
        @pl.loop(0, 4)
        def _(level):
            target[level] = low(wide(target[level]) + wide(other[level]))

    def second(self, n, source, twos):
        both, far = self.to_far(n, source, twos)
        both.wait()
        self.add(self.view(source, self.near), twos.at[0])
        self.to_near(n, source, twos).start()
        far.wait()
        self.add(self.view(source, self.own), twos.at[1])

    def third(self, n, source, twos, ends):
        self.to_near(n, source, twos).wait()
        own = self.view(source, self.own)
        self.add(own, twos.at[2])
        for step in (1, 2, 3):
            block = own.at[(self.here.z + step) % 4]
            self.copy(n, 3, block, ends.at[step - 1], self.here.along_z(step)).start()

    def fourth(self, n, source, ends):
        self.copy(n, 3, ends, ends, self.here.along_z(1)).wait()
        own = self.view(source, self.own)
        return wide(own[self.here.z]), [wide(ends[i]) for i in range(3)]


def layer_kernel(
    x_in, og_in, lengths_ref, one_in, two_in, wq_in, wk_in, wv_in, wo_in, wg_in, wu_in, wd_in,
    out_ref, gi_to, oq_to, ok_to, ov_to, oo_to, og_to, ou_to, od_to, on_to,
    gi_ref, oq_ref, ok_ref, ov_ref, oo_ref, og_out, ou_out, od_out, on_ref,
    wn, wa, wo, wm, pack_a, pack_m, xm, og8, nt8, no8, at8, atb, og_peer, nt_peer, no_peer, at_peer,
    og_t, nt_t, q_ref, k_ref, v_ref, p_ref, mid, acc, gn, gain, tri, tri_peer,
    swap, swap_in, gat, edge, edge_in, outs, outs_peer, gb, gb_peer, mga,
    nb_peer, nb_sum, mlp_twos, mlp_ends, mga_twos, mga_ends, mgo_twos, mgo_ends, nb_twos, nb_ends,
    own_sem, g_send, g_recv, s_send, s_recv, halo_send, halo_recv, edge_send, edge_recv,
    side_send, side_recv, tri_send, tri_recv, swap_send, swap_recv, out_send, out_recv, host_sem, row_send, row_recv,
):
    nb, no_t = wn, nt_t
    here = Place()
    z, c, k, h = here.z, here.c, here.k, here.h
    tiles = wm.shape[0]
    span = tiles * PART
    scale = 1.0 / math.sqrt(HEAD_DIM)
    tokens = x_in.shape[0]
    piece = tokens // 2
    rows = wn.shape[4]
    gather = Gather(here, own_sem, g_send, g_recv)
    scatter = Scatter(here, s_send, s_recv)
    early = 6
    total = early + tiles

    def whole_of(n):
        if n == 0:
            return wn
        return wa.at[n - 1] if n < 4 else wo.at[n - 4]

    def pack_of(n):
        return pack_a.at[n - 1] if 1 <= n < 4 else None

    def parts_of(n):
        if n == 0:
            return []
        if n < 4:
            source = (wk_in, wv_in, wq_in)[n - 1]
            return [(source.at[:, lanes_at(h * HALF, HALF)], source.at[:, lanes_at((1 - h) * HALF, HALF)], 0, HALF)]
        return [(wo_in.at[:, pl.ds((n - 4) * HALF, HALF)], None, 0, HALF)]

    def mlp_parts(f):
        return [
            (
                w.at[:, lanes_at(h * span + f * PART, PART)],
                w.at[:, lanes_at((1 - h) * span + f * PART, PART)],
                i * PART, PART,
            )
            for i, w in enumerate((wg_in, wu_in, wd_in))
        ]

    def step(stage, n):
        late = n >= early
        whole = wm.at[n - early] if late else whole_of(n)
        if stage == 0:
            gather.first(n, whole, pack_m.at[n - early] if late else pack_of(n), n != 0)
        else:
            (gather.second, gather.third, gather.fourth, gather.fifth)[stage - 1](n, whole)

    def steps(stage, *chunks_of):
        for n in chunks_of:
            step(stage, n)

    def tile_steps(f):
        for stage, ahead in enumerate(AHEAD):
            tile = f + ahead

            @pl.when(tile < tiles)
            def _(stage=stage, tile=tile):
                if stage == 0:
                    gather.first(early + tile, wm.at[tile], pack_m.at[tile])
                else:
                    (gather.second, gather.third, gather.fourth)[stage - 1](early + tile, wm.at[tile])

    def halo(which, kind):
        ref = (k_ref, v_ref)[which]
        tail, head = pl.ds((PAD + piece - WINDOW) // rows, WINDOW // rows), pl.ds((PAD - WINDOW) // rows, WINDOW // rows)
        if kind == 0:
            source, target, device = ref.at[:, tail], ref.at[:, head], here.peer()
        elif kind == 1:
            source, target, device = ref.at[pl.ds(0, 2), tail], ref.at[pl.ds(2, 2), head], here.peer()
        else:
            source, target, device = ref.at[pl.ds(2, 2), tail], ref.at[pl.ds(0, 2), head], here.cross()
        return remote(source, target, halo_send.at[which, kind // 2], halo_recv.at[which, kind // 2], device)

    def edge_copy(kind):
        if kind == 0:
            source, target, device = edge, edge_in, here.peer()
        elif kind == 1:
            source, target, device = edge.at[:, 1], edge_in.at[:, 0], here.peer()
        else:
            source, target, device = edge.at[:, 0], edge_in.at[:, 1], here.cross()
        return remote(source, target, edge_send.at[kind // 2], edge_recv.at[kind // 2], device)

    def x_copy():
        return remote(x_in, xm, swap_send.at[0], swap_recv.at[0], here.mate())

    def og_copy(slot):
        view = og8.at[:, :, slot]
        return remote(view, view, swap_send.at[1], swap_recv.at[1], here.mate())

    def nt_copy(slot):
        view = nt8.at[:, :, slot]
        return remote(view, view, swap_send.at[2], swap_recv.at[2], here.mate())

    def at_copy():
        return remote(atb.at[1 - h], at8.at[pl.ds(2 * h, 2)], swap_send.at[3], swap_recv.at[3], here.mate())

    def ga_copy(row):
        there = pl.ds(row * piece, piece)
        return remote(
            swap.at[0, there, pl.ds(0, HALF)], gat.at[h, there], row_send.at[2 + row], row_recv.at[2 + row], here.mate()
        )

    def gn_copy(row):
        there = pl.ds(row * piece, piece)
        return remote(swap.at[0, there], swap_in.at[0, there], row_send.at[row], row_recv.at[row], here.mate())

    def swap_copy(number):
        return remote(
            swap.at[number % 2], swap_in.at[number], swap_send.at[5 + number], swap_recv.at[5 + number], here.mate()
        )

    def out_store():
        return pltpu.make_async_copy(swap.at[1], out_ref, host_sem.at[8])

    def x_again(i):
        return pltpu.make_async_copy(x_in.at[:, pl.ds(i * HALF, HALF)], gat.at[i], host_sem.at[9 + i])

    def side_copy(number, source, target):
        return remote(source, target, side_send.at[number], side_recv.at[number], here.peer())

    def og_side(number, slot):
        return side_copy(number, og8.at[:, 1 - c, slot], og_peer.at[:, slot])

    def nt_side(number, slot):
        return side_copy(number, nt8.at[:, 1 - c, slot], nt_peer.at[:, slot])

    def no_side():
        return side_copy(4, no8.at[:, 1 - c], no_peer)

    def at_side():
        return side_copy(5, at8.at[:, 1 - c], at_peer)

    def gb_side():
        return side_copy(6, gb, gb_peer)

    def pair_side():
        return side_copy(7, nb.at[:, 1 - c], nb_peer)

    def out_copy(m):
        return remote(outs.at[m], outs_peer.at[m], out_send.at[m], out_recv.at[m], here.peer())

    def tri_copy(f, slot):
        return remote(
            tri.at[f, :, slot], tri_peer.at[f, :, slot], tri_send.at[f], tri_recv.at[f], here.peer()
        )

    def spread(value, target, slot):
        for i in range(8):
            target[i // 2, i % 2, slot] = value[:, i * PART : (i + 1) * PART]

    def joined(source, slot):
        return jnp.concatenate([source[i // 2, i % 2, slot] for i in range(8)], axis=1)

    def turned(own_part, peer_part, target):
        for level in range(4):
            rows = slice(level * PART, (level + 1) * PART)
            left, right = own_part(level), peer_part(level)
            target[rows, 0 : left.shape[0]] = low(wide(left).T)
            target[rows, left.shape[0] : 2 * left.shape[0]] = low(wide(right).T)

    def turned_slot(source, peer, target, slot):
        for level in range(4):
            rows = slice(level * PART, (level + 1) * PART)
            target[rows, lanes_at(slot * tokens, tokens)] = low(wide(source[level, c, slot]).T)
            target[rows, lanes_at((2 + slot) * tokens, tokens)] = low(wide(peer[level, slot]).T)

    og_fetches = [
        pltpu.make_async_copy(og_in.at[:, pl.ds(i * PART, PART)], og8.at[i // 2, i % 2, h], host_sem.at[i])
        for i in range(8)
    ]
    x_fetches = [
        pltpu.make_async_copy(x_in.at[:, pl.ds(i * HALF, HALF)], outs.at[0, i], host_sem.at[9 + i]) for i in range(2)
    ]
    for n in range(early):
        gather.begin(n, parts_of(n), whole_of(n), pack_of(n))
    gain_columns = [jnp.broadcast_to(wide(g[...])[None, :], (LANES // 2, rows)) for g in (one_in, two_in)]
    gather.slot(wn)[...] = low(jnp.concatenate(gain_columns, axis=0).T)
    for copy in og_fetches + x_fetches:
        copy.start()

    @pl.loop(0, tiles)
    def _(f):
        gather.begin(early + f, mlp_parts(f), wm.at[f], pack_m.at[f])

    skipped, begun = (PAD - WINDOW) // rows, PAD // rows
    nothing = jnp.zeros((4, skipped, rows, HALF), jnp.bfloat16)
    for ref in (k_ref, v_ref):
        ref[:, 0:skipped] = nothing

    @pl.when((c == 0) & (k == 0))
    def _():
        for ref in (k_ref, v_ref):
            ref[0:2, skipped:begun] = nothing[0:2]

    @pl.when((c == 1) & (k == 1))
    def _():
        edge_in[:, 1] = jnp.zeros((2, 2, WINDOW, HALF), jnp.bfloat16)

    greet(here.partners())

    steps(0, 0, 1, 2, 3)
    steps(0, 4, 5)
    x_copy().start()
    steps(0, 6, 7)
    steps(1, 0, 1, 2, 3)
    steps(2, 0, 1, 2, 3)
    steps(1, 4, 5)
    steps(3, 0, 1, 2, 3)
    for copy in og_fetches:
        copy.wait()
    og_side(0, h).start()
    steps(4, 0)

    gain_rows = wide(flat(wn[...])).T
    gain[0:8, :] = jnp.broadcast_to(gain_rows[0:1, :], (8, gain_rows.shape[1]))
    gain[8:16, :] = jnp.broadcast_to(gain_rows[64:65, :], (8, gain_rows.shape[1]))

    def normed_of(value, row):
        factor = lax.rsqrt(jnp.mean(value * value, axis=-1, keepdims=True) + 1e-05)
        return low(value * factor * gain[row : row + 1, :])

    for copy in x_fetches:
        copy.wait()
    spread(normed_of(wide(jnp.concatenate([outs[0, 0], outs[0, 1]], axis=1)), 0), no8, h)
    x_copy().wait()
    spread(normed_of(wide(xm[...]), 0), no8, 1 - h)
    no_side().start()

    def projected(n, slot):
        return low(mm(joined(no8, slot), flat(wa[n])))

    steps(1, 6)
    for n, ref in ((0, k_ref), (1, v_ref)):
        steps(4, 1 + n)
        for slot in range(2):
            ref[2 * slot : 2 * slot + 2, begun:] = projected(n, slot).reshape(2, piece // rows, rows, HALF)

        @pl.when(c == 0)
        def _(n=n):
            halo(n, 0).start()

        @pl.when(c == 1)
        def _(n=n):
            halo(n, 1).start()

        @pl.when((c == 1) & (k == 0))
        def _(n=n):
            halo(n, 2).start()

        if n == 1:
            steps(0, 8, 9)
            steps(1, 7)
            steps(2, 4)

    steps(4, 3)
    for slot in range(2):
        q_ref[slot] = projected(2, slot)

    for n in range(2):

        @pl.when(c == 0)
        def _(n=n):
            halo(n, 0).wait_send()
            halo(n, 1).wait_recv()

        @pl.when(c == 1)
        def _(n=n):
            halo(n, 0).wait_recv()
            halo(n, 1).wait_send()

        @pl.when((c == 1) & (k == 0))
        def _(n=n):
            halo(n, 2).wait_send()

        @pl.when((c == 0) & (k == 1))
        def _(n=n):
            halo(n, 2).wait_recv()

    def mask_of(slot, row):
        first = (4 * k + 2 * slot + c) * piece
        query_pos = first + lax.broadcasted_iota(jnp.int32, (piece, PAD + piece), 0)
        key_pos = first - PAD + lax.broadcasted_iota(jnp.int32, (piece, PAD + piece), 1)
        start = jnp.zeros((piece, PAD + piece), jnp.int32)
        reached = 0
        for doc in range(lengths_ref.shape[1]):
            reached = reached + lengths_ref[row, doc]
            start = jnp.maximum(start, jnp.where(query_pos >= reached, reached, 0))
        return (key_pos >= start) & (key_pos <= query_pos) & (query_pos - key_pos < WINDOW)

    def attend(slot, row):
        allowed = mask_of(slot, row)
        span_rows = slice(row * piece, (row + 1) * piece)
        for head in range(HEADS // 2):
            cols = slice(head * HEAD_DIM, (head + 1) * HEAD_DIM)
            scores = nt_dot(q_ref[slot, span_rows, cols], flat(k_ref[2 * slot + row, :, :, cols])) * scale
            scores = jnp.where(allowed, scores, -1e30)
            exps = jnp.exp(scores - jnp.max(scores, axis=-1, keepdims=True))
            probs = exps / jnp.sum(exps, axis=-1, keepdims=True)
            p_ref[slot, row, head] = probs
            atb[slot, head // 2, head % 2, span_rows, :] = low(mm(low(probs), flat(v_ref[2 * slot + row, :, :, cols])))

    attend(1 - h, 0)
    attend(1 - h, 1)
    at_copy().start()
    steps(0, 10, 11, 12, 13, 14, 15, 16)
    steps(2, 5)
    steps(1, 8)
    attend(h, 0)
    attend(h, 1)
    at8[pl.ds(2 * h, 2)] = atb[h]
    steps(3, 4)
    steps(2, 6)
    steps(3, 5)
    steps(4, 4, 5)
    steps(1, 9)
    steps(2, 7)
    at_copy().wait()
    at_side().start()
    attended = jnp.concatenate([at8[i // 2, i % 2] for i in range(8)], axis=1)
    for n in range(2):
        cols = slice(n * HALF, (n + 1) * HALF)
        mid[:, cols] = wide(outs[0, n]) + mm(attended, flat(wo[n]))
    middle = mid[...]
    spread(normed_of(middle, 8), nt8, h)
    nt_copy(h).start()
    nt_side(2, h).start()
    og_copy(h).start()
    steps(1, 10, 11)
    steps(2, 8)
    steps(3, 6)
    steps(2, 9)
    steps(3, 7)
    acc[h] = middle
    acc[1 - h] = jnp.zeros(middle.shape, jnp.float32)
    gn[...] = jnp.zeros(gn.shape, jnp.float32)

    def feed(slot, *numbers):
        left, out_grad = joined(nt8, slot), joined(og8, slot)
        w_pairs = [flat(wm[f, :, :, :, :, :, 0 : 2 * PART]) for f in numbers]
        w_down = jnp.concatenate([flat(wm[f, :, :, :, :, :, 2 * PART : 3 * PART]) for f in numbers], axis=1)
        grads_hidden = mm(out_grad, w_down)
        hidden_acts, grads = [], []
        for i, f in enumerate(numbers):
            both = mm(left, w_pairs[i])
            gates, ups = both[:, 0:PART], both[:, PART:]
            grad_hidden = grads_hidden[:, i * PART : (i + 1) * PART]
            sigmoid = 1.0 / (1.0 + jnp.exp(-gates))
            silu = gates * sigmoid
            hidden = low(silu * ups)
            grad_gates = low(grad_hidden * ups * sigmoid * (1.0 + gates * (1.0 - sigmoid)))
            grad_ups = low(grad_hidden * silu)
            tri[f, 0, slot] = grad_gates
            tri[f, 1, slot] = grad_ups
            tri[f, 2, slot] = hidden
            tri_copy(f, slot).start()
            hidden_acts.append(hidden)
            grads += [grad_gates, grad_ups]
        acc[slot] += nt_dot(jnp.concatenate(hidden_acts, axis=1), w_down)
        gn[slot] += nt_dot(jnp.concatenate(grads, axis=1), jnp.concatenate(w_pairs, axis=1))

    og_side(0, h).wait()
    turned_slot(og8, og_peer, og_t, h)
    nt_side(2, h).wait()
    turned_slot(nt8, nt_peer, nt_t, h)
    n_tokens = 2 * tokens

    def ff_grads(f):
        remote(tri.at[f], tri_peer.at[f], tri_send.at[f], tri_recv.at[f], here.peer()).wait()
        pair = mm(nt_t[:, 0:n_tokens], jnp.concatenate([flat(tri[f, 0]), flat(tri[f, 1])], axis=1)) + mm(
            nt_t[:, n_tokens:], jnp.concatenate([flat(tri_peer[f, 0]), flat(tri_peer[f, 1])], axis=1)
        )
        down = mm(og_t[:, 0:n_tokens], flat(tri[f, 2])) + mm(og_t[:, n_tokens:], flat(tri_peer[f, 2]))
        wm[f, :, 0, :, :, :, 0 : 2 * PART] = low(pair).reshape(4, 2, 2, -1, 2 * PART)
        wm[f, :, 0, :, :, :, 2 * PART : 3 * PART] = low(down).reshape(4, 2, 2, -1, PART)

    chunks = tiles + 6

    def chunk(n):
        if n < tiles:
            return wm.at[n, :, 0], mlp_twos.at[n], mlp_ends.at[n]
        n -= tiles
        if n < 2:
            return k_ref.at[:, pl.ds(4 * n, 4)], mgo_twos.at[n], mgo_ends.at[n]
        if n < 5:
            source = mga if n == 2 else v_ref.at[:, pl.ds(4 * (n - 3), 4)]
            return source, mga_twos.at[n - 2], mga_ends.at[n - 2]
        return nb_sum, nb_twos, nb_ends

    def store_tile(n, mine, others):
        back, across, on = others
        for half, value in ((h, mine + across), (1 - h, back + on)):
            for i, ref in enumerate((og_out, ou_out, od_out)):
                ref[:, lanes_at(half * span + n * PART, PART)] = value[:, i * PART : (i + 1) * PART]

    def store(n, mine, others):
        if n < tiles:
            store_tile(n, mine, others)
            return
        back, across, on = others
        n -= tiles
        if 2 <= n < 5:
            for half, value in ((h, mine + across), (1 - h, back + on)):
                (oq_ref, ok_ref, ov_ref)[n - 2][:, lanes_at(half * HALF, HALF)] = value
            return
        value = mine + back + across + on
        if n < 2:
            oo_ref[:, n * HALF : (n + 1) * HALF] = value
        else:
            on_ref[...] = value

    def sum_tick(t):
        for stage, lag in enumerate(SUM_LAGS):
            n = t - lag
            if not 0 <= n < chunks:
                continue
            source, twos, ends = chunk(n)
            if stage == 0:
                scatter.second(n, source, twos)
            elif stage == 1:
                scatter.third(n, source, twos, ends)
            else:
                store(n, *scatter.fourth(n, source, ends))

    def launch_tile(f):
        scatter.first(f, wm.at[f, :, 0], mlp_twos.at[f])

    def launch(n):
        source, twos, _ = chunk(n)
        scatter.first(n, source, twos)

    @pl.loop(0, FIRST_TILES)
    def _(f):
        tile_steps(f)
        gather.fifth(early + f, wm.at[f])
        feed(h, f)

    og_copy(1 - h).wait()
    og_side(1, 1 - h).start()
    nt_copy(1 - h).wait()
    nt_side(3, 1 - h).start()

    @pl.loop(0, FIRST_TILES // 2)
    def _(i):
        for f in (FIRST_TILES + 2 * i, FIRST_TILES + 2 * i + 1):

            @pl.when(f < tiles)
            def _(f=f):
                tile_steps(f)

        feed(1 - h, 2 * i, 2 * i + 1)

    feed(1 - h, FIRST_TILES - 1)

    @pl.loop(0, (tiles - FIRST_TILES) // 2)
    def _(i):
        f = FIRST_TILES + 2 * i
        for tile in (f, f + 1):
            gather.fifth(early + tile, wm.at[tile])

        @pl.loop(0, 2)
        def _(slot):
            feed(slot, f, f + 1)

    for row in range(2):
        there = slice(row * piece, (row + 1) * piece)
        swap[0, there, :] = low(gn[1 - h, there, :])
        gn_copy(row).start()
    og_side(1, 1 - h).wait()
    turned_slot(og8, og_peer, og_t, 1 - h)
    nt_side(3, 1 - h).wait()
    turned_slot(nt8, nt_peer, nt_t, 1 - h)

    @pl.loop(0, tiles)
    def _(f):
        ff_grads(f)
        launch_tile(f)


    def close_middle(row):
        gn_copy(row).wait()
        there = slice(row * piece, (row + 1) * piece)
        middle = mid[there, :]
        factor = lax.rsqrt(jnp.mean(middle * middle, axis=-1, keepdims=True) + 1e-05)
        grad_normed = gn[h, there, :] + wide(swap_in[0, there, :])
        through = grad_normed * gain[8:9, :]
        shift = jnp.mean(through * middle, axis=-1, keepdims=True) * factor * factor * factor
        out_grad = jnp.concatenate([og8[i // 2, i % 2, h, there, :] for i in range(8)], axis=1)
        grad_middle = wide(out_grad) + factor * through - middle * shift
        gi_ref[there, :] = grad_middle
        gb[there, :] = low(grad_middle)
        return jnp.sum(grad_normed * middle * factor, axis=0, keepdims=True)

    def to_attended(row):
        there = slice(row * piece, (row + 1) * piece)

        def part(half):
            rows = pl.ds(2 * half, 2)
            return low(
                nt_dot(gb[there, 0:HALF], flat(wo[0, rows])) + nt_dot(gb[there, HALF:], flat(wo[1, rows]))
            )

        swap[0, there, 0:HALF] = part(1 - h)
        ga_copy(row).start()
        gat[h, there, :] = part(h)

    def send_out(ones):
        gb_side().start()
        swap[1] = low(acc[1 - h])
        swap_copy(1).start()
        gain[8:16, :] = jnp.broadcast_to(ones[0] + ones[1], (8, gain.shape[1]))

    def keep_out():
        mid[...] = acc[h]

    def close_out():
        swap_copy(1).wait()
        swap[1] = low(mid[...] + wide(swap_in[1]))
        out_store().start()

    def attend_back(slot, row):
        span_rows = slice(row * piece, (row + 1) * piece)
        for head in range(HEADS // 2):
            cols = slice(head * HEAD_DIM, (head + 1) * HEAD_DIM)
            there = slice(row * HALF + head * HEAD_DIM, row * HALF + (head + 1) * HEAD_DIM)
            grad = gat[slot, span_rows, cols]
            probs = p_ref[slot, row, head]
            gn[slot, :, there] = tn_dot(low(probs), grad)
            grad_probs = nt_dot(grad, flat(v_ref[2 * slot + row, :, :, cols]))
            inner = jnp.sum(grad_probs * probs, axis=-1, keepdims=True)
            grad_scores = low(probs * (grad_probs - inner))
            outs[2, slot, span_rows, cols] = low(mm(grad_scores, flat(k_ref[2 * slot + row, :, :, cols])) * scale)
            acc[slot, :, there] = tn_dot(grad_scores, q_ref[slot, span_rows, cols]) * scale
        there = slice(row * HALF, (row + 1) * HALF)
        edge[0, slot, row] = low(acc[slot, PAD - WINDOW : PAD, there])
        edge[1, slot, row] = low(gn[slot, PAD - WINDOW : PAD, there])

    def send_edge():
        out_copy(2).start()

        @pl.when(c == 1)
        def _():
            edge_copy(0).start()

        @pl.when(c == 0)
        def _():
            edge_copy(1).start()

        @pl.when((c == 0) & (k == 1))
        def _():
            edge_copy(2).start()

    def close_edge():
        @pl.when(c == 1)
        def _():
            edge_copy(0).wait_send()
            edge_copy(1).wait_recv()

        @pl.when(c == 0)
        def _():
            edge_copy(0).wait_recv()
            edge_copy(1).wait_send()

        @pl.when((c == 0) & (k == 1))
        def _():
            edge_copy(2).wait_send()

        @pl.when((c == 1) & (k == 0))
        def _():
            edge_copy(2).wait_recv()

        inside = piece - WINDOW
        for m, source in ((0, acc), (1, gn)):
            for slot in range(2):
                for row in range(2):
                    there = slice(row * HALF, (row + 1) * HALF)
                    first = row * piece
                    outs[m, slot, first : first + inside, :] = low(source[slot, PAD : PAD + inside, there])
                    outs[m, slot, first + inside : first + piece, :] = low(
                        source[slot, PAD + inside : PAD + piece, there] + wide(edge_in[m, slot, row])
                    )
            out_copy(m).start()

    def to_input(slot):
        grad = nt_dot(outs[0, slot], flat(wa[0]))
        for m in (1, 2):
            grad = grad + nt_dot(outs[m, slot], flat(wa[m]))
        return grad

    def inverse_rms(value):
        return lax.rsqrt(jnp.mean(value * value, axis=-1, keepdims=True) + 1e-05)

    def send_input():
        part = to_input(1 - h)
        swap[0] = low(part)
        swap_copy(2).start()
        x = wide(xm[...])
        return jnp.sum(part * x * inverse_rms(x), axis=0, keepdims=True)

    def send_norm(one):
        part = to_input(h)
        acc[0] = part
        for i in range(2):
            x_again(i).wait()
        x = wide(jnp.concatenate([gat[0], gat[1]], axis=1))
        one = one + jnp.sum(part * x * inverse_rms(x), axis=0, keepdims=True)
        width = one.shape[1]
        stacked = jnp.concatenate(
            [
                jnp.broadcast_to(one, (LANES // 2, width)),
                jnp.broadcast_to(gain[8:9, :], (LANES // 2, width)),
            ],
            axis=0,
        )
        nb[...] = low(stacked.T).reshape(nb.shape)
        pair_side().start()

    def close_input():
        swap_copy(2).wait()
        grad_normed = acc[0] + wide(swap_in[2])
        x = wide(jnp.concatenate([gat[0], gat[1]], axis=1))
        factor = inverse_rms(x)
        through = grad_normed * gain[0:1, :]
        shift = jnp.mean(through * x, axis=-1, keepdims=True) * factor * factor * factor
        gi_ref[...] += factor * through - x * shift

    def close_norm():
        pair_side().wait()
        nb_sum[...] = low(wide(nb[:, c]) + wide(nb_peer[...]))

    def turn_normed():
        no_side().wait()
        turned(lambda i: flat(no8[i, c]), lambda i: flat(no_peer[i]), no_t)

    def wout_grads():
        at_side().wait()
        turned(lambda i: at8[i, c], lambda i: at_peer[i], og_t)
        gb_side().wait()
        for n in range(2):
            cols = slice(n * HALF, (n + 1) * HALF)
            grad = mm(og_t[:, 0:tokens], gb[:, cols]) + mm(og_t[:, tokens : 2 * tokens], gb_peer[:, cols])
            k_ref[:, 4 * n : 4 * n + 4] = low(grad).reshape(4, 4, -1, HALF)

    def attn_grads(m):
        out_copy(m).wait()
        grad = mm(no_t[:, 0:n_tokens], flat(outs[m])) + mm(no_t[:, n_tokens:], flat(outs_peer[m]))
        if m == 2:
            mga[...] = low(grad).reshape(mga.shape)
        else:
            v_ref[:, 4 * m : 4 * m + 4] = low(grad).reshape(4, 4, -1, HALF)

    def ticks(first, last):
        for t in range(first, last):
            sum_tick(t)

    ticks(0, 2)
    ones = []
    for row in range(2):
        ones.append(close_middle(row))
        to_attended(row)
    send_out(ones)
    keep_out()
    ticks(2, 4)
    attend_back(h, 0)
    attend_back(h, 1)
    for row in range(2):
        ga_copy(row).wait()
        attend_back(1 - h, row)
    send_edge()
    for i in range(2):
        x_again(i).start()
    turn_normed()
    wout_grads()
    launch(tiles)
    launch(tiles + 1)
    attn_grads(2)
    launch(tiles + 2)
    ticks(4, 8)
    close_edge()
    one = send_input()
    for m in range(2):
        attn_grads(m)
        launch(tiles + 3 + m)
    send_norm(one)
    ticks(8, 9)
    close_norm()
    launch(tiles + 5)
    ticks(9, 11)
    close_out()
    ticks(11, 14)
    close_input()
    stores = [
        pltpu.make_async_copy(source, target, host_sem.at[12 + i])
        for i, (source, target) in enumerate(
            zip(
                (gi_ref, og_out, ou_out, od_out, oo_ref, oq_ref, ok_ref, ov_ref, on_ref),
                (gi_to, og_to, ou_to, od_to, oo_to, oq_to, ok_to, ov_to, on_to),
            )
        )
    ]
    stores[0].start()
    ticks(14, tiles + SUM_LAGS[-1])
    for store_out in stores[1:4]:
        store_out.start()
    ticks(tiles + SUM_LAGS[-1], tiles + SUM_LAGS[-1] + 2)
    stores[4].start()
    ticks(tiles + SUM_LAGS[-1] + 2, chunks + SUM_LAGS[-1])
    for store_out in stores[5:]:
        store_out.start()
    out_store().wait()
    for store_out in stores:
        store_out.wait()


def deliver_kernel(count, *refs):
    sources, targets, refs = refs[:count], refs[count : 2 * count + 1], refs[2 * count + 1 :]
    held, vectors, (in_sem, out_sem) = refs[:count], refs[count : count + 2], refs[count + 2 :]
    ins = [pltpu.make_async_copy(s, v, in_sem.at[i]) for i, (s, v) in enumerate(zip(sources, held))]
    leave = (*vectors, *held[1:])
    outs = [pltpu.make_async_copy(v, t, out_sem.at[i]) for i, (v, t) in enumerate(zip(leave, targets))]
    for copy in ins:
        copy.start()
    ins[0].wait()
    turned = held[0][...].T
    for i in range(2):
        vectors[i][...] = turned[i * LANES // 2, :]
        outs[i].start()
    for arrived, leaving in zip(ins[1:], outs[2:]):
        arrived.wait()
        leaving.start()
    for copy in outs:
        copy.wait()


def delivered(norms, arrays):
    anywhere = pl.BlockSpec(memory_space=pl.ANY)
    count = len(arrays) + 1
    vector = (norms.shape[:1], norms.dtype)
    return pl.pallas_call(
        functools.partial(deliver_kernel, count),
        out_shape=[jax.ShapeDtypeStruct(*vector)] * 2 + [jax.ShapeDtypeStruct(a.shape, a.dtype) for a in arrays],
        in_specs=[anywhere] * count,
        out_specs=[anywhere] * (count + 1),
        scratch_shapes=[pltpu.VMEM(a.shape, a.dtype) for a in (norms, *arrays)]
        + [pltpu.VMEM(*vector)] * 2
        + [pltpu.SemaphoreType.DMA((count,)), pltpu.SemaphoreType.DMA((count + 1,))],
        compiler_params=pltpu.CompilerParams(vmem_limit_bytes=60 * 2**20),
        name="deliver",
    )(norms, *arrays)


def fused(hidden_in, lengths, out_grad, gain_shards, weight_shards):
    hidden = hidden_in.reshape(-1, hidden_in.shape[-1])
    tokens, width = hidden.shape
    rows = weight_shards[0].shape[0]
    tiles = weight_shards[4].shape[1] // (2 * PART)
    bf, fl = jnp.bfloat16, jnp.float32
    every, mine = (4, 2, 2, 2, rows), (4, 2, 2, rows)
    part = 3 * PART
    dma = pltpu.SemaphoreType.DMA
    vmem, anywhere = pl.BlockSpec(memory_space=pltpu.VMEM), pl.BlockSpec(memory_space=pl.ANY)
    shape = jax.ShapeDtypeStruct
    piece = tokens // 2
    keys = (4, (PAD + piece) // rows, rows, HALF)
    scratch = [
        ((*every, LANES), bf), ((3, *every, HALF), bf), ((2, *every, HALF), bf), ((tiles, *every, part), bf),
        ((3, rows, HALF), bf), ((tiles, rows, part), bf), ((tokens, width), bf),
        *[((4, 2, 2, tokens, PART), bf)] * 3, ((4, 2, tokens, PART), bf), ((2, 2, 2, tokens, PART), bf),
        *[((4, 2, tokens, PART), bf)] * 3, ((4, tokens, PART), bf),
        *[((width // 2, 4 * tokens), bf)] * 2,
        ((2, tokens, HALF), bf), (keys, bf), (keys, bf), ((2, 2, HEADS // 2, piece, PAD + piece), fl),
        ((tokens, width), fl), ((2, tokens, width), fl), ((2, tokens, width), fl),
        ((16, width), fl), ((tiles, 3, 2, tokens, PART), bf), ((tiles, 3, 2, tokens, PART), bf),
        ((2, tokens, width), bf), ((3, tokens, width), bf), ((2, tokens, HALF), bf),
        ((2, 2, 2, WINDOW, HALF), bf), ((2, 2, 2, WINDOW, HALF), bf),
        ((3, 2, tokens, HALF), bf), ((3, 2, tokens, HALF), bf), ((tokens, width), bf), ((tokens, width), bf),
        ((*mine, HALF), bf),
        ((*mine, LANES), bf), ((*mine, LANES), bf),
        ((tiles, 3, 4, rows, part), bf), ((tiles, 3, rows, part), bf),
        ((3, 3, 4, rows, HALF), bf), ((3, 3, rows, HALF), bf),
        ((2, 3, 4, rows, HALF), bf), ((2, 3, rows, HALF), bf),
        ((3, 4, rows, LANES), bf), ((3, rows, LANES), bf),
    ]
    count, chunks = 6 + tiles, 6 + tiles
    sums = [((tokens, width), fl)] + [((rows, width), fl)] * 4
    sums += [((rows, 2 * tiles * PART), fl)] * 3 + [((rows, LANES), fl)]
    results = pl.pallas_call(
        layer_kernel,
        out_shape=[shape((tokens, width), bf)] + [shape(*s) for s in sums],
        in_specs=[anywhere, anywhere, pl.BlockSpec(memory_space=pltpu.SMEM), vmem, vmem] + [anywhere] * 7,
        out_specs=[anywhere] * 10,
        scratch_shapes=[pltpu.VMEM(*s) for s in sums + scratch]
        + [
            dma((count, 2)), dma((count, 4)), dma((count, 4)), dma((chunks, 4)), dma((chunks, 4)),
            dma((2, 2)), dma((2, 2)), dma((2,)), dma((2,)), dma((8,)), dma((8,)),
            dma((tiles,)), dma((tiles,)), dma((8,)), dma((8,)), dma((3,)), dma((3,)), dma((21,)), dma((4,)), dma((4,)),
        ],
        compiler_params=pltpu.CompilerParams(
            collective_id=0, has_side_effects=True, vmem_limit_bytes=63 * 2**20
        ),
        name="layer",
    )(hidden, out_grad.reshape(hidden.shape), lengths, *gain_shards, *weight_shards)
    one, two, block_out, grad_in, query, key, value, wout, gate, up, down = delivered(results[9], results[:9])
    return (
        block_out.reshape(hidden_in.shape), grad_in.reshape(hidden_in.shape),
        one, query, key, value, wout, two, gate, up, down,
    )


def layer(hidden_in, lengths, out_grad, gains, weights):
    score_scale = 1.0 / math.sqrt(HEAD_DIM)
    tokens = hidden_in.shape[1]
    gain_one, gain_two = gains
    w_query, w_key, w_value, w_out, w_gate, w_up, w_down = weights
    inputs = hidden_in.astype(jnp.float32)
    normed_one = rms_scale(inputs, gain_one).astype(jnp.bfloat16)
    queries = project(normed_one, w_query).astype(jnp.bfloat16)
    keys = project(normed_one, w_key).astype(jnp.bfloat16)
    values = project(normed_one, w_value).astype(jnp.bfloat16)
    tails = jnp.stack([keys[:, tokens - WINDOW :], values[:, tokens - WINDOW :]])
    received = passed_along(tails, "seq", 1)
    keys_all = jnp.concatenate([received[0], keys], axis=1)
    values_all = jnp.concatenate([received[1], values], axis=1)
    allowed = window_mask(lengths, lax.axis_index("seq"), tokens)
    scores = scores_of(queries, keys_all, allowed)
    top = jnp.max(scores, axis=-1, keepdims=True)
    exps = jnp.exp(scores - top)
    probs = exps / jnp.sum(exps, axis=-1, keepdims=True)
    probs_low = probs.astype(jnp.bfloat16)
    mixed = jnp.einsum(
        "rhqk,rkhd->rqhd", probs_low, split_heads(values_all), preferred_element_type=jnp.float32
    )
    attended = merge_heads(mixed).astype(jnp.bfloat16)
    middle = inputs + project(attended, w_out)
    normed_two = rms_scale(middle, gain_two).astype(jnp.bfloat16)
    gates = project(normed_two, w_gate)
    ups = project(normed_two, w_up)
    hidden_act = swiglu(gates, ups).astype(jnp.bfloat16)
    block_out = (middle + project_back(hidden_act, w_down)).astype(jnp.bfloat16)
    grad_hidden = project(out_grad, w_down)
    unused, swiglu_back = jax.vjp(swiglu, gates, ups)
    grad_gates, grad_ups = swiglu_back(grad_hidden)
    grad_gates = grad_gates.astype(jnp.bfloat16)
    grad_ups = grad_ups.astype(jnp.bfloat16)
    grad_down = weight_grad(out_grad, hidden_act)
    grad_gate = weight_grad(normed_two, grad_gates)
    grad_up = weight_grad(normed_two, grad_ups)
    grad_normed_two = project_back(grad_gates, w_gate) + project_back(grad_ups, w_up)
    unused, norm_two_back = jax.vjp(rms_scale, middle, gain_two)
    grad_middle_part, grad_norm2 = norm_two_back(grad_normed_two)
    grad_middle = out_grad.astype(jnp.float32) + grad_middle_part
    grad_branch = grad_middle.astype(jnp.bfloat16)
    grad_wout = weight_grad(attended, grad_branch)
    grad_attended = project_back(grad_branch, w_out).astype(jnp.bfloat16)
    grad_heads = split_heads(grad_attended)
    grad_values_all = jnp.einsum(
        "rhqk,rqhd->rkhd", probs_low, grad_heads, preferred_element_type=jnp.float32
    )
    grad_probs = jnp.einsum(
        "rqhd,rkhd->rhqk", grad_heads, split_heads(values_all), preferred_element_type=jnp.float32
    )
    grad_scores = (
        probs * (grad_probs - jnp.sum(grad_probs * probs, axis=-1, keepdims=True))
    ).astype(jnp.bfloat16)
    grad_queries = score_scale * merge_heads(
        jnp.einsum(
            "rhqk,rkhd->rqhd", grad_scores, split_heads(keys_all),
            preferred_element_type=jnp.float32,
        )
    )
    grad_keys_all = score_scale * merge_heads(
        jnp.einsum(
            "rhqk,rqhd->rkhd", grad_scores, split_heads(queries),
            preferred_element_type=jnp.float32,
        )
    )
    grad_values_all = merge_heads(grad_values_all)
    halo_grads = jnp.stack([grad_keys_all[:, :WINDOW], grad_values_all[:, :WINDOW]])
    returned = passed_along(halo_grads.astype(jnp.bfloat16), "seq", -1).astype(halo_grads.dtype)
    grad_keys = (
        grad_keys_all[:, WINDOW:].at[:, tokens - WINDOW :].add(returned[0]).astype(jnp.bfloat16)
    )
    grad_values = (
        grad_values_all[:, WINDOW:].at[:, tokens - WINDOW :].add(returned[1]).astype(jnp.bfloat16)
    )
    grad_queries = grad_queries.astype(jnp.bfloat16)
    grad_query = weight_grad(normed_one, grad_queries)
    grad_key = weight_grad(normed_one, grad_keys)
    grad_value = weight_grad(normed_one, grad_values)
    grad_normed_one = (
        project_back(grad_queries, w_query)
        + project_back(grad_keys, w_key)
        + project_back(grad_values, w_value)
    )
    unused, norm_one_back = jax.vjp(rms_scale, inputs, gain_one)
    grad_inputs_part, grad_norm1 = norm_one_back(grad_normed_one)
    grad_in = grad_middle + grad_inputs_part
    grads = (grad_query, grad_key, grad_value, grad_wout, grad_gate, grad_up, grad_down)
    return block_out, grad_in, (grad_norm1, grad_norm2), grads


def shards(
    hidden_in, lengths, norm1_gain, w_query, w_key, w_value, w_out,
    norm2_gain, w_gate, w_up, w_down, out_grad,
):
    gain_shards = (norm1_gain, norm2_gain)
    weight_shards = (w_query, w_key, w_value, w_out, w_gate, w_up, w_down)
    if (lax.axis_size("seq"), lax.axis_size("rows")) == (SEQ_PIECES, ROW_GROUPS):
        return fused(hidden_in, lengths, out_grad, gain_shards, weight_shards)
    gains = [g.astype(jnp.float32) for g in gathered_by_xla(gain_shards)]
    weights = gathered_by_xla(weight_shards)
    block_out, grad_in, norms, grads = layer(hidden_in, lengths, out_grad, gains, weights)
    norms, grads = scattered_by_xla(norms), scattered_by_xla(grads)
    return (
        block_out, grad_in, norms[0], grads[0], grads[1], grads[2], grads[3],
        norms[1], grads[4], grads[5], grads[6],
    )


def solution(mesh):
    tokens = P("rows", "seq", None)
    vector = P(("seq", "rows"))
    matrix = P(("seq", "rows"), None)
    in_specs = (
        tokens, P("rows", None), vector, matrix, matrix, matrix, matrix,
        vector, matrix, matrix, matrix, tokens,
    )
    out_specs = (
        tokens, tokens, vector, matrix, matrix, matrix, matrix,
        vector, matrix, matrix, matrix,
    )
    return jax.shard_map(shards, mesh=mesh, in_specs=in_specs, out_specs=out_specs, check_vma=False)
```
